128 devices in a mesh: req: 16 (over y, x), tp: 8 (over z, core).
Axes of the slice: x: 4, y: 4, z: 4, core: 2. Of those that a mesh axis runs over, the one named last changes fastest.
Arguments:
- stream: bfloat16 [512, 2048], P('req'), may hold values from -1.5 to 1.5
- attn_gain: bfloat16 [2048], replicated, may hold values from 0.25 to 1.75
- mlp_gain: bfloat16 [2048], replicated, may hold values from 0.25 to 1.75
- w_query: bfloat16 [2048, 2048], P(None, 'tp'), may hold values from -0.125 to 0.125
- w_keyval: bfloat16 [2048, 2, 2048], P(None, None, 'tp'), may hold values from -30 to 30
- w_out: bfloat16 [2048, 2048], P('tp'), may hold values from -0.125 to 0.125
- w_gate_up: bfloat16 [2048, 2, 8192], P(None, None, 'tp'), may hold values from -0.125 to 0.125
- w_down: bfloat16 [8192, 2048], P('tp'), may hold values from -0.0625 to 0.0625
- root_cache: bfloat16 [8, 4096, 2, 2048], P(None, 'req', None, 'tp'), may hold values from -240 to 240
- mid_cache: bfloat16 [16, 2048, 2, 2048], P('req', None, None, 'tp'), may hold values from -240 to 240
- leaf_cache: bfloat16 [512, 128, 2, 2048], P('req', None, None, 'tp'), may hold values from -240 to 240
- held_hidden: bfloat16 [16, 256, 2048], P('req', None, 'tp'), may hold values from -6 to 6
- recompute_rows: int32 [16, 256], P('req'), may hold values from 0 to 2047, as said below
- root_len: int32 [8], replicated, may hold values from 1024 to 4096
- mid_len: int32 [16], replicated, may hold values from 256 to 2048
- leaf_len: int32 [512], P('req'), may hold values from 1 to 128
- mid_parent: int32 [16], replicated, may hold values from 0 to 7
- leaf_parent: int32 [512], replicated, may hold values from 0 to 15
Outputs:
- layer_out: bfloat16 [512, 2048], P('req', 'tp')
The draws below stay inside these ranges and needn't reach their ends.
Inputs may be any that keep to these rules, and one draw needn't show every extreme that they name: `recompute_rows`: the 256 slots of one middle node are distinct.
All inputs are finite; a program needn't handle non-finite values.
Results may differ from the reference program's by a relative error of at most 0.02.
The reference program's roundings to bfloat16 on the way count: a program that leaves them out, or rounds other values in their place, can miss the bound.
Values may be sent and summed in bfloat16 or wider, within the bound.
A program may use at most 192 MiB of HBM per device.

```python
import math
import jax
import jax.numpy as jnp
from jax import lax

D = 2048
HEADS = 32
HEAD_DIM = 64
FF = 8192
ROOTS = 8
ROOT_SLICE = 256
MID_CAP = 2048
LEAF_CAP = 128
RECOMP = 256
REQUESTS = 512
ROOT_TOK = 4096
MIDS = 16


def clipped_normal(key, number, shape):
    return jnp.clip(jax.random.normal(jax.random.fold_in(key, number), shape, jnp.float32), -6.0, 6.0)


def capped_lengths(key, count, lowest, highest):
    values = jax.random.randint(key, (count,), lowest, highest + 1, jnp.int32)
    picked = jax.random.randint(jax.random.fold_in(key, 3), (), 0, count, jnp.int32)
    return jnp.where(jnp.arange(count, dtype=jnp.int32) == picked, highest, values).astype(jnp.int32)


def root_lengths(key):
    return capped_lengths(jax.random.fold_in(key, 101), ROOTS, ROOT_TOK // 4, ROOT_TOK)


def middle_lengths(key):
    return capped_lengths(jax.random.fold_in(key, 102), MIDS, MID_CAP // 8, MID_CAP)


def leaf_lengths(key):
    return capped_lengths(jax.random.fold_in(key, 103), REQUESTS, 1, LEAF_CAP)


def cache_draw(key, nodes, slots, block, lengths, needle_rate):
    width = HEADS * HEAD_DIM
    shape = (nodes, slots, width)
    live = (jnp.arange(slots, dtype=jnp.int32)[None, :] < lengths[:, None])[:, :, None]
    planted = jnp.where(jax.random.normal(jax.random.fold_in(key, 21), shape, jnp.float32) >= 0.0, 240.0, -240.0)
    levels = jnp.repeat(clipped_normal(key, 2, (nodes, slots // block, width)), block, axis=1)
    keys = levels * 0.6 + clipped_normal(key, 1, shape) * 0.2
    needle = jax.random.uniform(jax.random.fold_in(key, 3), (nodes, slots, 1), jnp.float32) < needle_rate
    keys = jnp.where(needle, clipped_normal(key, 4, shape) * 8.0, keys)
    offsets = jnp.repeat(clipped_normal(key, 6, (nodes, slots // block, width)), block, axis=1)
    values = clipped_normal(key, 5, (nodes, 1, width)) * 1.5 + offsets + clipped_normal(key, 8, shape) * 0.5
    values = jnp.where(needle, clipped_normal(key, 10, shape) * 1.5, values)
    keys = jnp.where(live, keys, planted)
    return jnp.stack([keys, values], axis=2).astype(jnp.bfloat16)


def draw_root_cache(key, part):
    return cache_draw(jax.random.fold_in(key, 201), ROOTS, ROOT_TOK, ROOT_SLICE, root_lengths(key), 1.0 / 1024.0)


def draw_mid_cache(key, part):
    return cache_draw(jax.random.fold_in(key, 202), MIDS, MID_CAP, MID_CAP // 8, middle_lengths(key), 1.0 / 1024.0)


def draw_leaf_cache(key, part):
    return cache_draw(jax.random.fold_in(key, 203), REQUESTS, LEAF_CAP, LEAF_CAP, leaf_lengths(key), 1.0 / 32.0)


def draw_w_keyval(key, part):
    base = clipped_normal(key, 204, (D, 2, HEADS * HEAD_DIM)) * D ** (-0.5)
    which = (jnp.arange(2) == 0)[:, None]
    key_scale = 3.0
    return jnp.where(which, base * key_scale, base).astype(jnp.bfloat16)


def draw_root_len(key, part):
    return root_lengths(key)


def draw_mid_len(key, part):
    return middle_lengths(key)


def draw_leaf_len(key, part):
    return leaf_lengths(key)


def node_rows(one_key):
    return jax.random.permutation(one_key, MID_CAP)[:RECOMP].astype(jnp.int32)


def draw_recompute_rows(key, part):
    rows_all = jax.vmap(node_rows)(jax.random.split(jax.random.fold_in(key, 205), MIDS))
    leading = rows_all[0]
    leading = jnp.where(leading == MID_CAP - 1, leading[0], leading).at[0].set(MID_CAP - 1)
    second = rows_all[1]
    second = jnp.where(second == 0, second[0], second).at[0].set(0)
    return rows_all.at[0].set(leading).at[1].set(second).astype(jnp.int32)


def touch_ends(result, rng, smallest, high):
    longest = result.shape.index(max(result.shape))
    spots = []
    for shift in (0, 1):
        where = [jax.random.randint(jax.random.fold_in(rng, axis), (), 0, length) for axis, length in enumerate(result.shape)]
        where[longest] = (where[longest] + shift) % result.shape[longest]
        spots.append(tuple(where))
    return result.at[spots[0]].set(smallest).at[spots[1]].set(high)


def block_scale(key, shape, cuts, least, high):
    def one(axis_at, parts):
        draws = jax.random.uniform(jax.random.fold_in(jax.random.fold_in(key, 6), axis_at), (parts,), jnp.float32, least / len(cuts), high / len(cuts))
        return jnp.repeat(jnp.exp(draws), shape[axis_at] // parts).reshape((-1,) + (1,) * (len(shape) - axis_at - 1))

    loudness = one(*cuts[0])
    for cut in cuts[1:]:
        loudness = loudness * one(*cut)
    return loudness


def centred(key, dims, scale, reach, pieces=(), kind=jnp.bfloat16):
    factor_of = block_scale(key, dims, pieces, -0.22, 0.18) if pieces else 1.0
    values = jax.random.normal(key, dims, jnp.float32) * scale * factor_of
    return jnp.minimum(jnp.maximum(values, -reach), reach).astype(kind)


def setup_inputs(seed: int = 0) -> dict:
    seeds = jax.random.split(jax.random.key(seed), 19)
    return {
        "stream": centred(seeds[0], (REQUESTS, D), 0.25, 1.5, ((0, 16),)),
        "attn_gain": jnp.clip(1.0 + 0.15 * jax.random.normal(seeds[1], (D,), jnp.float32), 0.25, 1.75).astype(jnp.bfloat16),
        "mlp_gain": jnp.clip(1.0 + 0.15 * jax.random.normal(seeds[2], (D,), jnp.float32), 0.25, 1.75).astype(jnp.bfloat16),
        "w_query": centred(seeds[3], (D, HEADS * HEAD_DIM), D ** -0.5, 0.125, ((1, 8),)),
        "w_keyval": draw_w_keyval(jax.random.fold_in(seeds[18], 71), 0),
        "w_out": centred(seeds[5], (HEADS * HEAD_DIM, D), (HEADS * HEAD_DIM) ** -0.5, 0.125, ((0, 8),)),
        "w_gate_up": centred(seeds[6], (D, 2, FF), D ** -0.5, 0.125, ((2, 8),)),
        "w_down": centred(seeds[7], (FF, D), FF ** -0.5, 0.0625, ((0, 8),)),
        "root_cache": draw_root_cache(jax.random.fold_in(seeds[18], 71), 0),
        "mid_cache": draw_mid_cache(jax.random.fold_in(seeds[18], 71), 0),
        "leaf_cache": draw_leaf_cache(jax.random.fold_in(seeds[18], 71), 0),
        "held_hidden": centred(seeds[11], (MIDS, RECOMP, D), 1.0, 6.0, ((0, 16), (2, 8))),
        "recompute_rows": draw_recompute_rows(jax.random.fold_in(seeds[18], 71), 0),
        "root_len": draw_root_len(jax.random.fold_in(seeds[18], 71), 0),
        "mid_len": draw_mid_len(jax.random.fold_in(seeds[18], 71), 0),
        "leaf_len": draw_leaf_len(jax.random.fold_in(seeds[18], 71), 0),
        "mid_parent": touch_ends(jax.random.randint(seeds[16], (MIDS,), 0, ROOTS), jax.random.fold_in(seeds[16], 1), 0, ROOTS - 1).astype(jnp.int32),
        "leaf_parent": touch_ends(jax.random.randint(seeds[17], (REQUESTS,), 0, MIDS), jax.random.fold_in(seeds[17], 1), 0, MIDS - 1).astype(jnp.int32),
    }


EPSILON = 1e-05
THETA_BASE = 130000.0
NEG_FILL = -1e+30

def rms_scale(values, gain):
    return values * lax.rsqrt(lax.optimization_barrier(jnp.mean(values * values, axis=-1, keepdims=True)) + EPSILON) * gain.astype(jnp.float32)

def rotate(values, positions):
    half_dim = values.shape[-1] // 2
    inv_freq = jnp.exp(jnp.arange(half_dim, dtype=jnp.float32) * (-2.0 * math.log(THETA_BASE) / values.shape[-1]))
    angles = positions.astype(jnp.float32)[..., None, None] * inv_freq
    cosines = jnp.cos(angles)
    sines = jnp.sin(angles)
    leading = values[..., :half_dim]
    trailing = values[..., half_dim:]
    return jnp.concatenate([leading * cosines - trailing * sines, trailing * cosines + leading * sines], axis=-1)

def reference(stream, attn_gain, mlp_gain, w_query, w_keyval, w_out, w_gate_up, w_down, root_cache, mid_cache, leaf_cache, held_hidden, recompute_rows, root_len, mid_len, leaf_len, mid_parent, leaf_parent):
    width_all = HEADS * HEAD_DIM
    score_scale = HEAD_DIM ** (-0.5)
    stream_float = stream.astype(jnp.float32)
    normed = rms_scale(stream_float, attn_gain).astype(jnp.bfloat16)
    req_roots = mid_parent[leaf_parent]
    positions = root_len[req_roots] + mid_len[leaf_parent] + leaf_len
    queries = rotate(jnp.dot(normed, w_query, preferred_element_type=jnp.float32).reshape(REQUESTS, HEADS, HEAD_DIM), positions).astype(jnp.bfloat16)
    fresh = jnp.dot(normed, w_keyval.reshape(D, 2 * width_all), preferred_element_type=jnp.float32).reshape(REQUESTS, 2, HEADS, HEAD_DIM)
    key_new = rotate(fresh[:, 0], positions).astype(jnp.bfloat16)
    value_new = fresh[:, 1].astype(jnp.bfloat16)
    held_normed = rms_scale(held_hidden.astype(jnp.float32), attn_gain).astype(jnp.bfloat16)
    rebuilt = jnp.dot(held_normed.reshape(MIDS * RECOMP, D), w_keyval.reshape(D, 2 * width_all), preferred_element_type=jnp.float32).reshape(MIDS, RECOMP, 2, HEADS, HEAD_DIM)
    rebuilt_pos = root_len[mid_parent][:, None] + recompute_rows
    rebuilt = jnp.stack([rotate(rebuilt[:, :, 0], rebuilt_pos), rebuilt[:, :, 1]], axis=2).astype(jnp.bfloat16).reshape(MIDS, RECOMP, 2, width_all)
    node_ids = jnp.arange(MIDS, dtype=jnp.int32)[:, None]
    mid_fixed = mid_cache.at[node_ids, recompute_rows].set(rebuilt)
    root_float = root_cache.astype(jnp.float32).reshape(ROOTS, ROOT_TOK, 2, HEADS, HEAD_DIM)
    mid_float = mid_fixed.astype(jnp.float32).reshape(MIDS, MID_CAP, 2, HEADS, HEAD_DIM)
    leaf_float = leaf_cache.astype(jnp.float32).reshape(REQUESTS, LEAF_CAP, 2, HEADS, HEAD_DIM)

    def attend(item):
        request, root_id, middle = item
        query_f = queries[request].astype(jnp.float32)
        tables = [root_float[root_id], mid_float[middle], leaf_float[request]]
        lives = [jnp.arange(ROOT_TOK, dtype=jnp.int32) < root_len[root_id], jnp.arange(MID_CAP, dtype=jnp.int32) < mid_len[middle], jnp.arange(LEAF_CAP, dtype=jnp.int32) < leaf_len[request]]
        scores = [jnp.einsum('hd,khd->hk', query_f, tables[number][:, 0]) * score_scale for number in range(3)]
        self_score = lax.optimization_barrier(jnp.sum(query_f * key_new[request].astype(jnp.float32), axis=-1)) * score_scale
        row_max = self_score
        for number in range(3):
            row_max = jnp.maximum(row_max, lax.optimization_barrier(jnp.max(jnp.where(lives[number], scores[number], NEG_FILL), axis=1)))
        self_weight = jnp.exp(self_score - row_max)
        row_sum = self_weight
        weighted = lax.optimization_barrier(self_weight.astype(jnp.bfloat16)).astype(jnp.float32)[:, None] * value_new[request].astype(jnp.float32)
        for number in range(3):
            weights = jnp.where(lives[number], jnp.exp(scores[number] - row_max[:, None]), 0.0)
            row_sum = row_sum + lax.optimization_barrier(jnp.sum(weights, axis=1))
            rounded = lax.optimization_barrier(weights.astype(jnp.bfloat16)).astype(jnp.float32)
            weighted = weighted + jnp.einsum('hk,khd->hd', rounded, tables[number][:, 1])
        return (weighted / row_sum[:, None]).astype(jnp.bfloat16).reshape(width_all)
    attended = lax.map(attend, (jnp.arange(REQUESTS, dtype=jnp.int32), req_roots, leaf_parent))
    residual = stream_float + jnp.dot(attended, w_out, preferred_element_type=jnp.float32)
    mixed_in = rms_scale(residual, mlp_gain).astype(jnp.bfloat16)
    projected = jnp.dot(mixed_in, w_gate_up.reshape(D, 2 * FF), preferred_element_type=jnp.float32).reshape(REQUESTS, 2, FF)
    hidden = (jax.nn.silu(projected[:, 0]) * projected[:, 1]).astype(jnp.bfloat16)
    return (residual + jnp.dot(hidden, w_down, preferred_element_type=jnp.float32)).astype(jnp.bfloat16)
```

```python
import math

import jax
import jax.numpy as jnp
import numpy as np
from jax import lax
from jax.experimental import pallas as pl
from jax.experimental.pallas import tpu as pltpu
from jax.sharding import PartitionSpec as P

F32 = jnp.float32
BF16 = jnp.bfloat16
I32 = jnp.int32
D = 2048
HEAD_DIM = 64
EPSILON = 1e-05
THETA_BASE = 130000.0
NEG_FILL = -1e30
NREQ = 16
NTP = 8
ROWS = 32
WIDTH = 256
HEADS = 4
BLOCK = 32
MAX_BLOCKS = 32
STATS = 128
MSG = WIDTH + STATS


def iota(shape, dim):
    return lax.broadcasted_iota(I32, shape, dim)


def dot(a, b):
    return jnp.dot(a, b, preferred_element_type=F32)


def dot_t(a, b):
    return lax.dot_general(a, b, (((1,), (1,)), ((), ())), preferred_element_type=F32)


def as_col(row):
    n = row.shape[1]
    eye = iota((n, n), 0) == iota((n, n), 1)
    return jnp.sum(jnp.where(eye, row, 0.0), axis=1, keepdims=True)


def as_row(col):
    n = col.shape[0]
    eye = iota((n, n), 0) == iota((n, n), 1)
    return jnp.sum(jnp.where(eye, col, 0.0), axis=0, keepdims=True)


def rope_tables(positions, inv_freq):
    angles = positions * inv_freq
    return jnp.cos(angles), jnp.sin(angles)


def rope(values, cosines, sines):
    n = values.shape[0]
    low = (iota((n, 128), 1) % 64) < 32
    parts = []
    for t in range(2):
        v = values[:, t * 128 : (t + 1) * 128]
        turned = jnp.where(low, -pltpu.roll(v, 96, 1), pltpu.roll(v, 32, 1))
        parts.append(v * cosines + turned * sines)
    return jnp.concatenate(parts, axis=1)


def shift_pairs(scores):
    width = scores.shape[1]
    return jnp.concatenate(
        [pltpu.roll(scores[:, i : i + 128], 1, 1) for i in range(0, width, 128)], axis=1
    )


def three_terms(values):
    first = values.astype(BF16)
    rest = values - first.astype(F32)
    second = rest.astype(BF16)
    third = (rest - second.astype(F32)).astype(BF16)
    return first, second, third


def project_kernel(
    stream_ref,
    gain_ref,
    wq_hbm,
    wkv_hbm,
    leaf_hbm,
    held_ref,
    lp_ref,
    mp_ref,
    rl_ref,
    ml_ref,
    ll_ref,
    rr_ref,
    freq_ref,
    qall_out,
    knew_out,
    vnew_out,
    oleaf_out,
    lleaf_out,
    wq_v,
    wkv_v,
    wk_v,
    wv_v,
    leaf_v,
    held_v,
    qall_v,
    qbd_v,
    score_v,
    acc_v,
    copy_sem,
    hsend,
    hrecv,
    qsend,
    qrecv,
):
    rank = lax.axis_index("req")
    tp = lax.axis_index("tp")
    barrier = pltpu.get_barrier_semaphore()
    for d in range(1, NREQ):
        pl.semaphore_signal(barrier, inc=1, device_id={"req": lax.rem(rank + d, NREQ)})
    for d in range(1, NTP):
        pl.semaphore_signal(barrier, inc=1, device_id={"tp": lax.rem(tp + d, NTP)})
    wq_copy = pltpu.make_async_copy(wq_hbm, wq_v, copy_sem.at[0])
    wkv_copy = pltpu.make_async_copy(wkv_hbm.reshape(2 * D, WIDTH), wkv_v, copy_sem.at[1])
    leaf_copy = pltpu.make_async_copy(leaf_hbm.reshape(8192, WIDTH), leaf_v, copy_sem.at[2])
    wq_copy.start()
    wkv_copy.start()
    leaf_copy.start()
    pl.semaphore_wait(barrier, NREQ + NTP - 2)
    held_copies = []
    for d in range(1, NTP):
        copy = pltpu.make_async_remote_copy(
            src_ref=held_ref,
            dst_ref=held_v.at[tp],
            send_sem=hsend.at[d],
            recv_sem=hrecv.at[d],
            device_id={"tp": lax.rem(tp + d, NTP)},
        )
        copy.start()
        held_copies.append(copy)
    held_v[tp] = held_ref[...]

    gain = gain_ref[...].astype(F32)
    x = stream_ref[...].astype(F32)
    normed = (
        x * lax.rsqrt(jnp.mean(x * x, axis=-1, keepdims=True) + EPSILON) * gain
    ).astype(BF16)

    lp_row = lp_ref[...]
    mp_col = as_col(mp_ref[...].astype(F32))
    ml_col = as_col(ml_ref[...].astype(F32))
    rl_row = rl_ref[...].astype(F32)
    parent_len = jnp.sum(
        jnp.where(iota((16, 8), 1).astype(F32) == mp_col, rl_row, 0.0), axis=1, keepdims=True
    )
    mid_base = parent_len + ml_col
    belongs = iota((16, 512), 0) == lp_row
    base_row = jnp.sum(jnp.where(belongs, mid_base, 0.0), axis=0, keepdims=True)
    own = iota((ROWS, 512), 1) == iota((ROWS, 512), 0) + rank * ROWS
    leaf_len_row = ll_ref[...].astype(F32)
    positions = jnp.sum(jnp.where(own, base_row, 0.0), axis=1, keepdims=True) + as_col(leaf_len_row)
    freq = freq_ref[...]
    cosines, sines = rope_tables(positions, freq)

    wq_copy.wait()
    queries = rope(dot(normed, wq_v[...]), cosines, sines).astype(BF16)
    queries = (queries.astype(F32) * (HEAD_DIM**-0.5)).astype(BF16)
    own_rows = pl.ds(pl.multiple_of(rank * ROWS, ROWS), ROWS)
    qall_v[own_rows, :] = queries
    q_copies = []
    for d in range(1, NREQ):
        copy = pltpu.make_async_remote_copy(
            src_ref=qall_v.at[own_rows],
            dst_ref=qall_v.at[own_rows],
            send_sem=qsend.at[d],
            recv_sem=qrecv.at[d],
            device_id={"req": lax.rem(rank + d, NREQ)},
        )
        copy.start()
        q_copies.append(copy)

    r2, c2 = iota((256, 256), 0), iota((256, 256), 1)
    split = (c2 == jnp.where(r2 < 128, 2 * r2, 2 * r2 - 255)).astype(BF16)
    wkv_copy.wait()
    for k in range(16):
        both = dot(split, wkv_v[k * 256 : (k + 1) * 256, :]).astype(BF16)
        wk_v[k * 128 : (k + 1) * 128, :] = both[:128]
        wv_v[k * 128 : (k + 1) * 128, :] = both[128:]
    key_new = rope(dot(normed, wk_v[...]), cosines, sines).astype(BF16)
    value_new = dot(normed, wv_v[...]).astype(BF16)

    repeat = (iota((256, ROWS), 0) // 8 == iota((256, ROWS), 1)).astype(BF16)
    head_mask = (r2 % 8) == (c2 // HEAD_DIM)
    qbd = jnp.where(head_mask, dot(repeat, queries), 0.0)
    qbd_v[...] = qbd.astype(BF16)
    self_score = jnp.sum(qbd * dot(repeat, key_new), axis=1, keepdims=True)
    live_len = jnp.sum(repeat.astype(F32) * leaf_len_row, axis=1, keepdims=True)
    leaf_copy.wait()
    for r in range(ROWS):
        score_v[r * 8 : (r + 1) * 8, :] = dot_t(
            qbd_v[r * 8 : (r + 1) * 8, :], leaf_v[r * 256 : (r + 1) * 256, :]
        )
    live = ((c2 % 2) == 1) & ((c2 // 2).astype(F32) < live_len)
    scores = jnp.where(live, shift_pairs(score_v[...]), NEG_FILL)
    best = jnp.maximum(jnp.max(scores, axis=1, keepdims=True), self_score)
    weights = jnp.exp(scores - best)
    self_weight = jnp.exp(self_score - best)
    row_sum = jnp.sum(weights, axis=1, keepdims=True) + self_weight
    qbd_v[...] = weights.astype(BF16)
    for r in range(ROWS):
        acc_v[r * 8 : (r + 1) * 8, :] = dot(
            qbd_v[r * 8 : (r + 1) * 8, :], leaf_v[r * 256 : (r + 1) * 256, :]
        )
    acc = acc_v[...] + self_weight.astype(BF16).astype(F32) * dot(repeat, value_new)
    acc = jnp.where(head_mask, acc / row_sum, 0.0)
    oleaf_out[...] = jnp.sum(acc.reshape(ROWS, 8, WIDTH), axis=1)
    lse = best + jnp.log(row_sum)
    spread = jnp.where((r2 % 8)[:, :STATS] == c2[:, :STATS], lse, 0.0)
    lleaf_out[...] = jnp.sum(spread.reshape(ROWS, 8, STATS), axis=1)

    held_pos = jnp.sum(
        jnp.where(iota((16, 1), 0) == rank, parent_len, 0.0), axis=0, keepdims=True
    ) + as_col(rr_ref[...].astype(F32))
    held_cos, held_sin = rope_tables(held_pos, freq)
    for copy in held_copies:
        copy.wait_recv()
    total = jnp.zeros((256, 1), F32)
    for c in range(NTP):
        part = held_v[c].astype(F32)
        total = total + jnp.sum(part * part, axis=1, keepdims=True)
    scale = lax.rsqrt(total * (1.0 / D) + EPSILON)
    keys = jnp.zeros((256, WIDTH), F32)
    values = jnp.zeros((256, WIDTH), F32)
    for c in range(NTP):
        part = (held_v[c].astype(F32) * scale * gain[:, c * 256 : (c + 1) * 256]).astype(BF16)
        keys = keys + dot(part, wk_v[c * 256 : (c + 1) * 256, :])
        values = values + dot(part, wv_v[c * 256 : (c + 1) * 256, :])
    knew_out[...] = rope(keys, held_cos, held_sin).astype(BF16)
    vnew_out[...] = values.astype(BF16)

    for copy in q_copies:
        copy.wait_recv()
    qall_out[...] = qall_v[...]
    for copy in held_copies:
        copy.wait_send()
    for copy in q_copies:
        copy.wait_send()


def attend_kernel(
    rl_s,
    ml_s,
    rank_s,
    qall_ref,
    root_hbm,
    mid_hbm,
    knew_ref,
    vnew_ref,
    lp_ref,
    mp_ref,
    rr_ref,
    out_ref,
    root_v,
    mid_v,
    qs_v,
    xs_v,
    bias_v,
    table_v,
    table_s,
    m_v,
    l_v,
    acc_v,
    copy_sem,
):
    rank = rank_s[0]
    root_copy = pltpu.make_async_copy(root_hbm.reshape(8, 512, WIDTH), root_v, copy_sem.at[0])
    mid_copy = pltpu.make_async_copy(mid_hbm.reshape(4096, WIDTH), mid_v, copy_sem.at[1])
    root_copy.start()
    mid_copy.start()
    belongs = iota((16, 512), 0) == lp_ref[...]
    belongs_f = belongs.astype(F32)
    before = (iota((512, 512), 0) < iota((512, 512), 1)).astype(BF16)
    order = dot(belongs_f.astype(BF16), before)
    counts = jnp.sum(belongs_f, axis=1, keepdims=True)
    blocks = jnp.floor((counts + (BLOCK - 1)) * (1.0 / BLOCK))
    start = jnp.sum(
        jnp.where(iota((16, 16), 1) < iota((16, 16), 0), as_row(blocks), 0.0), axis=1, keepdims=True
    )
    dest = jnp.sum(jnp.where(belongs, order + start * BLOCK, 0.0), axis=0, keepdims=True)
    lane = iota((16, 128), 1).astype(F32)
    node = jnp.sum((start + blocks <= lane).astype(F32), axis=0, keepdims=True)
    of_node = iota((16, 128), 0).astype(F32) == node
    mp_col = as_col(mp_ref[...].astype(F32))
    root = jnp.sum(jnp.where(of_node, mp_col, 0.0), axis=0, keepdims=True)
    used = jnp.sum(blocks, axis=0, keepdims=True)
    row8 = iota((8, 128), 0)
    table = jnp.where(row8 == 0, node, jnp.where(row8 == 1, root, used))
    table_v[...] = table.astype(I32)
    table_copy = pltpu.make_async_copy(table_v, table_s, copy_sem.at[2])
    table_copy.start()

    dest_i = dest.astype(I32)
    pick = (iota((MAX_BLOCKS * BLOCK, 512), 0) == dest_i).astype(BF16)
    qs_v[...] = dot(pick, qall_ref[...]).astype(BF16)
    xs_v[...] = jnp.zeros_like(xs_v)

    own_len = ml_s[rank]
    rr = rr_ref[...]
    slot_col = as_col(rr.astype(F32)).astype(I32)
    hit_hi = (iota((16, 256), 0) == rr // 128).astype(BF16)
    hit_lo = (iota((256, 256), 1) == 2 * (slot_col % 128) + 1).astype(BF16)
    replaced = dot(hit_hi, hit_lo)
    lane16 = iota((16, 256), 1)
    token = iota((16, 256), 0) * 128 + lane16 // 2
    alive = ((lane16 % 2) == 1) & (token < own_len) & (replaced < 0.5)
    bias_v[...] = jnp.where(alive, 0.0, NEG_FILL)
    new_bias = jnp.where(rr < own_len, 0.0, NEG_FILL)

    lane512 = iota((1, 512), 1)
    head_row = iota((128, WIDTH), 0) // BLOCK
    head_mask = (head_row == iota((128, WIDTH), 1) // HEAD_DIM).astype(BF16)
    lane_head = iota((BLOCK, WIDTH), 1) // HEAD_DIM
    lane128 = iota((BLOCK, STATS), 1)
    table_copy.wait()
    root_copy.wait()
    mid_copy.wait()
    n_blocks = table_s[2, 0]

    def update(scores, values):
        m_old = m_v[...]
        m_new = jnp.maximum(m_old, jnp.max(scores, axis=1, keepdims=True))
        fade = jnp.exp(m_old - m_new)
        weights = jnp.exp(scores - m_new)
        m_v[...] = m_new
        l_v[...] = l_v[...] * fade + jnp.sum(weights, axis=1, keepdims=True)
        acc_v[...] = acc_v[...] * fade + dot(weights.astype(BF16), values)

    def one_block(j, _):
        at = pl.ds(pl.multiple_of(j * BLOCK, BLOCK), BLOCK)
        q = qs_v[at, :]
        qbd = jnp.concatenate([q] * HEADS, axis=0) * head_mask
        node_j = table_s[0, j]
        root_j = table_s[1, j]
        pairs = root_v[root_j]
        live = ((lane512 % 2) == 1) & (rank * 256 + lane512 // 2 < rl_s[root_j])
        bias = jnp.where(live, 0.0, NEG_FILL)
        scores = shift_pairs(dot_t(qbd, pairs)) + bias
        m = jnp.max(scores, axis=1, keepdims=True)
        weights = jnp.exp(scores - m)
        m_v[...] = m
        l_v[...] = jnp.sum(weights, axis=1, keepdims=True)
        acc_v[...] = dot(weights.astype(BF16), pairs)

        @pl.when(node_j == rank)
        def _():
            for c in range(8):
                chunk = mid_v[c * 512 : (c + 1) * 512, :]
                bias_c = jnp.concatenate(
                    [bias_v[2 * c : 2 * c + 1, :], bias_v[2 * c + 1 : 2 * c + 2, :]], axis=1
                )
                update(shift_pairs(dot_t(qbd, chunk)) + bias_c, chunk)
            update(dot_t(qbd, knew_ref[...]) + new_bias, vnew_ref[...])

        l = l_v[...]
        out = acc_v[...] / l
        lse = m_v[...] + jnp.log(l)
        picked = jnp.zeros((BLOCK, WIDTH), F32)
        stats = jnp.zeros((BLOCK, STATS), F32)
        for h in range(HEADS):
            rows = slice(h * BLOCK, (h + 1) * BLOCK)
            picked = jnp.where(lane_head == h, out[rows], picked)
            stats = jnp.where((lane128 % 4) == h, lse[rows], stats)
        a, b, c = three_terms(stats)
        stats = jnp.where(
            lane128 < 4,
            a.astype(F32),
            jnp.where(lane128 < 8, b.astype(F32), jnp.where(lane128 < 12, c.astype(F32), 0.0)),
        )
        xs_v[at, :] = jnp.concatenate([picked, stats], axis=1).astype(BF16)
        return 0

    lax.fori_loop(0, n_blocks, one_block, 0)
    dest_col = as_col(dest).astype(I32)
    back = (iota((512, MAX_BLOCKS * BLOCK), 1) == dest_col).astype(BF16)
    out_ref[...] = dot(back, xs_v[...]).astype(BF16)


def finish_kernel(
    parts_ref,
    oleaf_ref,
    lleaf_ref,
    stream_ref,
    gain_ref,
    wout_hbm,
    wgu_hbm,
    wdn_hbm,
    out_ref,
    wout_v,
    wgu_v,
    wdn_v,
    in_v,
    rs_out,
    rs_in,
    ag_v,
    ds_out,
    ds_in,
    proj_v,
    copy_sem,
    asend,
    arecv,
    rsend,
    rrecv,
    gsend,
    grecv,
    dsend,
    drecv,
):
    rank = lax.axis_index("req")
    tp = lax.axis_index("tp")
    barrier = pltpu.get_barrier_semaphore()
    for d in range(1, NREQ):
        pl.semaphore_signal(barrier, inc=1, device_id={"req": lax.rem(rank + d, NREQ)})
    for d in range(1, NTP):
        pl.semaphore_signal(barrier, inc=1, device_id={"tp": lax.rem(tp + d, NTP)})
    wout_copy = pltpu.make_async_copy(wout_hbm, wout_v, copy_sem.at[0])
    wgu_copy = pltpu.make_async_copy(wgu_hbm.reshape(2 * D, 1024), wgu_v, copy_sem.at[1])
    wdn_copy = pltpu.make_async_copy(wdn_hbm, wdn_v, copy_sem.at[2])
    wout_copy.start()
    wgu_copy.start()
    wdn_copy.start()
    pl.semaphore_wait(barrier, NREQ + NTP - 2)
    copies = []
    for d in range(1, NREQ):
        peer = lax.rem(rank + d, NREQ)
        copy = pltpu.make_async_remote_copy(
            src_ref=parts_ref.at[pl.ds(pl.multiple_of(peer * ROWS, ROWS), ROWS)],
            dst_ref=in_v.at[d],
            send_sem=asend.at[d],
            recv_sem=arecv.at[d],
            device_id={"req": peer},
        )
        copy.start()
        copies.append(copy)
    in_v[0] = parts_ref[pl.ds(pl.multiple_of(rank * ROWS, ROWS), ROWS), :]
    i2, j2 = iota((256, 512), 0), iota((256, 512), 1)
    to_even = (j2 == 2 * i2).astype(BF16)
    to_odd = (j2 == 2 * i2 + 1).astype(BF16)
    e0, e1 = iota((STATS, WIDTH), 0), iota((STATS, WIDTH), 1)
    expand = ((e0 < 8) & ((e0 % 4) == e1 // HEAD_DIM)).astype(BF16)
    lane = iota((ROWS, STATS), 1)
    for copy in copies:
        copy.wait_recv()
    lses = []
    for s in range(NREQ):
        stats = in_v[s, :, WIDTH:].astype(F32)
        lses.append(stats + pltpu.roll(stats, 124, 1) + pltpu.roll(stats, 120, 1))
    lses.append(lleaf_ref[...])
    best = lses[0]
    for value in lses[1:]:
        best = jnp.maximum(best, value)
    shares = [jnp.exp(value - best) for value in lses]
    total = shares[0]
    for value in shares[1:]:
        total = total + value
    attended = jnp.zeros((ROWS, WIDTH), F32)
    for s in range(NREQ + 1):
        share = shares[s] / total
        first = share.astype(BF16)
        second = (share - first.astype(F32)).astype(BF16)
        both = jnp.where(
            lane < 4, first.astype(F32), jnp.where(lane < 8, pltpu.roll(second.astype(F32), 4, 1), 0.0)
        )
        factor = dot(both.astype(BF16), expand)
        source = in_v[s, :, :WIDTH].astype(F32) if s < NREQ else oleaf_ref[...]
        attended = attended + factor * source
    attended = attended.astype(BF16)

    wout_copy.wait()
    rs_copies = []
    for d in range(1, NTP):
        peer = lax.rem(tp + d, NTP)
        cols = pl.ds(pl.multiple_of(peer * WIDTH, WIDTH), WIDTH)
        rs_out[d] = dot(attended, wout_v[:, cols]).astype(BF16)
        copy = pltpu.make_async_remote_copy(
            src_ref=rs_out.at[d],
            dst_ref=rs_in.at[d],
            send_sem=rsend.at[d],
            recv_sem=rrecv.at[d],
            device_id={"tp": peer},
        )
        copy.start()
        rs_copies.append(copy)
    own_cols = pl.ds(pl.multiple_of(tp * WIDTH, WIDTH), WIDTH)
    residual = dot(attended, wout_v[:, own_cols]) + stream_ref[:, own_cols].astype(F32)
    for d in range(1, NTP):
        rs_copies[d - 1].wait_recv()
        residual = residual + rs_in[d].astype(F32)

    square = jnp.sum(residual * residual, axis=1, keepdims=True)
    a, b, c = three_terms(jnp.broadcast_to(square, (ROWS, STATS)))
    stats = jnp.where(
        lane == 0,
        a.astype(F32),
        jnp.where(lane == 1, b.astype(F32), jnp.where(lane == 2, c.astype(F32), 0.0)),
    )
    scaled = residual * gain_ref[:, own_cols].astype(F32)
    ag_v[0] = jnp.concatenate([scaled, stats], axis=1).astype(BF16)
    ag_copies = []
    for d in range(1, NTP):
        copy = pltpu.make_async_remote_copy(
            src_ref=ag_v.at[0],
            dst_ref=ag_v.at[d],
            send_sem=gsend.at[d],
            recv_sem=grecv.at[d],
            device_id={"tp": lax.rem(tp + d, NTP)},
        )
        copy.start()
        ag_copies.append(copy)
    wgu_copy.wait()
    squares = jnp.zeros((ROWS, STATS), F32)
    for d in range(NTP):
        if d > 0:
            ag_copies[d - 1].wait_recv()
        owner = lax.rem(tp + NTP - d, NTP)
        part = ag_v[d]
        squares = squares + part[:, WIDTH:].astype(F32)
        chunk = part[:, :WIDTH]
        mixed = jnp.concatenate([dot(chunk, to_even), dot(chunk, to_odd)], axis=0).astype(BF16)
        rows = pl.ds(pl.multiple_of(owner * 512, 512), 512)
        for n in range(4):
            cols = slice(n * 256, (n + 1) * 256)
            product = dot(mixed, wgu_v[rows, cols])
            if d == 0:
                proj_v[:, cols] = product
            else:
                proj_v[:, cols] += product
    mean = jnp.sum(squares, axis=1, keepdims=True) * (1.0 / D)
    scale = lax.rsqrt(mean + EPSILON)
    gate = proj_v[:ROWS, :] * scale
    up = proj_v[ROWS:, :] * scale
    hidden = (gate / (1.0 + jnp.exp(-gate)) * up).astype(BF16)

    wdn_copy.wait()
    ds_copies = []
    for d in range(1, NTP):
        peer = lax.rem(tp + d, NTP)
        cols = pl.ds(pl.multiple_of(peer * WIDTH, WIDTH), WIDTH)
        ds_out[d] = dot(hidden, wdn_v[:, cols]).astype(BF16)
        copy = pltpu.make_async_remote_copy(
            src_ref=ds_out.at[d],
            dst_ref=ds_in.at[d],
            send_sem=dsend.at[d],
            recv_sem=drecv.at[d],
            device_id={"tp": peer},
        )
        copy.start()
        ds_copies.append(copy)
    result = residual + dot(hidden, wdn_v[:, own_cols])
    for d in range(1, NTP):
        ds_copies[d - 1].wait_recv()
        result = result + ds_in[d].astype(F32)
    out_ref[...] = result.astype(BF16)
    for copy in copies + rs_copies + ag_copies + ds_copies:
        copy.wait_send()


VMEM = pl.BlockSpec(memory_space=pltpu.VMEM)
SMEM = pl.BlockSpec(memory_space=pltpu.SMEM)
ANY = pl.BlockSpec(memory_space=pl.ANY)
DMA = pltpu.SemaphoreType.DMA
LIMIT = 48 * 1024 * 1024


def on_device(
    stream,
    attn_gain,
    mlp_gain,
    w_query,
    w_keyval,
    w_out,
    w_gate_up,
    w_down,
    root_cache,
    mid_cache,
    leaf_cache,
    held_hidden,
    recompute_rows,
    root_len,
    mid_len,
    leaf_len,
    mid_parent,
    leaf_parent,
):
    freq = np.exp(np.arange(32, dtype=np.float32) * np.float32(-2.0 * math.log(THETA_BASE) / HEAD_DIM))
    freq = jnp.asarray(np.tile(freq.astype(np.float32), 4)[None, :])
    lp = leaf_parent.reshape(1, 512)
    mp = mid_parent.reshape(1, 16)
    qall, knew, vnew, oleaf, lleaf = pl.pallas_call(
        project_kernel,
        name="project",
        out_shape=(
            jax.ShapeDtypeStruct((512, WIDTH), BF16),
            jax.ShapeDtypeStruct((256, WIDTH), BF16),
            jax.ShapeDtypeStruct((256, WIDTH), BF16),
            jax.ShapeDtypeStruct((ROWS, WIDTH), F32),
            jax.ShapeDtypeStruct((ROWS, STATS), F32),
        ),
        in_specs=[VMEM, VMEM, ANY, ANY, ANY] + [VMEM] * 8,
        out_specs=(VMEM,) * 5,
        scratch_shapes=[
            pltpu.VMEM((D, WIDTH), BF16),
            pltpu.VMEM((2 * D, WIDTH), BF16),
            pltpu.VMEM((D, WIDTH), BF16),
            pltpu.VMEM((D, WIDTH), BF16),
            pltpu.VMEM((8192, WIDTH), BF16),
            pltpu.VMEM((NTP, 256, 256), BF16),
            pltpu.VMEM((512, WIDTH), BF16),
            pltpu.VMEM((256, WIDTH), BF16),
            pltpu.VMEM((256, WIDTH), F32),
            pltpu.VMEM((256, WIDTH), F32),
            DMA((3,)),
            DMA((NTP,)),
            DMA((NTP,)),
            DMA((NREQ,)),
            DMA((NREQ,)),
        ],
        compiler_params=pltpu.CompilerParams(
            collective_id=0, has_side_effects=True, vmem_limit_bytes=LIMIT
        ),
    )(
        stream,
        attn_gain.reshape(1, D),
        w_query,
        w_keyval,
        leaf_cache,
        held_hidden.reshape(256, 256),
        lp,
        mp,
        root_len.reshape(1, 8),
        mid_len.reshape(1, 16),
        leaf_len.reshape(1, ROWS),
        recompute_rows,
        freq,
    )
    rank = lax.axis_index("req").reshape(1).astype(I32)
    parts = pl.pallas_call(
        attend_kernel,
        name="attend",
        out_shape=jax.ShapeDtypeStruct((512, MSG), BF16),
        in_specs=[SMEM, SMEM, SMEM, VMEM, ANY, ANY] + [VMEM] * 5,
        out_specs=VMEM,
        scratch_shapes=[
            pltpu.VMEM((8, 512, WIDTH), BF16),
            pltpu.VMEM((4096, WIDTH), BF16),
            pltpu.VMEM((MAX_BLOCKS * BLOCK, WIDTH), BF16),
            pltpu.VMEM((MAX_BLOCKS * BLOCK, MSG), BF16),
            pltpu.VMEM((16, 256), F32),
            pltpu.VMEM((8, 128), I32),
            pltpu.SMEM((8, 128), I32),
            pltpu.VMEM((128, 1), F32),
            pltpu.VMEM((128, 1), F32),
            pltpu.VMEM((128, WIDTH), F32),
            DMA((3,)),
        ],
        compiler_params=pltpu.CompilerParams(vmem_limit_bytes=LIMIT),
    )(
        root_len,
        mid_len,
        rank,
        qall,
        root_cache,
        mid_cache,
        knew,
        vnew,
        lp,
        mp,
        recompute_rows,
    )
    return pl.pallas_call(
        finish_kernel,
        name="finish",
        out_shape=jax.ShapeDtypeStruct((ROWS, WIDTH), BF16),
        in_specs=[VMEM] * 5 + [ANY] * 3,
        out_specs=VMEM,
        scratch_shapes=[
            pltpu.VMEM((WIDTH, D), BF16),
            pltpu.VMEM((2 * D, 1024), BF16),
            pltpu.VMEM((1024, D), BF16),
            pltpu.VMEM((NREQ, ROWS, MSG), BF16),
            pltpu.VMEM((NTP, ROWS, WIDTH), BF16),
            pltpu.VMEM((NTP, ROWS, WIDTH), BF16),
            pltpu.VMEM((NTP, ROWS, MSG), BF16),
            pltpu.VMEM((NTP, ROWS, WIDTH), BF16),
            pltpu.VMEM((NTP, ROWS, WIDTH), BF16),
            pltpu.VMEM((2 * ROWS, 1024), F32),
            DMA((3,)),
            DMA((NREQ,)),
            DMA((NREQ,)),
            DMA((NTP,)),
            DMA((NTP,)),
            DMA((NTP,)),
            DMA((NTP,)),
            DMA((NTP,)),
            DMA((NTP,)),
        ],
        compiler_params=pltpu.CompilerParams(
            collective_id=1, has_side_effects=True, vmem_limit_bytes=LIMIT
        ),
    )(
        parts,
        oleaf,
        lleaf,
        stream,
        mlp_gain.reshape(1, D),
        w_out,
        w_gate_up,
        w_down,
    )


def solution(mesh):
    placed = (
        P("req", None),
        P(),
        P(),
        P(None, "tp"),
        P(None, None, "tp"),
        P("tp", None),
        P(None, None, "tp"),
        P("tp", None),
        P(None, "req", None, "tp"),
        P("req", None, None, "tp"),
        P("req", None, None, "tp"),
        P("req", None, "tp"),
        P("req", None),
        P(),
        P(),
        P("req"),
        P(),
        P(),
    )
    return jax.shard_map(
        on_device, mesh=mesh, in_specs=placed, out_specs=P("req", "tp"), check_vma=False
    )
```

```python
import functools
import math

import jax
import jax.numpy as jnp
import numpy as np
from jax import lax
from jax.experimental import pallas as pl
from jax.experimental.pallas import tpu as pltpu
from jax.sharding import PartitionSpec as P

F32 = jnp.float32
BF16 = jnp.bfloat16
I32 = jnp.int32
D = 2048
HEAD_DIM = 64
EPSILON = 1e-05
THETA_BASE = 130000.0
NEG_FILL = -1e30
NREQ = 16
NTP = 8
ROWS = 32
WIDTH = 256
HEADS = 4
BLOCK = 32
BLOCKS = 24
SORTED = BLOCKS * BLOCK
MID_ROWS = 64
STATS = 128
MSG = WIDTH + STATS


def iota(shape, dim):
    return lax.broadcasted_iota(I32, shape, dim)


def dot(a, b):
    return jnp.dot(a, b, preferred_element_type=F32)


def dot_t(a, b):
    return lax.dot_general(a, b, (((1,), (1,)), ((), ())), preferred_element_type=F32)


def as_col(row):
    n = row.shape[1]
    eye = iota((n, n), 0) == iota((n, n), 1)
    return jnp.sum(jnp.where(eye, row, 0.0), axis=1, keepdims=True)


def as_row(col):
    n = col.shape[0]
    eye = iota((n, n), 0) == iota((n, n), 1)
    return jnp.sum(jnp.where(eye, col, 0.0), axis=0, keepdims=True)


def rope_tables(positions, inv_freq):
    angles = positions * inv_freq
    return jnp.cos(angles), jnp.sin(angles)


def rope(values, cosines, sines):
    n = values.shape[0]
    low = (iota((n, 128), 1) % 64) < 32
    parts = []
    for t in range(2):
        v = values[:, t * 128 : (t + 1) * 128]
        turned = jnp.where(low, -pltpu.roll(v, 96, 1), pltpu.roll(v, 32, 1))
        parts.append(v * cosines + turned * sines)
    return jnp.concatenate(parts, axis=1)


def shift_pairs(scores):
    width = scores.shape[1]
    return jnp.concatenate(
        [pltpu.roll(scores[:, i : i + 128], 1, 1) for i in range(0, width, 128)], axis=1
    )


def three_terms(values):
    first = values.astype(BF16)
    rest = values - first.astype(F32)
    second = rest.astype(BF16)
    third = (rest - second.astype(F32)).astype(BF16)
    return first, second, third


def total(values, axis):
    return jnp.sum(values, axis=axis, keepdims=True)


def head_columns(stacked, rows, width):
    lanes = iota((rows, width), 1)
    group = lanes // HEAD_DIM if width == WIDTH else lanes % HEADS
    picked = jnp.broadcast_to(stacked[:rows], (rows, width))
    for h in range(1, HEADS):
        picked = jnp.where(group == h, stacked[h * rows : (h + 1) * rows], picked)
    return picked


def packed(out, lse):
    lanes = iota(lse.shape, 1)
    a, b, c = three_terms(lse)
    stats = jnp.where(
        lanes < 4,
        a.astype(F32),
        jnp.where(lanes < 8, b.astype(F32), jnp.where(lanes < 12, c.astype(F32), 0.0)),
    )
    return jnp.concatenate([out, stats], axis=1).astype(BF16)


def unpacked_lse(stats):
    return stats + pltpu.roll(stats, 124, 1) + pltpu.roll(stats, 120, 1)


def split_pairs(split, pairs_v, first_v, second_v, tiles):
    for k in range(tiles):
        both = dot(split, pairs_v[k * 256 : (k + 1) * 256, :]).astype(BF16)
        first_v[k * 128 : (k + 1) * 128, :] = both[:128]
        second_v[k * 128 : (k + 1) * 128, :] = both[128:]


SMALL = (
    ((ROWS, D), BF16),
    ((D,), BF16),
    ((D,), BF16),
    ((512,), I32),
    ((16,), I32),
    ((8,), I32),
    ((16,), I32),
    ((ROWS,), I32),
    ((1, 256), I32),
    ((1, 128), F32),
)
WORK = dict(
    wq=((D, WIDTH), BF16),
    wkv=((2 * D, WIDTH), BF16),
    wk=((D, WIDTH), BF16),
    wv=((D, WIDTH), BF16),
    wout=((WIDTH, D), BF16),
    wgu=((2 * D, 1024), BF16),
    wdn=((1024, D), BF16),
    root=((4096, WIDTH), BF16),
    root_k=((8, 256, WIDTH), BF16),
    root_v=((8, 256, WIDTH), BF16),
    root_bias=((8, 1, 256), F32),
    mid=((4096, WIDTH), BF16),
    mid_k=((2048, WIDTH), BF16),
    mid_v=((2048, WIDTH), BF16),
    mid_bias=((16, 128), F32),
    leaf=((8192, WIDTH), BF16),
    held=((NTP, 256, 256), BF16),
    qall=((512, WIDTH), BF16),
    pick=((SORTED, 512), BF16),
    qs=((SORTED, WIDTH), BF16),
    table=((8, 128), I32),
    new_k=((256, WIDTH), BF16),
    new_v=((256, WIDTH), BF16),
    scores=((256, 2048), F32),
    weights=((256, 2048), BF16),
    leaf_q=((256, WIDTH), BF16),
    leaf_s=((256, WIDTH), F32),
    parts=((512, MSG), BF16),
    arrived=((NREQ, ROWS, MSG), BF16),
    rs_out=((NTP, ROWS, WIDTH), BF16),
    rs_in=((NTP, ROWS, WIDTH), BF16),
    ag=((NTP, ROWS, MSG), BF16),
    ds_out=((NTP, ROWS, WIDTH), BF16),
    ds_in=((NTP, ROWS, WIDTH), BF16),
    proj=((2 * ROWS, 1024), F32),
)


def sized(passes):
    gathered = -(-(SORTED + passes * MID_ROWS) // 128) * 128
    return dict(WORK, back=((512, gathered), BF16), xs=((gathered, MSG), BF16))


def layer_kernel(passes, *refs):
    sizes = sized(passes)
    gathered = sizes["xs"][0][0]
    mid_end = SORTED + passes * MID_ROWS
    small_hbm = refs[:10]
    wq_hbm, wkv_hbm, wout_hbm, wgu_hbm, wdn_hbm, root_hbm, mid_hbm, leaf_hbm, held_hbm = refs[10:19]
    out_ref = refs[19]
    small = refs[20:30]
    v = dict(zip(sizes, refs[30 : 30 + len(sizes)]))
    table_s, copy_sem, hsem, qsem, asem, rsem, gsem, dsem = refs[30 + len(sizes) :]
    stream_v, again_v, mgain_v, lp_v, mp_v, rl_v, ml_v, ll_v, rr_v, freq_v = small
    rank = lax.axis_index("req")
    tp = lax.axis_index("tp")

    def req_peer(d):
        return lax.rem(rank + d, NREQ)

    def tp_peer(d):
        return lax.rem(tp + d, NTP)

    def send(src, dst, sems, d, target):
        copy = pltpu.make_async_remote_copy(
            src_ref=src,
            dst_ref=dst,
            send_sem=sems.at[0, d],
            recv_sem=sems.at[1, d],
            device_id=target,
        )
        copy.start()
        return copy

    barrier = pltpu.get_barrier_semaphore()
    for d in range(1, NREQ):
        pl.semaphore_signal(barrier, inc=1, device_id={"req": req_peer(d)})
    for d in range(1, NTP):
        pl.semaphore_signal(barrier, inc=1, device_id={"tp": tp_peer(d)})

    small_copies = [
        pltpu.make_async_copy(src, dst, copy_sem.at[i])
        for i, (src, dst) in enumerate(zip(small_hbm, small))
    ]
    wq_copy = pltpu.make_async_copy(wq_hbm, v["wq"], copy_sem.at[10])
    wkv_copy = pltpu.make_async_copy(wkv_hbm.reshape(2 * D, WIDTH), v["wkv"], copy_sem.at[11])
    root_copy = pltpu.make_async_copy(root_hbm.reshape(4096, WIDTH), v["root"], copy_sem.at[12])
    mid_copy = pltpu.make_async_copy(mid_hbm.reshape(4096, WIDTH), v["mid"], copy_sem.at[13])
    leaf_copy = pltpu.make_async_copy(leaf_hbm.reshape(8192, WIDTH), v["leaf"], copy_sem.at[14])
    wout_copy = pltpu.make_async_copy(wout_hbm, v["wout"], copy_sem.at[15])
    wgu_copy = pltpu.make_async_copy(wgu_hbm.reshape(2 * D, 1024), v["wgu"], copy_sem.at[16])
    wdn_copy = pltpu.make_async_copy(wdn_hbm, v["wdn"], copy_sem.at[17])
    held_copy = pltpu.make_async_copy(held_hbm.at[0], v["held"].at[tp], copy_sem.at[18])
    for copy in small_copies + [wq_copy, held_copy, wkv_copy, root_copy, mid_copy]:
        copy.start()
    for copy in small_copies:
        copy.wait()
    held_copy.wait()
    pl.semaphore_wait(barrier, NREQ + NTP - 2)
    held_copies = [
        send(v["held"].at[tp], v["held"].at[tp], hsem, d, {"tp": tp_peer(d)}) for d in range(1, NTP)
    ]

    gain = again_v[...].reshape(1, D).astype(F32)
    x = stream_v[...].astype(F32)
    normed = (
        x * lax.rsqrt(jnp.mean(x * x, axis=-1, keepdims=True) + EPSILON) * gain
    ).astype(BF16)
    lp_row = lp_v[...].reshape(1, 512)
    mp_col = as_col(mp_v[...].reshape(1, 16).astype(F32))
    ml_col = as_col(ml_v[...].reshape(1, 16).astype(F32))
    rl_row = rl_v[...].reshape(1, 8).astype(F32)
    parent_len = total(jnp.where(iota((16, 8), 1).astype(F32) == mp_col, rl_row, 0.0), 1)
    belongs = iota((16, 512), 0) == lp_row
    base_row = total(jnp.where(belongs, parent_len + ml_col, 0.0), 0)
    mine = iota((ROWS, 512), 1) == iota((ROWS, 512), 0) + rank * ROWS
    leaf_len_row = ll_v[...].reshape(1, ROWS).astype(F32)
    positions = total(jnp.where(mine, base_row, 0.0), 1) + as_col(leaf_len_row)
    freq = freq_v[...]
    cosines, sines = rope_tables(positions, freq)
    wq_copy.wait()
    queries = rope(dot(normed, v["wq"][...]), cosines, sines).astype(BF16)
    queries = (queries.astype(F32) * (HEAD_DIM**-0.5)).astype(BF16)
    own_rows = pl.ds(pl.multiple_of(rank * ROWS, ROWS), ROWS)
    v["qall"][own_rows, :] = queries
    q_slot = v["qall"].at[own_rows]
    q_copies = [send(q_slot, q_slot, qsem, d, {"req": req_peer(d)}) for d in range(1, NREQ)]
    for copy in (leaf_copy, wout_copy, wgu_copy, wdn_copy):
        copy.start()

    root_row = total(jnp.where(belongs, mp_col, 0.0), 0)
    by_root = (iota((8, 512), 0).astype(F32) == root_row).astype(F32)
    in_mid = lp_row == rank
    groups = jnp.concatenate(
        [by_root, jnp.broadcast_to(in_mid.astype(F32), (8, 512))], axis=0
    ).astype(BF16)
    before = (iota((512, 512), 0) < iota((512, 512), 1)).astype(BF16)
    order = dot(groups, before)
    blocks = jnp.floor((total(by_root, 1) + (BLOCK - 1)) * (1.0 / BLOCK))
    first = total(jnp.where(iota((8, 8), 1) < iota((8, 8), 0), as_row(blocks), 0.0), 1)
    dest = total(by_root * (order[:8] + first * BLOCK), 0)
    ends = (first + blocks) <= iota((8, 128), 1).astype(F32)
    root_of = jnp.minimum(total(ends.astype(F32), 0), 7.0)
    v["table"][...] = jnp.broadcast_to(root_of, (8, 128)).astype(I32)
    table_copy = pltpu.make_async_copy(v["table"], table_s, copy_sem.at[19])
    table_copy.start()
    mid_order = order[8:9]
    v["pick"][...] = (iota((SORTED, 512), 0) == dest.astype(I32)).astype(BF16)
    final = as_col(jnp.where(in_mid, SORTED + mid_order, dest)).astype(I32)
    v["back"][...] = (iota((512, gathered), 1) == final).astype(BF16)
    if gathered > mid_end:
        v["xs"][mid_end:, :] = jnp.zeros((gathered - mid_end, MSG), BF16)
    lane256 = iota((1, 256), 1)
    for r in range(8):
        v["root_bias"][r] = jnp.where(
            (lane256 + rank * 256).astype(F32) < rl_row[:, r : r + 1], 0.0, NEG_FILL
        )
    own_len = total(jnp.where(iota((16, 1), 0) == rank, ml_col, 0.0), 0)
    own_parent = total(jnp.where(iota((16, 1), 0) == rank, parent_len, 0.0), 0)
    rr = rr_v[...]
    rr_col = as_col(rr.astype(F32))
    slot_col = rr_col.astype(I32)
    hit_hi = (iota((16, 256), 0) == rr // 128).astype(BF16)
    hit_lo = (iota((256, 128), 1) == slot_col % 128).astype(BF16)
    token = (iota((16, 128), 0) * 128 + iota((16, 128), 1)).astype(F32)
    alive = (token < own_len) & (dot(hit_hi, hit_lo) < 0.5)
    v["mid_bias"][...] = jnp.where(alive, 0.0, NEG_FILL)
    new_bias = jnp.where(rr.astype(F32) < own_len, 0.0, NEG_FILL)
    held_cos, held_sin = rope_tables(own_parent + rr_col, freq)

    r2, c2 = iota((256, 256), 0), iota((256, 256), 1)
    split = (c2 == jnp.where(r2 < 128, 2 * r2, 2 * r2 - 255)).astype(BF16)
    wkv_copy.wait()
    split_pairs(split, v["wkv"], v["wk"], v["wv"], 16)
    root_copy.wait()
    for k in range(16):
        both = dot(split, v["root"][k * 256 : (k + 1) * 256, :]).astype(BF16)
        half = slice((k % 2) * 128, (k % 2) * 128 + 128)
        v["root_k"][k // 2, half, :] = both[:128]
        v["root_v"][k // 2, half, :] = both[128:]
    mid_copy.wait()
    split_pairs(split, v["mid"], v["mid_k"], v["mid_v"], 16)
    key_new = rope(dot(normed, v["wk"][...]), cosines, sines).astype(BF16)
    value_new = dot(normed, v["wv"][...]).astype(BF16)

    for copy in q_copies:
        copy.wait_recv()
    v["qs"][...] = dot(v["pick"][...], v["qall"][...]).astype(BF16)
    block_mask = (iota((128, WIDTH), 0) // BLOCK == iota((128, WIDTH), 1) // HEAD_DIM).astype(BF16)
    table_copy.wait()

    def root_block(j):
        at = pl.ds(pl.multiple_of(j * BLOCK, BLOCK), BLOCK)
        q = v["qs"][at, :]
        qbd = jnp.concatenate([q] * HEADS, axis=0) * block_mask
        root = jnp.clip(table_s[0, j], 0, 7)
        scores = dot_t(qbd, v["root_k"][root]) + v["root_bias"][root]
        m = jnp.max(scores, axis=1, keepdims=True)
        weights = jnp.exp(scores - m)
        row_sum = total(weights, 1)
        acc = dot(weights.astype(BF16), v["root_v"][root])
        out = head_columns(acc, BLOCK, WIDTH) / head_columns(row_sum, BLOCK, WIDTH)
        lse = head_columns(m + jnp.log(row_sum), BLOCK, STATS)
        v["xs"][at, :] = packed(out, lse)

    def root_blocks(i, carry):
        for u in range(4):
            root_block(i * 4 + u)
        return carry

    lax.fori_loop(0, BLOCKS // 4, root_blocks, 0)

    for copy in held_copies:
        copy.wait_recv()
    square = jnp.zeros((256, 1), F32)
    for c in range(NTP):
        part = v["held"][c].astype(F32)
        square = square + total(part * part, 1)
    scale = lax.rsqrt(square * (1.0 / D) + EPSILON)
    keys = jnp.zeros((256, WIDTH), F32)
    values = jnp.zeros((256, WIDTH), F32)
    for c in range(NTP):
        rows = slice(c * 256, (c + 1) * 256)
        part = (v["held"][c].astype(F32) * scale * gain[:, rows]).astype(BF16)
        keys = keys + dot(part, v["wk"][rows, :])
        values = values + dot(part, v["wv"][rows, :])
    v["new_k"][...] = rope(keys, held_cos, held_sin).astype(BF16)
    v["new_v"][...] = values.astype(BF16)

    mid_mask = (iota((256, WIDTH), 0) // MID_ROWS == iota((256, WIDTH), 1) // HEAD_DIM).astype(BF16)
    e0, e1 = iota((STATS, WIDTH), 0), iota((STATS, WIDTH), 1)
    expand3 = ((e0 < 12) & ((e0 % HEADS) == e1 // HEAD_DIM)).astype(BF16)
    expand2 = ((e0 < 8) & ((e0 % HEADS) == e1 // HEAD_DIM)).astype(BF16)
    lane64 = iota((MID_ROWS, STATS), 1)

    def mid_pass(p):
        chosen = (iota((MID_ROWS, 512), 0) + p * MID_ROWS == mid_order.astype(I32)) & in_mid
        mid_dest = total(jnp.where(chosen, dest, 0.0), 1)
        q_mid = dot(chosen.astype(BF16), v["qall"][...]).astype(BF16)
        take = (iota((MID_ROWS, SORTED), 1) == mid_dest.astype(I32)).astype(BF16)
        rooted = dot(take, v["xs"][:SORTED, :])
        qbd = jnp.concatenate([q_mid] * HEADS, axis=0) * mid_mask
        fresh = dot_t(qbd, v["new_k"][...]) + new_bias
        m = jnp.max(fresh, axis=1, keepdims=True)
        for c in range(8):
            cols = slice(c * 256, (c + 1) * 256)
            bias = jnp.concatenate(
                [v["mid_bias"][2 * c : 2 * c + 1, :], v["mid_bias"][2 * c + 1 : 2 * c + 2, :]], axis=1
            )
            scores = dot_t(qbd, v["mid_k"][cols, :]) + bias
            v["scores"][:, cols] = scores
            m = jnp.maximum(m, jnp.max(scores, axis=1, keepdims=True))
        weights = jnp.exp(fresh - m)
        row_sum = total(weights, 1)
        acc = dot(weights.astype(BF16), v["new_v"][...])
        for c in range(8):
            cols = slice(c * 256, (c + 1) * 256)
            weights = jnp.exp(v["scores"][:, cols] - m)
            row_sum = row_sum + total(weights, 1)
            v["weights"][:, cols] = weights.astype(BF16)
        acc = acc + dot(v["weights"][...], v["mid_v"][...])
        mid_out = head_columns(acc, MID_ROWS, WIDTH) / head_columns(row_sum, MID_ROWS, WIDTH)
        mid_lse = m + jnp.log(row_sum)
        lse_a = dot(rooted[:, WIDTH:].astype(BF16), expand3)
        lse_b = head_columns(mid_lse, MID_ROWS, WIDTH)
        top = jnp.maximum(lse_a, lse_b)
        part_a, part_b = jnp.exp(lse_a - top), jnp.exp(lse_b - top)
        merged = (part_a * rooted[:, :WIDTH] + part_b * mid_out) / (part_a + part_b)
        lse_a = jnp.where(lane64 < 4, unpacked_lse(rooted[:, WIDTH:]), 0.0)
        lse_a = lse_a + pltpu.roll(lse_a, 4, 1) + pltpu.roll(lse_a, 8, 1)
        lse_b = head_columns(mid_lse, MID_ROWS, STATS)
        top = jnp.maximum(lse_a, lse_b)
        joined = top + jnp.log(jnp.exp(lse_a - top) + jnp.exp(lse_b - top))
        at = SORTED if passes == 1 else pl.multiple_of(SORTED + p * MID_ROWS, MID_ROWS)
        v["xs"][pl.ds(at, MID_ROWS), :] = packed(merged, joined)

    if passes == 1:
        mid_pass(0)
    else:

        def mid_step(p, carry):
            mid_pass(p)
            return carry

        lax.fori_loop(0, passes, mid_step, 0)

    v["parts"][...] = dot(v["back"][...], v["xs"][...]).astype(BF16)
    a_copies = []
    for d in range(1, NREQ):
        peer = req_peer(d)
        rows = pl.ds(pl.multiple_of(peer * ROWS, ROWS), ROWS)
        a_copies.append(
            send(v["parts"].at[rows], v["arrived"].at[d], asem, d, {"req": peer})
        )
    v["arrived"][0] = v["parts"][own_rows, :]

    repeat = (iota((256, ROWS), 0) // 8 == iota((256, ROWS), 1)).astype(BF16)
    head_mask = (r2 % 8) == (c2 // HEAD_DIM)
    qrep = jnp.where(head_mask, dot(repeat, queries), 0.0)
    v["leaf_q"][...] = qrep.astype(BF16)
    self_score = total(qrep * dot(repeat, key_new), 1)
    live_len = total(repeat.astype(F32) * leaf_len_row, 1)
    leaf_copy.wait()
    for r in range(ROWS):
        v["leaf_s"][r * 8 : (r + 1) * 8, :] = dot_t(
            v["leaf_q"][r * 8 : (r + 1) * 8, :], v["leaf"][r * 256 : (r + 1) * 256, :]
        )
    live = ((c2 % 2) == 1) & ((c2 // 2).astype(F32) < live_len)
    scores = jnp.where(live, shift_pairs(v["leaf_s"][...]), NEG_FILL)
    best = jnp.maximum(jnp.max(scores, axis=1, keepdims=True), self_score)
    weights = jnp.exp(scores - best)
    self_weight = jnp.exp(self_score - best)
    row_sum = total(weights, 1) + self_weight
    v["leaf_q"][...] = weights.astype(BF16)
    for r in range(ROWS):
        v["leaf_s"][r * 8 : (r + 1) * 8, :] = dot(
            v["leaf_q"][r * 8 : (r + 1) * 8, :], v["leaf"][r * 256 : (r + 1) * 256, :]
        )
    acc = v["leaf_s"][...] + self_weight.astype(BF16).astype(F32) * dot(repeat, value_new)
    acc = jnp.where(head_mask, acc / row_sum, 0.0)
    leaf_out = jnp.sum(acc.reshape(ROWS, 8, WIDTH), axis=1)
    lse = best + jnp.log(row_sum)
    spread = jnp.where((r2 % 8)[:, :STATS] == c2[:, :STATS], lse, 0.0)
    leaf_lse = jnp.sum(spread.reshape(ROWS, 8, STATS), axis=1)

    lane = iota((ROWS, STATS), 1)
    for copy in a_copies:
        copy.wait_recv()
    lses = [unpacked_lse(v["arrived"][s, :, WIDTH:].astype(F32)) for s in range(NREQ)]
    lses.append(leaf_lse)
    best = lses[0]
    for value in lses[1:]:
        best = jnp.maximum(best, value)
    shares = [jnp.exp(value - best) for value in lses]
    row_sum = shares[0]
    for value in shares[1:]:
        row_sum = row_sum + value
    attended = jnp.zeros((ROWS, WIDTH), F32)
    for s in range(NREQ + 1):
        share = shares[s] / row_sum
        high = share.astype(BF16).astype(F32)
        both = jnp.where(
            lane < 4, high, jnp.where(lane < 8, pltpu.roll(share - high, 4, 1), 0.0)
        )
        factor = dot(both.astype(BF16), expand2)
        source = v["arrived"][s, :, :WIDTH].astype(F32) if s < NREQ else leaf_out
        attended = attended + factor * source
    attended = attended.astype(BF16)

    own_cols = pl.ds(pl.multiple_of(tp * WIDTH, WIDTH), WIDTH)

    def scatter(left, weight_v, outgoing, incoming, sems):
        copies = []
        for d in range(1, NTP):
            peer = tp_peer(d)
            cols = pl.ds(pl.multiple_of(peer * WIDTH, WIDTH), WIDTH)
            outgoing[d] = dot(left, weight_v[:, cols]).astype(BF16)
            copies.append(send(outgoing.at[d], incoming.at[d], sems, d, {"tp": peer}))
        return copies, dot(left, weight_v[:, own_cols])

    wout_copy.wait()
    r_copies, own_part = scatter(attended, v["wout"], v["rs_out"], v["rs_in"], rsem)
    residual = own_part + stream_v[:, own_cols].astype(F32)
    i2, j2 = iota((256, 512), 0), iota((256, 512), 1)
    to_even = (j2 == 2 * i2).astype(BF16)
    to_odd = (j2 == 2 * i2 + 1).astype(BF16)
    gain_row = mgain_v[...].reshape(1, D).astype(F32)
    own_gain = jnp.zeros((1, WIDTH), F32)
    for c in range(NTP):
        own_gain = jnp.where(tp == c, gain_row[:, c * WIDTH : (c + 1) * WIDTH], own_gain)
    for d in range(1, NTP):
        r_copies[d - 1].wait_recv()
        residual = residual + v["rs_in"][d].astype(F32)

    a, b, c = three_terms(jnp.broadcast_to(total(residual * residual, 1), (ROWS, STATS)))
    stats = jnp.where(
        lane == 0,
        a.astype(F32),
        jnp.where(lane == 1, b.astype(F32), jnp.where(lane == 2, c.astype(F32), 0.0)),
    )
    v["ag"][0] = jnp.concatenate([residual * own_gain, stats], axis=1).astype(BF16)
    g_copies = [
        send(v["ag"].at[0], v["ag"].at[d], gsem, d, {"tp": tp_peer(d)}) for d in range(1, NTP)
    ]
    wgu_copy.wait()
    squares = jnp.zeros((ROWS, STATS), F32)
    for d in range(NTP):
        if d > 0:
            g_copies[d - 1].wait_recv()
        owner = tp_peer(NTP - d)
        part = v["ag"][d]
        squares = squares + part[:, WIDTH:].astype(F32)
        chunk = part[:, :WIDTH]
        mixed = jnp.concatenate([dot(chunk, to_even), dot(chunk, to_odd)], axis=0).astype(BF16)
        rows = pl.ds(pl.multiple_of(owner * 512, 512), 512)
        for n in range(4):
            cols = slice(n * 256, (n + 1) * 256)
            product = dot(mixed, v["wgu"][rows, cols])
            if d == 0:
                v["proj"][:, cols] = product
            else:
                v["proj"][:, cols] += product
    scale = lax.rsqrt(total(squares, 1) * (1.0 / D) + EPSILON)
    gate = v["proj"][:ROWS, :] * scale
    up = v["proj"][ROWS:, :] * scale
    hidden = (gate / (1.0 + jnp.exp(-gate)) * up).astype(BF16)
    wdn_copy.wait()
    d_copies, own_part = scatter(hidden, v["wdn"], v["ds_out"], v["ds_in"], dsem)
    result = residual + own_part
    for d in range(1, NTP):
        d_copies[d - 1].wait_recv()
        result = result + v["ds_in"][d].astype(F32)
    out_ref[...] = result.astype(BF16)
    for copy in held_copies + q_copies + a_copies + r_copies + g_copies + d_copies:
        copy.wait_send()


def layer_device(
    passes,
    stream,
    attn_gain,
    mlp_gain,
    w_query,
    w_keyval,
    w_out,
    w_gate_up,
    w_down,
    root_cache,
    mid_cache,
    leaf_cache,
    held_hidden,
    recompute_rows,
    root_len,
    mid_len,
    leaf_len,
    mid_parent,
    leaf_parent,
):
    freq = np.exp(np.arange(32, dtype=np.float32) * np.float32(-2.0 * math.log(THETA_BASE) / HEAD_DIM))
    freq = jnp.asarray(np.tile(freq.astype(np.float32), 4)[None, :])
    dma = pltpu.SemaphoreType.DMA
    return pl.pallas_call(
        functools.partial(layer_kernel, passes),
        name="layer" if passes == 1 else "layer_crowded",
        out_shape=jax.ShapeDtypeStruct((ROWS, WIDTH), BF16),
        in_specs=[pl.BlockSpec(memory_space=pltpu.HBM)] * 19,
        out_specs=pl.BlockSpec(memory_space=pltpu.VMEM),
        scratch_shapes=[pltpu.VMEM(*s) for s in SMALL]
        + [pltpu.VMEM(*s) for s in sized(passes).values()]
        + [
            pltpu.SMEM((8, 128), I32),
            dma((20,)),
            dma((2, NTP)),
            dma((2, NREQ)),
            dma((2, NREQ)),
            dma((2, NTP)),
            dma((2, NTP)),
            dma((2, NTP)),
        ],
        compiler_params=pltpu.CompilerParams(
            collective_id=0 if passes == 1 else 1, has_side_effects=True, vmem_limit_bytes=56 * 1024 * 1024
        ),
    )(
        stream,
        attn_gain,
        mlp_gain,
        leaf_parent,
        mid_parent,
        root_len,
        mid_len,
        leaf_len,
        recompute_rows,
        freq,
        w_query,
        w_keyval,
        w_out,
        w_gate_up,
        w_down,
        root_cache,
        mid_cache,
        leaf_cache,
        held_hidden,
    )


def on_device(*args):
    leaf_parent = args[17]
    counts = jnp.sum(
        (leaf_parent[None, :] == jnp.arange(16, dtype=I32)[:, None]).astype(I32), axis=1
    )
    usual = functools.partial(layer_device, 1)
    crowded = functools.partial(layer_device, 512 // MID_ROWS)
    return lax.cond(jnp.max(counts) <= MID_ROWS, usual, crowded, *args)


def solution(mesh):
    placed = (
        P("req", None),
        P(),
        P(),
        P(None, "tp"),
        P(None, None, "tp"),
        P("tp", None),
        P(None, None, "tp"),
        P("tp", None),
        P(None, "req", None, "tp"),
        P("req", None, None, "tp"),
        P("req", None, None, "tp"),
        P("req", None, "tp"),
        P("req", None),
        P(),
        P(),
        P("req"),
        P(),
        P(),
    )
    return jax.shard_map(
        on_device, mesh=mesh, in_specs=placed, out_specs=P("req", "tp"), check_vma=False
    )
```

```python
import functools
import math

import jax
import jax.numpy as jnp
import numpy as np
from jax import lax
from jax.experimental import pallas as pl
from jax.experimental.pallas import tpu as pltpu
from jax.sharding import PartitionSpec as P

F32 = jnp.float32
BF16 = jnp.bfloat16
I32 = jnp.int32
D = 2048
HEAD_DIM = 64
EPSILON = 1e-05
THETA_BASE = 130000.0
NEG_FILL = -1e30
NREQ = 16
NTP = 8
ROWS = 32
WIDTH = 256
HEADS = 4
BLOCK = 32
BLOCKS = 24
GROUP = 8
SORTED = BLOCKS * BLOCK
MID_ROWS = 64
STATS = 128
MSG = WIDTH + STATS


def iota(shape, dim):
    return lax.broadcasted_iota(I32, shape, dim)


def dot(a, b):
    return jnp.dot(a, b, preferred_element_type=F32)


def dot_t(a, b):
    return lax.dot_general(a, b, (((1,), (1,)), ((), ())), preferred_element_type=F32)


def as_col(row):
    n = row.shape[1]
    eye = iota((n, n), 0) == iota((n, n), 1)
    return jnp.sum(jnp.where(eye, row, 0.0), axis=1, keepdims=True)


def as_row(col):
    n = col.shape[0]
    eye = iota((n, n), 0) == iota((n, n), 1)
    return jnp.sum(jnp.where(eye, col, 0.0), axis=0, keepdims=True)


def rope_tables(positions, inv_freq):
    angles = positions * inv_freq
    return jnp.cos(angles), jnp.sin(angles)


def rope(values, cosines, sines):
    n = values.shape[0]
    low = (iota((n, 128), 1) % 64) < 32
    parts = []
    for t in range(2):
        v = values[:, t * 128 : (t + 1) * 128]
        turned = jnp.where(low, -pltpu.roll(v, 96, 1), pltpu.roll(v, 32, 1))
        parts.append(v * cosines + turned * sines)
    return jnp.concatenate(parts, axis=1)


def shift_pairs(scores):
    width = scores.shape[1]
    return jnp.concatenate(
        [pltpu.roll(scores[:, i : i + 128], 1, 1) for i in range(0, width, 128)], axis=1
    )


def three_terms(values):
    first = values.astype(BF16)
    rest = values - first.astype(F32)
    second = rest.astype(BF16)
    third = (rest - second.astype(F32)).astype(BF16)
    return first, second, third


def total(values, axis):
    return jnp.sum(values, axis=axis, keepdims=True)


def head_columns(stacked, rows, width):
    lanes = iota((rows, width), 1)
    group = lanes // HEAD_DIM if width == WIDTH else lanes % HEADS
    picked = jnp.broadcast_to(stacked[:rows], (rows, width))
    for h in range(1, HEADS):
        picked = jnp.where(group == h, stacked[h * rows : (h + 1) * rows], picked)
    return picked


def packed(out, lse):
    lanes = iota(lse.shape, 1)
    a, b, c = three_terms(lse)
    stats = jnp.where(
        lanes < 4,
        a.astype(F32),
        jnp.where(lanes < 8, b.astype(F32), jnp.where(lanes < 12, c.astype(F32), 0.0)),
    )
    return jnp.concatenate([out, stats], axis=1).astype(BF16)


def unpacked_lse(stats):
    return stats + pltpu.roll(stats, 124, 1) + pltpu.roll(stats, 120, 1)


def split_pairs(split, pairs_v, first_v, second_v, tiles):
    for k in range(tiles):
        both = dot(split, pairs_v[k * 256 : (k + 1) * 256, :]).astype(BF16)
        first_v[k * 128 : (k + 1) * 128, :] = both[:128]
        second_v[k * 128 : (k + 1) * 128, :] = both[128:]


SMALL = (
    ((ROWS, D), BF16),
    ((D,), BF16),
    ((D,), BF16),
    ((512,), I32),
    ((16,), I32),
    ((8,), I32),
    ((16,), I32),
    ((ROWS,), I32),
    ((1, 256), I32),
    ((1, 128), F32),
)
WORK = dict(
    wq=((D, WIDTH), BF16),
    wkv=((2 * D, WIDTH), BF16),
    wk=((D, WIDTH), BF16),
    wv=((D, WIDTH), BF16),
    wout=((WIDTH, D), BF16),
    wgu=((2 * D, 1024), BF16),
    wdn=((1024, D), BF16),
    root=((4096, WIDTH), BF16),
    root_k=((8, 256, WIDTH), BF16),
    root_v=((8, 256, WIDTH), BF16),
    root_bias=((8, 1, 256), F32),
    mid=((4096, WIDTH), BF16),
    mid_k=((2048, WIDTH), BF16),
    mid_v=((2048, WIDTH), BF16),
    mid_bias=((16, 128), F32),
    leaf=((8192, WIDTH), BF16),
    held=((NTP, 256, 256), BF16),
    qall=((512, WIDTH), BF16),
    pick=((SORTED, 512), BF16),
    qs=((SORTED, WIDTH), BF16),
    table=((8, 128), I32),
    new_k=((256, WIDTH), BF16),
    new_v=((256, WIDTH), BF16),
    scores=((256, 2048), F32),
    weights=((256, 2048), BF16),
    leaf_q=((256, WIDTH), BF16),
    leaf_s=((256, WIDTH), F32),
    parts=((512, MSG), BF16),
    arrived=((NREQ, ROWS, MSG), BF16),
    rs_out=((NTP, ROWS, WIDTH), BF16),
    rs_in=((NTP, ROWS, WIDTH), BF16),
    ag=((NTP, ROWS, WIDTH), BF16),
    gain=((1, D), F32),
    ds_out=((NTP, ROWS, WIDTH), BF16),
    ds_in=((NTP, ROWS, WIDTH), BF16),
    proj=((2 * ROWS, 1024), F32),
)


def sized(passes):
    gathered = -(-(SORTED + passes * MID_ROWS) // 128) * 128
    return dict(WORK, back=((512, gathered), BF16), xs=((gathered, MSG), BF16))


def layer_kernel(passes, *refs):
    sizes = sized(passes)
    gathered = sizes["xs"][0][0]
    mid_end = SORTED + passes * MID_ROWS
    small_hbm = refs[:10]
    wq_hbm, wkv_hbm, wout_hbm, wgu_hbm, wdn_hbm, root_hbm, mid_hbm, leaf_hbm, held_hbm = refs[10:19]
    out_ref = refs[19]
    small = refs[20:30]
    v = dict(zip(sizes, refs[30 : 30 + len(sizes)]))
    table_s, copy_sem, hsem, qsem, asem, rsem, gsem, dsem = refs[30 + len(sizes) :]
    stream_v, again_v, mgain_v, lp_v, mp_v, rl_v, ml_v, ll_v, rr_v, freq_v = small
    rank = lax.axis_index("req")
    tp = lax.axis_index("tp")

    def req_peer(d):
        return lax.rem(rank + d, NREQ)

    def tp_peer(d):
        return lax.rem(tp + d, NTP)

    def send(src, dst, sems, d, target):
        copy = pltpu.make_async_remote_copy(
            src_ref=src,
            dst_ref=dst,
            send_sem=sems.at[0, d],
            recv_sem=sems.at[1, d],
            device_id=target,
        )
        copy.start()
        return copy

    barrier = pltpu.get_barrier_semaphore()
    for d in range(1, NREQ):
        pl.semaphore_signal(barrier, inc=1, device_id={"req": req_peer(d)})
    for d in range(1, NTP):
        pl.semaphore_signal(barrier, inc=1, device_id={"tp": tp_peer(d)})

    small_copies = [
        pltpu.make_async_copy(src, dst, copy_sem.at[i])
        for i, (src, dst) in enumerate(zip(small_hbm, small))
    ]
    wq_copy = pltpu.make_async_copy(wq_hbm, v["wq"], copy_sem.at[10])
    wkv_copy = pltpu.make_async_copy(wkv_hbm.reshape(2 * D, WIDTH), v["wkv"], copy_sem.at[11])
    root_copy = pltpu.make_async_copy(root_hbm.reshape(4096, WIDTH), v["root"], copy_sem.at[12])
    mid_copy = pltpu.make_async_copy(mid_hbm.reshape(4096, WIDTH), v["mid"], copy_sem.at[13])
    leaf_copy = pltpu.make_async_copy(leaf_hbm.reshape(8192, WIDTH), v["leaf"], copy_sem.at[14])
    wout_copy = pltpu.make_async_copy(wout_hbm, v["wout"], copy_sem.at[15])
    wgu_copy = pltpu.make_async_copy(wgu_hbm.reshape(2 * D, 1024), v["wgu"], copy_sem.at[16])
    wdn_copy = pltpu.make_async_copy(wdn_hbm, v["wdn"], copy_sem.at[17])
    held_copy = pltpu.make_async_copy(held_hbm.at[0], v["held"].at[tp], copy_sem.at[18])
    for copy in small_copies + [wq_copy, held_copy, wkv_copy, root_copy, mid_copy]:
        copy.start()
    for copy in small_copies:
        copy.wait()

    gain = again_v[...].reshape(1, D).astype(F32)
    x = stream_v[...].astype(F32)
    normed = (
        x * lax.rsqrt(jnp.mean(x * x, axis=-1, keepdims=True) + EPSILON) * gain
    ).astype(BF16)
    lp_row = lp_v[...].reshape(1, 512)
    mp_col = as_col(mp_v[...].reshape(1, 16).astype(F32))
    ml_col = as_col(ml_v[...].reshape(1, 16).astype(F32))
    rl_row = rl_v[...].reshape(1, 8).astype(F32)
    parent_len = total(jnp.where(iota((16, 8), 1).astype(F32) == mp_col, rl_row, 0.0), 1)
    belongs = iota((16, 512), 0) == lp_row
    base_row = total(jnp.where(belongs, parent_len + ml_col, 0.0), 0)
    mine = iota((ROWS, 512), 1) == iota((ROWS, 512), 0) + rank * ROWS
    leaf_len_row = ll_v[...].reshape(1, ROWS).astype(F32)
    positions = total(jnp.where(mine, base_row, 0.0), 1) + as_col(leaf_len_row)
    freq = freq_v[...]
    cosines, sines = rope_tables(positions, freq)
    wq_copy.wait()
    queries = rope(dot(normed, v["wq"][...]), cosines, sines).astype(BF16)
    queries = (queries.astype(F32) * (HEAD_DIM**-0.5)).astype(BF16)
    held_copy.wait()
    pl.semaphore_wait(barrier, NREQ + NTP - 2)

    after, ahead, across, sibling = tp_peer(2), tp_peer(6), tp_peer(4), tp + 1 - 2 * lax.rem(tp, 2)
    held = v["held"]
    low, high = slice(0, 128), slice(128, 256)
    held_copies = [
        send(held.at[tp], held.at[tp], hsem, 0, {"tp": after}),
        send(held.at[tp], held.at[tp], hsem, 1, {"tp": ahead}),
        send(held.at[tp], held.at[tp], hsem, 4, {"tp": sibling}),
    ]
    own_rows = pl.ds(pl.multiple_of(rank * ROWS, ROWS), ROWS)
    v["qall"][own_rows, :] = queries
    q_slot = v["qall"].at[own_rows]
    q_copies = [send(q_slot, q_slot, qsem, d, {"req": req_peer(d)}) for d in range(1, NREQ)]
    for copy in (leaf_copy, wout_copy, wgu_copy, wdn_copy):
        copy.start()

    root_row = total(jnp.where(belongs, mp_col, 0.0), 0)
    by_root = (iota((8, 512), 0).astype(F32) == root_row).astype(F32)
    in_mid = lp_row == rank
    groups = jnp.concatenate(
        [by_root, jnp.broadcast_to(in_mid.astype(F32), (8, 512))], axis=0
    ).astype(BF16)
    before = (iota((512, 512), 0) < iota((512, 512), 1)).astype(BF16)
    order = dot(groups, before)
    blocks = jnp.floor((total(by_root, 1) + (BLOCK - 1)) * (1.0 / BLOCK))
    first = total(jnp.where(iota((8, 8), 1) < iota((8, 8), 0), as_row(blocks), 0.0), 1)
    dest = total(by_root * (order[:8] + first * BLOCK), 0)
    ends = (first + blocks) <= iota((8, 128), 1).astype(F32)
    root_of = jnp.minimum(total(ends.astype(F32), 0), 7.0)
    v["table"][...] = jnp.broadcast_to(root_of, (8, 128)).astype(I32)
    table_copy = pltpu.make_async_copy(v["table"], table_s, copy_sem.at[19])
    table_copy.start()
    mid_order = order[8:9]
    v["pick"][...] = (iota((SORTED, 512), 0) == dest.astype(I32)).astype(BF16)
    final = as_col(jnp.where(in_mid, SORTED + mid_order, dest)).astype(I32)
    v["back"][...] = (iota((512, gathered), 1) == final).astype(BF16)
    if gathered > mid_end:
        v["xs"][mid_end:, :] = jnp.zeros((gathered - mid_end, MSG), BF16)
    lane256 = iota((1, 256), 1)
    for r in range(8):
        v["root_bias"][r] = jnp.where(
            (lane256 + rank * 256).astype(F32) < rl_row[:, r : r + 1], 0.0, NEG_FILL
        )
    own_len = total(jnp.where(iota((16, 1), 0) == rank, ml_col, 0.0), 0)
    own_parent = total(jnp.where(iota((16, 1), 0) == rank, parent_len, 0.0), 0)
    rr = rr_v[...]
    rr_col = as_col(rr.astype(F32))
    slot_col = rr_col.astype(I32)
    hit_hi = (iota((16, 256), 0) == rr // 128).astype(BF16)
    hit_lo = (iota((256, 128), 1) == slot_col % 128).astype(BF16)
    token = (iota((16, 128), 0) * 128 + iota((16, 128), 1)).astype(F32)
    alive = (token < own_len) & (dot(hit_hi, hit_lo) < 0.5)
    v["mid_bias"][...] = jnp.where(alive, 0.0, NEG_FILL)
    new_bias = jnp.where(rr.astype(F32) < own_len, 0.0, NEG_FILL)
    held_cos, held_sin = rope_tables(own_parent + rr_col, freq)

    r2, c2 = iota((256, 256), 0), iota((256, 256), 1)
    split = (c2 == jnp.where(r2 < 128, 2 * r2, 2 * r2 - 255)).astype(BF16)
    wkv_copy.wait()
    split_pairs(split, v["wkv"], v["wk"], v["wv"], 16)
    root_copy.wait()
    for k in range(16):
        both = dot(split, v["root"][k * 256 : (k + 1) * 256, :]).astype(BF16)
        half = slice((k % 2) * 128, (k % 2) * 128 + 128)
        v["root_k"][k // 2, half, :] = both[:128]
        v["root_v"][k // 2, half, :] = both[128:]
    held_copies[0].wait_recv()
    held_copies[1].wait_recv()
    held_copies += [
        send(held.at[ahead, low], held.at[ahead, low], hsem, 2, {"tp": after}),
        send(held.at[after, high], held.at[after, high], hsem, 3, {"tp": ahead}),
        send(held.at[ahead], held.at[ahead], hsem, 5, {"tp": sibling}),
        send(held.at[after], held.at[after], hsem, 6, {"tp": sibling}),
    ]

    mid_copy.wait()
    split_pairs(split, v["mid"], v["mid_k"], v["mid_v"], 16)
    key_new = rope(dot(normed, v["wk"][...]), cosines, sines).astype(BF16)
    value_new = dot(normed, v["wv"][...]).astype(BF16)

    for copy in q_copies:
        copy.wait_recv()
    v["qs"][...] = dot(v["pick"][...], v["qall"][...]).astype(BF16)
    held_copies[3].wait_recv()
    held_copies[4].wait_recv()
    held_copies += [
        send(held.at[across, low], held.at[across, low], hsem, 7, {"tp": sibling}),
        send(held.at[across, high], held.at[across, high], hsem, 8, {"tp": sibling}),
    ]
    block_mask = (iota((128, WIDTH), 0) // BLOCK == iota((128, WIDTH), 1) // HEAD_DIM).astype(BF16)
    table_copy.wait()

    def root_blocks(i, carry):
        ats = [
            pl.ds(pl.multiple_of((i * GROUP + u) * BLOCK, BLOCK), BLOCK) for u in range(GROUP)
        ]
        roots = [jnp.clip(table_s[0, i * GROUP + u], 0, 7) for u in range(GROUP)]
        qbds = [jnp.concatenate([v["qs"][at, :]] * HEADS, axis=0) * block_mask for at in ats]
        scores = [
            dot_t(qbd, v["root_k"][root]) + v["root_bias"][root] for qbd, root in zip(qbds, roots)
        ]
        tops = [jnp.max(score, axis=1, keepdims=True) for score in scores]
        weights = [jnp.exp(score - m) for score, m in zip(scores, tops)]
        sums = [total(weight, 1) for weight in weights]
        accs = [
            dot(weight.astype(BF16), v["root_v"][root]) for weight, root in zip(weights, roots)
        ]
        outs = []
        for m, row_sum, acc in zip(tops, sums, accs):
            out = head_columns(acc, BLOCK, WIDTH) / head_columns(row_sum, BLOCK, WIDTH)
            outs.append(packed(out, head_columns(m + jnp.log(row_sum), BLOCK, STATS)))
        for at, out in zip(ats, outs):
            v["xs"][at, :] = out
        return carry

    lax.fori_loop(0, BLOCKS // GROUP, root_blocks, 0)

    for copy in [held_copies[2]] + held_copies[5:]:
        copy.wait_recv()
    square = jnp.zeros((256, 1), F32)
    for c in range(NTP):
        part = v["held"][c].astype(F32)
        square = square + total(part * part, 1)
    scale = lax.rsqrt(square * (1.0 / D) + EPSILON)
    keys = jnp.zeros((256, WIDTH), F32)
    values = jnp.zeros((256, WIDTH), F32)
    for c in range(NTP):
        rows = slice(c * 256, (c + 1) * 256)
        part = (v["held"][c].astype(F32) * scale * gain[:, rows]).astype(BF16)
        keys = keys + dot(part, v["wk"][rows, :])
        values = values + dot(part, v["wv"][rows, :])
    v["new_k"][...] = rope(keys, held_cos, held_sin).astype(BF16)
    v["new_v"][...] = values.astype(BF16)

    mid_mask = (iota((256, WIDTH), 0) // MID_ROWS == iota((256, WIDTH), 1) // HEAD_DIM).astype(BF16)
    e0, e1 = iota((STATS, WIDTH), 0), iota((STATS, WIDTH), 1)
    expand3 = ((e0 < 12) & ((e0 % HEADS) == e1 // HEAD_DIM)).astype(BF16)
    expand2 = ((e0 < 8) & ((e0 % HEADS) == e1 // HEAD_DIM)).astype(BF16)
    lane64 = iota((MID_ROWS, STATS), 1)

    def mid_pass(p):
        chosen = (iota((MID_ROWS, 512), 0) + p * MID_ROWS == mid_order.astype(I32)) & in_mid
        mid_dest = total(jnp.where(chosen, dest, 0.0), 1)
        q_mid = dot(chosen.astype(BF16), v["qall"][...]).astype(BF16)
        take = (iota((MID_ROWS, SORTED), 1) == mid_dest.astype(I32)).astype(BF16)
        rooted = dot(take, v["xs"][:SORTED, :])
        qbd = jnp.concatenate([q_mid] * HEADS, axis=0) * mid_mask
        fresh = dot_t(qbd, v["new_k"][...]) + new_bias
        m = jnp.max(fresh, axis=1, keepdims=True)
        for c in range(8):
            cols = slice(c * 256, (c + 1) * 256)
            bias = jnp.concatenate(
                [v["mid_bias"][2 * c : 2 * c + 1, :], v["mid_bias"][2 * c + 1 : 2 * c + 2, :]], axis=1
            )
            scores = dot_t(qbd, v["mid_k"][cols, :]) + bias
            v["scores"][:, cols] = scores
            m = jnp.maximum(m, jnp.max(scores, axis=1, keepdims=True))
        weights = jnp.exp(fresh - m)
        row_sum = total(weights, 1)
        acc = dot(weights.astype(BF16), v["new_v"][...])
        for c in range(8):
            cols = slice(c * 256, (c + 1) * 256)
            weights = jnp.exp(v["scores"][:, cols] - m)
            row_sum = row_sum + total(weights, 1)
            v["weights"][:, cols] = weights.astype(BF16)
        acc = acc + dot(v["weights"][...], v["mid_v"][...])
        mid_out = head_columns(acc, MID_ROWS, WIDTH) / head_columns(row_sum, MID_ROWS, WIDTH)
        mid_lse = m + jnp.log(row_sum)
        lse_a = dot(rooted[:, WIDTH:].astype(BF16), expand3)
        lse_b = head_columns(mid_lse, MID_ROWS, WIDTH)
        top = jnp.maximum(lse_a, lse_b)
        part_a, part_b = jnp.exp(lse_a - top), jnp.exp(lse_b - top)
        merged = (part_a * rooted[:, :WIDTH] + part_b * mid_out) / (part_a + part_b)
        lse_a = jnp.where(lane64 < 4, unpacked_lse(rooted[:, WIDTH:]), 0.0)
        lse_a = lse_a + pltpu.roll(lse_a, 4, 1) + pltpu.roll(lse_a, 8, 1)
        lse_b = head_columns(mid_lse, MID_ROWS, STATS)
        top = jnp.maximum(lse_a, lse_b)
        joined = top + jnp.log(jnp.exp(lse_a - top) + jnp.exp(lse_b - top))
        at = SORTED if passes == 1 else pl.multiple_of(SORTED + p * MID_ROWS, MID_ROWS)
        v["xs"][pl.ds(at, MID_ROWS), :] = packed(merged, joined)

    if passes == 1:
        mid_pass(0)
    else:

        def mid_step(p, carry):
            mid_pass(p)
            return carry

        lax.fori_loop(0, passes, mid_step, 0)

    v["parts"][...] = dot(v["back"][...], v["xs"][...]).astype(BF16)
    a_copies = []
    for d in range(1, NREQ):
        peer = req_peer(d)
        rows = pl.ds(pl.multiple_of(peer * ROWS, ROWS), ROWS)
        a_copies.append(
            send(v["parts"].at[rows], v["arrived"].at[d], asem, d, {"req": peer})
        )
    v["arrived"][0] = v["parts"][own_rows, :]

    repeat = (iota((256, ROWS), 0) // 8 == iota((256, ROWS), 1)).astype(BF16)
    head_mask = (r2 % 8) == (c2 // HEAD_DIM)
    qrep = jnp.where(head_mask, dot(repeat, queries), 0.0)
    v["leaf_q"][...] = qrep.astype(BF16)
    self_score = total(qrep * dot(repeat, key_new), 1)
    live_len = total(repeat.astype(F32) * leaf_len_row, 1)
    leaf_copy.wait()
    for r in range(ROWS):
        v["leaf_s"][r * 8 : (r + 1) * 8, :] = dot_t(
            v["leaf_q"][r * 8 : (r + 1) * 8, :], v["leaf"][r * 256 : (r + 1) * 256, :]
        )
    live = ((c2 % 2) == 1) & ((c2 // 2).astype(F32) < live_len)
    scores = jnp.where(live, shift_pairs(v["leaf_s"][...]), NEG_FILL)
    best = jnp.maximum(jnp.max(scores, axis=1, keepdims=True), self_score)
    weights = jnp.exp(scores - best)
    self_weight = jnp.exp(self_score - best)
    row_sum = total(weights, 1) + self_weight
    v["leaf_q"][...] = weights.astype(BF16)
    for r in range(ROWS):
        v["leaf_s"][r * 8 : (r + 1) * 8, :] = dot(
            v["leaf_q"][r * 8 : (r + 1) * 8, :], v["leaf"][r * 256 : (r + 1) * 256, :]
        )
    acc = v["leaf_s"][...] + self_weight.astype(BF16).astype(F32) * dot(repeat, value_new)
    acc = jnp.where(head_mask, acc / row_sum, 0.0)
    leaf_out = jnp.sum(acc.reshape(ROWS, 8, WIDTH), axis=1)
    lse = best + jnp.log(row_sum)
    spread = jnp.where((r2 % 8)[:, :STATS] == c2[:, :STATS], lse, 0.0)
    leaf_lse = jnp.sum(spread.reshape(ROWS, 8, STATS), axis=1)

    lane = iota((ROWS, STATS), 1)
    for copy in a_copies:
        copy.wait_recv()
    lses = [unpacked_lse(v["arrived"][s, :, WIDTH:].astype(F32)) for s in range(NREQ)]
    lses.append(leaf_lse)
    best = lses[0]
    for value in lses[1:]:
        best = jnp.maximum(best, value)
    shares = [jnp.exp(value - best) for value in lses]
    row_sum = shares[0]
    for value in shares[1:]:
        row_sum = row_sum + value
    attended = jnp.zeros((ROWS, WIDTH), F32)
    for s in range(NREQ + 1):
        share = shares[s] / row_sum
        high = share.astype(BF16).astype(F32)
        both = jnp.where(
            lane < 4, high, jnp.where(lane < 8, pltpu.roll(share - high, 4, 1), 0.0)
        )
        factor = dot(both.astype(BF16), expand2)
        source = v["arrived"][s, :, :WIDTH].astype(F32) if s < NREQ else leaf_out
        attended = attended + factor * source
    attended = attended.astype(BF16)

    own_cols = pl.ds(pl.multiple_of(tp * WIDTH, WIDTH), WIDTH)

    def scatter(left, weight_v, outgoing, incoming, sems):
        copies = []
        for d in range(1, NTP):
            peer = tp_peer(d)
            cols = pl.ds(pl.multiple_of(peer * WIDTH, WIDTH), WIDTH)
            outgoing[d] = dot(left, weight_v[:, cols]).astype(BF16)
            copies.append(send(outgoing.at[d], incoming.at[d], sems, d, {"tp": peer}))
        return copies, dot(left, weight_v[:, own_cols])

    wout_copy.wait()
    r_copies, own_part = scatter(attended, v["wout"], v["rs_out"], v["rs_in"], rsem)
    residual = own_part + stream_v[:, own_cols].astype(F32)
    i2, j2 = iota((256, 512), 0), iota((256, 512), 1)
    to_even = (j2 == 2 * i2).astype(BF16)
    to_odd = (j2 == 2 * i2 + 1).astype(BF16)
    gain_row = mgain_v[...].reshape(1, D).astype(F32)
    v["gain"][...] = gain_row
    for d in range(1, NTP):
        r_copies[d - 1].wait_recv()
        residual = residual + v["rs_in"][d].astype(F32)

    v["ag"][0] = residual.astype(BF16)
    g_copies = [
        send(v["ag"].at[0], v["ag"].at[d], gsem, d, {"tp": tp_peer(d)}) for d in range(1, NTP)
    ]
    wgu_copy.wait()
    squares = jnp.zeros((ROWS, WIDTH), F32)
    for d in range(NTP):
        if d > 0:
            g_copies[d - 1].wait_recv()
        owner = tp_peer(NTP - d)
        part = v["ag"][d].astype(F32)
        squares = squares + part * part
        gain_cols = pl.ds(pl.multiple_of(owner * WIDTH, WIDTH), WIDTH)
        chunk = (part * v["gain"][:, gain_cols]).astype(BF16)
        mixed = jnp.concatenate([dot(chunk, to_even), dot(chunk, to_odd)], axis=0).astype(BF16)
        rows = pl.ds(pl.multiple_of(owner * 512, 512), 512)
        for n in range(4):
            cols = slice(n * 256, (n + 1) * 256)
            product = dot(mixed, v["wgu"][rows, cols])
            if d == 0:
                v["proj"][:, cols] = product
            else:
                v["proj"][:, cols] += product
    scale = lax.rsqrt(total(squares, 1) * (1.0 / D) + EPSILON)
    gate = v["proj"][:ROWS, :] * scale
    up = v["proj"][ROWS:, :] * scale
    hidden = (gate / (1.0 + jnp.exp(-gate)) * up).astype(BF16)
    wdn_copy.wait()
    d_copies, own_part = scatter(hidden, v["wdn"], v["ds_out"], v["ds_in"], dsem)
    result = residual + own_part
    for d in range(1, NTP):
        d_copies[d - 1].wait_recv()
        result = result + v["ds_in"][d].astype(F32)
    out_ref[...] = result.astype(BF16)
    for copy in held_copies + q_copies + a_copies + r_copies + g_copies + d_copies:
        copy.wait_send()


def layer_device(
    passes,
    stream,
    attn_gain,
    mlp_gain,
    w_query,
    w_keyval,
    w_out,
    w_gate_up,
    w_down,
    root_cache,
    mid_cache,
    leaf_cache,
    held_hidden,
    recompute_rows,
    root_len,
    mid_len,
    leaf_len,
    mid_parent,
    leaf_parent,
):
    freq = np.exp(np.arange(32, dtype=np.float32) * np.float32(-2.0 * math.log(THETA_BASE) / HEAD_DIM))
    freq = jnp.asarray(np.tile(freq.astype(np.float32), 4)[None, :])
    dma = pltpu.SemaphoreType.DMA
    return pl.pallas_call(
        functools.partial(layer_kernel, passes),
        name="layer" if passes == 1 else "layer_crowded",
        out_shape=jax.ShapeDtypeStruct((ROWS, WIDTH), BF16),
        in_specs=[pl.BlockSpec(memory_space=pltpu.HBM)] * 19,
        out_specs=pl.BlockSpec(memory_space=pltpu.VMEM),
        scratch_shapes=[pltpu.VMEM(*s) for s in SMALL]
        + [pltpu.VMEM(*s) for s in sized(passes).values()]
        + [
            pltpu.SMEM((8, 128), I32),
            dma((20,)),
            dma((2, 9)),
            dma((2, NREQ)),
            dma((2, NREQ)),
            dma((2, NTP)),
            dma((2, NTP)),
            dma((2, NTP)),
        ],
        compiler_params=pltpu.CompilerParams(
            collective_id=0 if passes == 1 else 1, has_side_effects=True, vmem_limit_bytes=56 * 1024 * 1024
        ),
    )(
        stream,
        attn_gain,
        mlp_gain,
        leaf_parent,
        mid_parent,
        root_len,
        mid_len,
        leaf_len,
        recompute_rows,
        freq,
        w_query,
        w_keyval,
        w_out,
        w_gate_up,
        w_down,
        root_cache,
        mid_cache,
        leaf_cache,
        held_hidden,
    )


def on_device(*args):
    leaf_parent = args[17]
    counts = jnp.sum(
        (leaf_parent[None, :] == jnp.arange(16, dtype=I32)[:, None]).astype(I32), axis=1
    )
    usual = functools.partial(layer_device, 1)
    crowded = functools.partial(layer_device, 512 // MID_ROWS)
    return lax.cond(jnp.max(counts) <= MID_ROWS, usual, crowded, *args)


def solution(mesh):
    placed = (
        P("req", None),
        P(),
        P(),
        P(None, "tp"),
        P(None, None, "tp"),
        P("tp", None),
        P(None, None, "tp"),
        P("tp", None),
        P(None, "req", None, "tp"),
        P("req", None, None, "tp"),
        P("req", None, None, "tp"),
        P("req", None, "tp"),
        P("req", None),
        P(),
        P(),
        P("req"),
        P(),
        P(),
    )
    return jax.shard_map(
        on_device, mesh=mesh, in_specs=placed, out_specs=P("req", "tp"), check_vma=False
    )
```

```python
import functools
import math

import jax
import jax.numpy as jnp
import numpy as np
from jax import lax
from jax.experimental import pallas as pl
from jax.experimental.pallas import tpu as pltpu
from jax.sharding import PartitionSpec as P

F32 = jnp.float32
BF16 = jnp.bfloat16
I32 = jnp.int32
D = 2048
HEAD_DIM = 64
EPSILON = 1e-05
THETA_BASE = 130000.0
NEG_FILL = -1e30
NREQ = 16
NTP = 8
ROWS = 32
WIDTH = 256
HEADS = 4
BLOCK = 32
BLOCKS = 24
GROUP = 8
SORTED = BLOCKS * BLOCK
MID_ROWS = 64
STATS = 128
MSG = WIDTH + STATS


def iota(shape, dim):
    return lax.broadcasted_iota(I32, shape, dim)


def dot(a, b):
    return jnp.dot(a, b, preferred_element_type=F32)


def dot_t(a, b):
    return lax.dot_general(a, b, (((1,), (1,)), ((), ())), preferred_element_type=F32)


def as_col(row):
    n = row.shape[1]
    eye = iota((n, n), 0) == iota((n, n), 1)
    return jnp.sum(jnp.where(eye, row, 0.0), axis=1, keepdims=True)


def as_row(col):
    n = col.shape[0]
    eye = iota((n, n), 0) == iota((n, n), 1)
    return jnp.sum(jnp.where(eye, col, 0.0), axis=0, keepdims=True)


def rope_tables(positions, inv_freq):
    angles = positions * inv_freq
    return jnp.cos(angles), jnp.sin(angles)


def rope(values, cosines, sines):
    n = values.shape[0]
    low = (iota((n, 128), 1) % 64) < 32
    parts = []
    for t in range(2):
        v = values[:, t * 128 : (t + 1) * 128]
        turned = jnp.where(low, -pltpu.roll(v, 96, 1), pltpu.roll(v, 32, 1))
        parts.append(v * cosines + turned * sines)
    return jnp.concatenate(parts, axis=1)


def shift_pairs(scores):
    width = scores.shape[1]
    return jnp.concatenate(
        [pltpu.roll(scores[:, i : i + 128], 1, 1) for i in range(0, width, 128)], axis=1
    )


def three_terms(values):
    first = values.astype(BF16)
    rest = values - first.astype(F32)
    second = rest.astype(BF16)
    third = (rest - second.astype(F32)).astype(BF16)
    return first, second, third


def total(values, axis):
    return jnp.sum(values, axis=axis, keepdims=True)


def head_columns(stacked, rows, width):
    lanes = iota((rows, width), 1)
    group = lanes // HEAD_DIM if width == WIDTH else lanes % HEADS
    picked = jnp.broadcast_to(stacked[:rows], (rows, width))
    for h in range(1, HEADS):
        picked = jnp.where(group == h, stacked[h * rows : (h + 1) * rows], picked)
    return picked


def packed(out, lse):
    lanes = iota(lse.shape, 1)
    a, b, c = three_terms(lse)
    stats = jnp.where(
        lanes < 4,
        a.astype(F32),
        jnp.where(lanes < 8, b.astype(F32), jnp.where(lanes < 12, c.astype(F32), 0.0)),
    )
    return jnp.concatenate([out, stats], axis=1).astype(BF16)


def unpacked_lse(stats):
    return stats + pltpu.roll(stats, 124, 1) + pltpu.roll(stats, 120, 1)


def split_pairs(split, pairs_v, first_v, second_v, tiles):
    for k in range(tiles):
        both = dot(split, pairs_v[k * 256 : (k + 1) * 256, :]).astype(BF16)
        first_v[k * 128 : (k + 1) * 128, :] = both[:128]
        second_v[k * 128 : (k + 1) * 128, :] = both[128:]


SMALL = (
    ((ROWS, D), BF16),
    ((D,), BF16),
    ((D,), BF16),
    ((512,), I32),
    ((16,), I32),
    ((8,), I32),
    ((16,), I32),
    ((ROWS,), I32),
    ((1, 256), I32),
    ((1, 128), F32),
)
WORK = dict(
    wq=((D, WIDTH), BF16),
    wkv=((2 * D, WIDTH), BF16),
    wk=((D, WIDTH), BF16),
    wv=((D, WIDTH), BF16),
    wout=((WIDTH, D), BF16),
    wgu=((2 * D, 1024), BF16),
    wdn=((1024, D), BF16),
    root=((4096, WIDTH), BF16),
    root_k=((8, 256, WIDTH), BF16),
    root_v=((8, 256, WIDTH), BF16),
    root_bias=((8, 1, 256), F32),
    mid=((4096, WIDTH), BF16),
    mid_k=((2048, WIDTH), BF16),
    mid_v=((2048, WIDTH), BF16),
    mid_bias=((16, 128), F32),
    leaf=((8192, WIDTH), BF16),
    held=((NTP, 256, 256), BF16),
    qall=((512, WIDTH), BF16),
    pick=((SORTED, 512), BF16),
    qs=((SORTED, WIDTH), BF16),
    table=((8, 128), I32),
    new_k=((256, WIDTH), BF16),
    new_v=((256, WIDTH), BF16),
    scores=((256, 2048), F32),
    weights=((256, 2048), BF16),
    leaf_q=((256, WIDTH), BF16),
    leaf_s=((256, WIDTH), F32),
    parts=((NREQ, ROWS + 8, WIDTH), BF16),
    arrived=((NREQ, ROWS + 8, WIDTH), BF16),
    rs_out=((NTP, ROWS, WIDTH), BF16),
    rs_in=((NTP, ROWS, WIDTH), BF16),
    ag=((NTP, ROWS, WIDTH), BF16),
    gain=((1, D), F32),
    ds_out=((NTP, ROWS, WIDTH), BF16),
    ds_in=((NTP, ROWS, WIDTH), BF16),
    proj=((2 * ROWS, 1024), F32),
)


def sized(passes):
    gathered = -(-(SORTED + passes * MID_ROWS) // 128) * 128
    return dict(WORK, back=((512, gathered), BF16), xs=((gathered, MSG), BF16))


def layer_kernel(passes, *refs):
    sizes = sized(passes)
    gathered = sizes["xs"][0][0]
    mid_end = SORTED + passes * MID_ROWS
    small_hbm = refs[:10]
    wq_hbm, wkv_hbm, wout_hbm, wgu_hbm, wdn_hbm, root_hbm, mid_hbm, leaf_hbm, held_hbm = refs[10:19]
    out_ref = refs[19]
    small = refs[20:30]
    v = dict(zip(sizes, refs[30 : 30 + len(sizes)]))
    table_s, copy_sem, hsem, qsem, asem, rsem, gsem, dsem = refs[30 + len(sizes) :]
    stream_v, again_v, mgain_v, lp_v, mp_v, rl_v, ml_v, ll_v, rr_v, freq_v = small
    rank = lax.axis_index("req")
    tp = lax.axis_index("tp")

    def req_peer(d):
        return lax.rem(rank + d, NREQ)

    def tp_peer(d):
        return lax.rem(tp + d, NTP)

    def send(src, dst, sems, d, target):
        copy = pltpu.make_async_remote_copy(
            src_ref=src,
            dst_ref=dst,
            send_sem=sems.at[0, d],
            recv_sem=sems.at[1, d],
            device_id=target,
        )
        copy.start()
        return copy

    barrier = pltpu.get_barrier_semaphore()
    for d in range(1, NREQ):
        pl.semaphore_signal(barrier, inc=1, device_id={"req": req_peer(d)})
    for d in range(1, NTP):
        pl.semaphore_signal(barrier, inc=1, device_id={"tp": tp_peer(d)})

    small_copies = [
        pltpu.make_async_copy(src, dst, copy_sem.at[i])
        for i, (src, dst) in enumerate(zip(small_hbm, small))
    ]
    wq_copy = pltpu.make_async_copy(wq_hbm, v["wq"], copy_sem.at[10])
    wkv_copy = pltpu.make_async_copy(wkv_hbm.reshape(2 * D, WIDTH), v["wkv"], copy_sem.at[11])
    root_copy = pltpu.make_async_copy(root_hbm.reshape(4096, WIDTH), v["root"], copy_sem.at[12])
    mid_copy = pltpu.make_async_copy(mid_hbm.reshape(4096, WIDTH), v["mid"], copy_sem.at[13])
    leaf_copy = pltpu.make_async_copy(leaf_hbm.reshape(8192, WIDTH), v["leaf"], copy_sem.at[14])
    wout_copy = pltpu.make_async_copy(wout_hbm, v["wout"], copy_sem.at[15])
    wgu_copy = pltpu.make_async_copy(wgu_hbm.reshape(2 * D, 1024), v["wgu"], copy_sem.at[16])
    wdn_copy = pltpu.make_async_copy(wdn_hbm, v["wdn"], copy_sem.at[17])
    held_copy = pltpu.make_async_copy(held_hbm.at[0], v["held"].at[tp], copy_sem.at[18])
    for copy in small_copies + [wq_copy, held_copy, wkv_copy, root_copy, mid_copy]:
        copy.start()
    for copy in small_copies:
        copy.wait()

    gain = again_v[...].reshape(1, D).astype(F32)
    x = stream_v[...].astype(F32)
    normed = (
        x * lax.rsqrt(jnp.mean(x * x, axis=-1, keepdims=True) + EPSILON) * gain
    ).astype(BF16)
    lp_row = lp_v[...].reshape(1, 512)
    mp_col = as_col(mp_v[...].reshape(1, 16).astype(F32))
    ml_col = as_col(ml_v[...].reshape(1, 16).astype(F32))
    rl_row = rl_v[...].reshape(1, 8).astype(F32)
    parent_len = total(jnp.where(iota((16, 8), 1).astype(F32) == mp_col, rl_row, 0.0), 1)
    belongs = iota((16, 512), 0) == lp_row
    base_row = total(jnp.where(belongs, parent_len + ml_col, 0.0), 0)
    mine = iota((ROWS, 512), 1) == iota((ROWS, 512), 0) + rank * ROWS
    leaf_len_row = ll_v[...].reshape(1, ROWS).astype(F32)
    positions = total(jnp.where(mine, base_row, 0.0), 1) + as_col(leaf_len_row)
    freq = freq_v[...]
    cosines, sines = rope_tables(positions, freq)
    wq_copy.wait()
    queries = rope(dot(normed, v["wq"][...]), cosines, sines).astype(BF16)
    queries = (queries.astype(F32) * (HEAD_DIM**-0.5)).astype(BF16)
    held_copy.wait()
    pl.semaphore_wait(barrier, NREQ + NTP - 2)

    after, ahead, across, sibling = tp_peer(2), tp_peer(6), tp_peer(4), tp + 1 - 2 * lax.rem(tp, 2)
    held = v["held"]
    low, high = slice(0, 128), slice(128, 256)
    held_copies = [
        send(held.at[tp], held.at[tp], hsem, 0, {"tp": after}),
        send(held.at[tp], held.at[tp], hsem, 1, {"tp": ahead}),
        send(held.at[tp], held.at[tp], hsem, 4, {"tp": sibling}),
    ]
    own_rows = pl.ds(pl.multiple_of(rank * ROWS, ROWS), ROWS)
    v["qall"][own_rows, :] = queries
    q_slot = v["qall"].at[own_rows]
    q_copies = [send(q_slot, q_slot, qsem, d, {"req": req_peer(d)}) for d in range(1, NREQ)]
    for copy in (leaf_copy, wout_copy, wgu_copy, wdn_copy):
        copy.start()

    root_row = total(jnp.where(belongs, mp_col, 0.0), 0)
    by_root = (iota((8, 512), 0).astype(F32) == root_row).astype(F32)
    in_mid = lp_row == rank
    groups = jnp.concatenate(
        [by_root, jnp.broadcast_to(in_mid.astype(F32), (8, 512))], axis=0
    ).astype(BF16)
    before = (iota((512, 512), 0) < iota((512, 512), 1)).astype(BF16)
    order = dot(groups, before)
    blocks = jnp.floor((total(by_root, 1) + (BLOCK - 1)) * (1.0 / BLOCK))
    first = total(jnp.where(iota((8, 8), 1) < iota((8, 8), 0), as_row(blocks), 0.0), 1)
    dest = total(by_root * (order[:8] + first * BLOCK), 0)
    ends = (first + blocks) <= iota((8, 128), 1).astype(F32)
    root_of = jnp.minimum(total(ends.astype(F32), 0), 7.0)
    v["table"][...] = jnp.broadcast_to(root_of, (8, 128)).astype(I32)
    table_copy = pltpu.make_async_copy(v["table"], table_s, copy_sem.at[19])
    table_copy.start()
    mid_order = order[8:9]
    v["pick"][...] = (iota((SORTED, 512), 0) == dest.astype(I32)).astype(BF16)
    turned = iota((512, 512), 1) == lax.rem(iota((512, 512), 0) + rank * ROWS, 512)
    final = total(jnp.where(turned, jnp.where(in_mid, SORTED + mid_order, dest), 0.0), 1).astype(I32)
    v["back"][...] = (iota((512, gathered), 1) == final).astype(BF16)
    if gathered > mid_end:
        v["xs"][mid_end:, :] = jnp.zeros((gathered - mid_end, MSG), BF16)
    lane256 = iota((1, 256), 1)
    for r in range(8):
        v["root_bias"][r] = jnp.where(
            (lane256 + rank * 256).astype(F32) < rl_row[:, r : r + 1], 0.0, NEG_FILL
        )
    own_len = total(jnp.where(iota((16, 1), 0) == rank, ml_col, 0.0), 0)
    own_parent = total(jnp.where(iota((16, 1), 0) == rank, parent_len, 0.0), 0)
    rr = rr_v[...]
    rr_col = as_col(rr.astype(F32))
    slot_col = rr_col.astype(I32)
    hit_hi = (iota((16, 256), 0) == rr // 128).astype(BF16)
    hit_lo = (iota((256, 128), 1) == slot_col % 128).astype(BF16)
    token = (iota((16, 128), 0) * 128 + iota((16, 128), 1)).astype(F32)
    alive = (token < own_len) & (dot(hit_hi, hit_lo) < 0.5)
    v["mid_bias"][...] = jnp.where(alive, 0.0, NEG_FILL)
    new_bias = jnp.where(rr.astype(F32) < own_len, 0.0, NEG_FILL)
    held_cos, held_sin = rope_tables(own_parent + rr_col, freq)

    r2, c2 = iota((256, 256), 0), iota((256, 256), 1)
    split = (c2 == jnp.where(r2 < 128, 2 * r2, 2 * r2 - 255)).astype(BF16)
    wkv_copy.wait()
    split_pairs(split, v["wkv"], v["wk"], v["wv"], 16)
    root_copy.wait()
    for k in range(16):
        both = dot(split, v["root"][k * 256 : (k + 1) * 256, :]).astype(BF16)
        half = slice((k % 2) * 128, (k % 2) * 128 + 128)
        v["root_k"][k // 2, half, :] = both[:128]
        v["root_v"][k // 2, half, :] = both[128:]
    held_copies[0].wait_recv()
    held_copies[1].wait_recv()
    held_copies += [
        send(held.at[ahead, low], held.at[ahead, low], hsem, 2, {"tp": after}),
        send(held.at[after, high], held.at[after, high], hsem, 3, {"tp": ahead}),
        send(held.at[ahead], held.at[ahead], hsem, 5, {"tp": sibling}),
        send(held.at[after], held.at[after], hsem, 6, {"tp": sibling}),
    ]

    mid_copy.wait()
    split_pairs(split, v["mid"], v["mid_k"], v["mid_v"], 16)
    key_new = rope(dot(normed, v["wk"][...]), cosines, sines).astype(BF16)
    value_new = dot(normed, v["wv"][...]).astype(BF16)

    for copy in q_copies:
        copy.wait_recv()
    v["qs"][...] = dot(v["pick"][...], v["qall"][...]).astype(BF16)
    held_copies[3].wait_recv()
    held_copies[4].wait_recv()
    held_copies += [
        send(held.at[across, low], held.at[across, low], hsem, 7, {"tp": sibling}),
        send(held.at[across, high], held.at[across, high], hsem, 8, {"tp": sibling}),
    ]
    block_mask = (iota((128, WIDTH), 0) // BLOCK == iota((128, WIDTH), 1) // HEAD_DIM).astype(BF16)
    table_copy.wait()

    def root_blocks(i, carry):
        ats = [
            pl.ds(pl.multiple_of((i * GROUP + u) * BLOCK, BLOCK), BLOCK) for u in range(GROUP)
        ]
        roots = [jnp.clip(table_s[0, i * GROUP + u], 0, 7) for u in range(GROUP)]
        qbds = [jnp.concatenate([v["qs"][at, :]] * HEADS, axis=0) * block_mask for at in ats]
        scores = [
            dot_t(qbd, v["root_k"][root]) + v["root_bias"][root] for qbd, root in zip(qbds, roots)
        ]
        tops = [jnp.max(score, axis=1, keepdims=True) for score in scores]
        weights = [jnp.exp(score - m) for score, m in zip(scores, tops)]
        sums = [total(weight, 1) for weight in weights]
        accs = [
            dot(weight.astype(BF16), v["root_v"][root]) for weight, root in zip(weights, roots)
        ]
        outs = []
        for m, row_sum, acc in zip(tops, sums, accs):
            out = head_columns(acc, BLOCK, WIDTH) / head_columns(row_sum, BLOCK, WIDTH)
            outs.append(packed(out, head_columns(m + jnp.log(row_sum), BLOCK, STATS)))
        for at, out in zip(ats, outs):
            v["xs"][at, :] = out
        return carry

    lax.fori_loop(0, BLOCKS // GROUP, root_blocks, 0)

    for copy in [held_copies[2]] + held_copies[5:]:
        copy.wait_recv()
    square = jnp.zeros((256, 1), F32)
    for c in range(NTP):
        part = v["held"][c].astype(F32)
        square = square + total(part * part, 1)
    scale = lax.rsqrt(square * (1.0 / D) + EPSILON)
    keys = jnp.zeros((256, WIDTH), F32)
    values = jnp.zeros((256, WIDTH), F32)
    for c in range(NTP):
        rows = slice(c * 256, (c + 1) * 256)
        part = (v["held"][c].astype(F32) * scale * gain[:, rows]).astype(BF16)
        keys = keys + dot(part, v["wk"][rows, :])
        values = values + dot(part, v["wv"][rows, :])
    v["new_k"][...] = rope(keys, held_cos, held_sin).astype(BF16)
    v["new_v"][...] = values.astype(BF16)

    mid_mask = (iota((256, WIDTH), 0) // MID_ROWS == iota((256, WIDTH), 1) // HEAD_DIM).astype(BF16)
    e0, e1 = iota((STATS, WIDTH), 0), iota((STATS, WIDTH), 1)
    expand3 = ((e0 < 12) & ((e0 % HEADS) == e1 // HEAD_DIM)).astype(BF16)
    lane64 = iota((MID_ROWS, STATS), 1)

    def mid_pass(p):
        chosen = (iota((MID_ROWS, 512), 0) + p * MID_ROWS == mid_order.astype(I32)) & in_mid
        mid_dest = total(jnp.where(chosen, dest, 0.0), 1)
        q_mid = dot(chosen.astype(BF16), v["qall"][...]).astype(BF16)
        take = (iota((MID_ROWS, SORTED), 1) == mid_dest.astype(I32)).astype(BF16)
        rooted = dot(take, v["xs"][:SORTED, :])
        qbd = jnp.concatenate([q_mid] * HEADS, axis=0) * mid_mask
        fresh = dot_t(qbd, v["new_k"][...]) + new_bias
        m = jnp.max(fresh, axis=1, keepdims=True)
        for c in range(8):
            cols = slice(c * 256, (c + 1) * 256)
            bias = jnp.concatenate(
                [v["mid_bias"][2 * c : 2 * c + 1, :], v["mid_bias"][2 * c + 1 : 2 * c + 2, :]], axis=1
            )
            scores = dot_t(qbd, v["mid_k"][cols, :]) + bias
            v["scores"][:, cols] = scores
            m = jnp.maximum(m, jnp.max(scores, axis=1, keepdims=True))
        weights = jnp.exp(fresh - m)
        row_sum = total(weights, 1)
        acc = dot(weights.astype(BF16), v["new_v"][...])
        for c in range(8):
            cols = slice(c * 256, (c + 1) * 256)
            weights = jnp.exp(v["scores"][:, cols] - m)
            row_sum = row_sum + total(weights, 1)
            v["weights"][:, cols] = weights.astype(BF16)
        acc = acc + dot(v["weights"][...], v["mid_v"][...])
        mid_out = head_columns(acc, MID_ROWS, WIDTH) / head_columns(row_sum, MID_ROWS, WIDTH)
        mid_lse = m + jnp.log(row_sum)
        lse_a = dot(rooted[:, WIDTH:].astype(BF16), expand3)
        lse_b = head_columns(mid_lse, MID_ROWS, WIDTH)
        top = jnp.maximum(lse_a, lse_b)
        part_a, part_b = jnp.exp(lse_a - top), jnp.exp(lse_b - top)
        merged = (part_a * rooted[:, :WIDTH] + part_b * mid_out) / (part_a + part_b)
        lse_a = jnp.where(lane64 < 4, unpacked_lse(rooted[:, WIDTH:]), 0.0)
        lse_a = lse_a + pltpu.roll(lse_a, 4, 1) + pltpu.roll(lse_a, 8, 1)
        lse_b = head_columns(mid_lse, MID_ROWS, STATS)
        top = jnp.maximum(lse_a, lse_b)
        joined = top + jnp.log(jnp.exp(lse_a - top) + jnp.exp(lse_b - top))
        at = SORTED if passes == 1 else pl.multiple_of(SORTED + p * MID_ROWS, MID_ROWS)
        v["xs"][pl.ds(at, MID_ROWS), :] = packed(merged, joined)

    if passes == 1:
        mid_pass(0)
    else:

        def mid_step(p, carry):
            mid_pass(p)
            return carry

        lax.fori_loop(0, passes, mid_step, 0)

    lane128, row128 = iota((128, STATS), 1), iota((128, STATS), 0)
    to_place = ((row128 < 12) & (row128 % HEADS == lane128 // ROWS)).astype(BF16)
    diagonal = lane128 % ROWS == row128 % ROWS
    row8 = iota((8, WIDTH), 0)
    a_copies = []
    for g in range(4):
        natural = dot(v["back"][g * 128 : (g + 1) * 128, :], v["xs"][...])
        placed = dot(natural[:, WIDTH:].astype(BF16), to_place)
        placed = jnp.where(diagonal, placed, 0.0)
        for d in range(g * 4, g * 4 + 4):
            rows = slice((d - g * 4) * ROWS, (d - g * 4 + 1) * ROWS)
            v["parts"][d, :ROWS, :] = natural[rows, :WIDTH].astype(BF16)
            lse = total(placed[rows], 0)
            a, b, c = three_terms(jnp.concatenate([lse, jnp.zeros((1, STATS), F32)], axis=1))
            tail = jnp.where(
                row8 == 0,
                a.astype(F32),
                jnp.where(row8 == 1, b.astype(F32), jnp.where(row8 == 2, c.astype(F32), 0.0)),
            )
            v["parts"][d, ROWS:, :] = tail.astype(BF16)
            if d > 0:
                a_copies.append(
                    send(v["parts"].at[d], v["arrived"].at[d], asem, d, {"req": req_peer(d)})
                )
    v["arrived"][0] = v["parts"][0]

    repeat = (iota((256, ROWS), 0) // 8 == iota((256, ROWS), 1)).astype(BF16)
    head_mask = (r2 % 8) == (c2 // HEAD_DIM)
    qrep = jnp.where(head_mask, dot(repeat, queries), 0.0)
    v["leaf_q"][...] = qrep.astype(BF16)
    self_score = total(qrep * dot(repeat, key_new), 1)
    live_len = total(repeat.astype(F32) * leaf_len_row, 1)
    leaf_copy.wait()
    for r in range(ROWS):
        v["leaf_s"][r * 8 : (r + 1) * 8, :] = dot_t(
            v["leaf_q"][r * 8 : (r + 1) * 8, :], v["leaf"][r * 256 : (r + 1) * 256, :]
        )
    live = ((c2 % 2) == 1) & ((c2 // 2).astype(F32) < live_len)
    scores = jnp.where(live, shift_pairs(v["leaf_s"][...]), NEG_FILL)
    best = jnp.maximum(jnp.max(scores, axis=1, keepdims=True), self_score)
    weights = jnp.exp(scores - best)
    self_weight = jnp.exp(self_score - best)
    row_sum = total(weights, 1) + self_weight
    v["leaf_q"][...] = weights.astype(BF16)
    for r in range(ROWS):
        v["leaf_s"][r * 8 : (r + 1) * 8, :] = dot(
            v["leaf_q"][r * 8 : (r + 1) * 8, :], v["leaf"][r * 256 : (r + 1) * 256, :]
        )
    acc = v["leaf_s"][...] + self_weight.astype(BF16).astype(F32) * dot(repeat, value_new)
    acc = jnp.where(head_mask, acc / row_sum, 0.0)
    leaf_out = jnp.sum(acc.reshape(ROWS, 8, WIDTH), axis=1)
    lse = best + jnp.log(row_sum)
    place = ((r2 % 8) * ROWS + r2 // 8)[:, :STATS] == c2[:, :STATS]
    leaf_lse = total(jnp.where(place, lse, 0.0), 0)

    for copy in a_copies:
        copy.wait_recv()
    lses = [total(v["arrived"][s, ROWS:, :STATS].astype(F32), 0) for s in range(NREQ)]
    lses.append(leaf_lse)
    best = lses[0]
    for value in lses[1:]:
        best = jnp.maximum(best, value)
    shares = [jnp.exp(value - best) for value in lses]
    row_sum = shares[0]
    for value in shares[1:]:
        row_sum = row_sum + value
    diagonal = iota((ROWS, STATS), 1) % ROWS == iota((ROWS, STATS), 0)
    expand = ((r2 % STATS) // ROWS == c2 // HEAD_DIM).astype(BF16)
    pieces = []
    for share in shares:
        share = jnp.where(diagonal, share / row_sum, 0.0)
        high = share.astype(BF16)
        pieces.append(jnp.concatenate([high, (share - high.astype(F32)).astype(BF16)], axis=1))
    factors = dot(jnp.concatenate(pieces, axis=0), expand)
    attended = jnp.zeros((ROWS, WIDTH), F32)
    for s in range(NREQ + 1):
        source = v["arrived"][s, :ROWS, :].astype(F32) if s < NREQ else leaf_out
        attended = attended + factors[s * ROWS : (s + 1) * ROWS] * source
    attended = attended.astype(BF16)

    own_cols = pl.ds(pl.multiple_of(tp * WIDTH, WIDTH), WIDTH)

    def scatter(left, weight_v, outgoing, incoming, sems):
        copies = []
        for d in range(1, NTP):
            peer = tp_peer(d)
            cols = pl.ds(pl.multiple_of(peer * WIDTH, WIDTH), WIDTH)
            outgoing[d] = dot(left, weight_v[:, cols]).astype(BF16)
            copies.append(send(outgoing.at[d], incoming.at[d], sems, d, {"tp": peer}))
        return copies, dot(left, weight_v[:, own_cols])

    wout_copy.wait()
    r_copies, own_part = scatter(attended, v["wout"], v["rs_out"], v["rs_in"], rsem)
    residual = own_part + stream_v[:, own_cols].astype(F32)
    i2, j2 = iota((256, 512), 0), iota((256, 512), 1)
    to_even = (j2 == 2 * i2).astype(BF16)
    to_odd = (j2 == 2 * i2 + 1).astype(BF16)
    gain_row = mgain_v[...].reshape(1, D).astype(F32)
    v["gain"][...] = gain_row
    for d in range(1, NTP):
        r_copies[d - 1].wait_recv()
        residual = residual + v["rs_in"][d].astype(F32)

    v["ag"][0] = residual.astype(BF16)
    g_copies = [
        send(v["ag"].at[0], v["ag"].at[d], gsem, d, {"tp": tp_peer(d)}) for d in range(1, NTP)
    ]
    wgu_copy.wait()
    squares = jnp.zeros((ROWS, WIDTH), F32)
    for d in range(NTP):
        if d > 0:
            g_copies[d - 1].wait_recv()
        owner = tp_peer(NTP - d)
        part = v["ag"][d].astype(F32)
        squares = squares + part * part
        gain_cols = pl.ds(pl.multiple_of(owner * WIDTH, WIDTH), WIDTH)
        chunk = (part * v["gain"][:, gain_cols]).astype(BF16)
        mixed = jnp.concatenate([dot(chunk, to_even), dot(chunk, to_odd)], axis=0).astype(BF16)
        rows = pl.ds(pl.multiple_of(owner * 512, 512), 512)
        for n in range(4):
            cols = slice(n * 256, (n + 1) * 256)
            product = dot(mixed, v["wgu"][rows, cols])
            if d == 0:
                v["proj"][:, cols] = product
            else:
                v["proj"][:, cols] += product
    scale = lax.rsqrt(total(squares, 1) * (1.0 / D) + EPSILON)
    gate = v["proj"][:ROWS, :] * scale
    up = v["proj"][ROWS:, :] * scale
    hidden = (gate / (1.0 + jnp.exp(-gate)) * up).astype(BF16)
    wdn_copy.wait()
    d_copies, own_part = scatter(hidden, v["wdn"], v["ds_out"], v["ds_in"], dsem)
    result = residual + own_part
    for d in range(1, NTP):
        d_copies[d - 1].wait_recv()
        result = result + v["ds_in"][d].astype(F32)
    out_ref[...] = result.astype(BF16)
    for copy in held_copies + q_copies + a_copies + r_copies + g_copies + d_copies:
        copy.wait_send()


def layer_device(
    passes,
    stream,
    attn_gain,
    mlp_gain,
    w_query,
    w_keyval,
    w_out,
    w_gate_up,
    w_down,
    root_cache,
    mid_cache,
    leaf_cache,
    held_hidden,
    recompute_rows,
    root_len,
    mid_len,
    leaf_len,
    mid_parent,
    leaf_parent,
):
    freq = np.exp(np.arange(32, dtype=np.float32) * np.float32(-2.0 * math.log(THETA_BASE) / HEAD_DIM))
    freq = jnp.asarray(np.tile(freq.astype(np.float32), 4)[None, :])
    dma = pltpu.SemaphoreType.DMA
    return pl.pallas_call(
        functools.partial(layer_kernel, passes),
        name="layer" if passes == 1 else "layer_crowded",
        out_shape=jax.ShapeDtypeStruct((ROWS, WIDTH), BF16),
        in_specs=[pl.BlockSpec(memory_space=pltpu.HBM)] * 19,
        out_specs=pl.BlockSpec(memory_space=pltpu.VMEM),
        scratch_shapes=[pltpu.VMEM(*s) for s in SMALL]
        + [pltpu.VMEM(*s) for s in sized(passes).values()]
        + [
            pltpu.SMEM((8, 128), I32),
            dma((20,)),
            dma((2, 9)),
            dma((2, NREQ)),
            dma((2, NREQ)),
            dma((2, NTP)),
            dma((2, NTP)),
            dma((2, NTP)),
        ],
        compiler_params=pltpu.CompilerParams(
            collective_id=0 if passes == 1 else 1, has_side_effects=True, vmem_limit_bytes=56 * 1024 * 1024
        ),
    )(
        stream,
        attn_gain,
        mlp_gain,
        leaf_parent,
        mid_parent,
        root_len,
        mid_len,
        leaf_len,
        recompute_rows,
        freq,
        w_query,
        w_keyval,
        w_out,
        w_gate_up,
        w_down,
        root_cache,
        mid_cache,
        leaf_cache,
        held_hidden,
    )


def on_device(*args):
    leaf_parent = args[17]
    counts = jnp.sum(
        (leaf_parent[None, :] == jnp.arange(16, dtype=I32)[:, None]).astype(I32), axis=1
    )
    usual = functools.partial(layer_device, 1)
    crowded = functools.partial(layer_device, 512 // MID_ROWS)
    return lax.cond(jnp.max(counts) <= MID_ROWS, usual, crowded, *args)


def solution(mesh):
    placed = (
        P("req", None),
        P(),
        P(),
        P(None, "tp"),
        P(None, None, "tp"),
        P("tp", None),
        P(None, None, "tp"),
        P("tp", None),
        P(None, "req", None, "tp"),
        P("req", None, None, "tp"),
        P("req", None, None, "tp"),
        P("req", None, "tp"),
        P("req", None),
        P(),
        P(),
        P("req"),
        P(),
        P(),
    )
    return jax.shard_map(
        on_device, mesh=mesh, in_specs=placed, out_specs=P("req", "tp"), check_vma=False
    )
```

```python
import functools
import math

import jax
import jax.numpy as jnp
import numpy as np
from jax import lax
from jax.experimental import pallas as pl
from jax.experimental.pallas import tpu as pltpu
from jax.sharding import PartitionSpec as P

F32 = jnp.float32
BF16 = jnp.bfloat16
I32 = jnp.int32
D = 2048
HEAD_DIM = 64
EPSILON = 1e-05
THETA_BASE = 130000.0
NEG_FILL = -1e30
NREQ = 16
NTP = 8
ROWS = 32
WIDTH = 256
HEADS = 4
BLOCK = 32
BLOCKS = 24
GROUP = 8
FAR_TP = (4, 3, 5, 2, 6, 1, 7)
NEAR_TP = FAR_TP[::-1]
FAR_REQ = (10, 6, 9, 11, 14, 2, 8, 5, 7, 13, 15, 4, 12, 1, 3)
SORTED = BLOCKS * BLOCK
MID_ROWS = 64
STATS = 128
MSG = WIDTH + STATS


def iota(shape, dim):
    return lax.broadcasted_iota(I32, shape, dim)


def dot(a, b):
    return jnp.dot(a, b, preferred_element_type=F32)


def dot_t(a, b):
    return lax.dot_general(a, b, (((1,), (1,)), ((), ())), preferred_element_type=F32)


def as_col(row):
    n = row.shape[1]
    eye = iota((n, n), 0) == iota((n, n), 1)
    return jnp.sum(jnp.where(eye, row, 0.0), axis=1, keepdims=True)


def as_row(col):
    n = col.shape[0]
    eye = iota((n, n), 0) == iota((n, n), 1)
    return jnp.sum(jnp.where(eye, col, 0.0), axis=0, keepdims=True)


def rope_tables(positions, inv_freq):
    angles = positions * inv_freq
    return jnp.cos(angles), jnp.sin(angles)


def rope(values, cosines, sines):
    n = values.shape[0]
    low = (iota((n, 128), 1) % 64) < 32
    parts = []
    for t in range(2):
        v = values[:, t * 128 : (t + 1) * 128]
        turned = jnp.where(low, -pltpu.roll(v, 96, 1), pltpu.roll(v, 32, 1))
        parts.append(v * cosines + turned * sines)
    return jnp.concatenate(parts, axis=1)


def shift_pairs(scores):
    width = scores.shape[1]
    return jnp.concatenate(
        [pltpu.roll(scores[:, i : i + 128], 1, 1) for i in range(0, width, 128)], axis=1
    )


def three_terms(values):
    first = values.astype(BF16)
    rest = values - first.astype(F32)
    second = rest.astype(BF16)
    third = (rest - second.astype(F32)).astype(BF16)
    return first, second, third


def total(values, axis):
    return jnp.sum(values, axis=axis, keepdims=True)


def head_columns(stacked, rows, width):
    lanes = iota((rows, width), 1)
    group = lanes // HEAD_DIM if width == WIDTH else lanes % HEADS
    picked = jnp.broadcast_to(stacked[:rows], (rows, width))
    for h in range(1, HEADS):
        picked = jnp.where(group == h, stacked[h * rows : (h + 1) * rows], picked)
    return picked


def packed(out, lse):
    lanes = iota(lse.shape, 1)
    a, b, c = three_terms(lse)
    stats = jnp.where(
        lanes < 4,
        a.astype(F32),
        jnp.where(lanes < 8, b.astype(F32), jnp.where(lanes < 12, c.astype(F32), 0.0)),
    )
    return jnp.concatenate([out, stats], axis=1).astype(BF16)


def unpacked_lse(stats):
    return stats + pltpu.roll(stats, 124, 1) + pltpu.roll(stats, 120, 1)


def split_pairs(split, pairs_v, first_v, second_v, tiles):
    for k in range(tiles):
        both = dot(split, pairs_v[k * 256 : (k + 1) * 256, :]).astype(BF16)
        first_v[k * 128 : (k + 1) * 128, :] = both[:128]
        second_v[k * 128 : (k + 1) * 128, :] = both[128:]


SMALL = (
    ((ROWS, D), BF16),
    ((D,), BF16),
    ((D,), BF16),
    ((512,), I32),
    ((16,), I32),
    ((8,), I32),
    ((16,), I32),
    ((ROWS,), I32),
    ((1, 256), I32),
    ((1, 128), F32),
)
WORK = dict(
    wq=((D, WIDTH), BF16),
    wkv=((2 * D, WIDTH), BF16),
    wk=((D, WIDTH), BF16),
    wv=((D, WIDTH), BF16),
    wout=((WIDTH, D), BF16),
    wgu=((2 * D, 1024), BF16),
    wdn=((1024, D), BF16),
    root=((4096, WIDTH), BF16),
    root_k=((8, 256, WIDTH), BF16),
    root_v=((8, 256, WIDTH), BF16),
    root_bias=((8, 1, 256), F32),
    mid=((4096, WIDTH), BF16),
    mid_k=((2048, WIDTH), BF16),
    mid_v=((2048, WIDTH), BF16),
    mid_bias=((16, 128), F32),
    leaf=((8192, WIDTH), BF16),
    held=((NTP, 256, 256), BF16),
    qall=((512, WIDTH), BF16),
    pick=((SORTED, 512), BF16),
    qs=((SORTED, WIDTH), BF16),
    table=((8, 128), I32),
    new_k=((256, WIDTH), BF16),
    new_v=((256, WIDTH), BF16),
    scores=((256, 2048), F32),
    weights=((256, 2048), BF16),
    leaf_q=((256, WIDTH), BF16),
    leaf_s=((256, WIDTH), F32),
    parts=((NREQ, ROWS + 8, WIDTH), BF16),
    arrived=((NREQ, ROWS + 8, WIDTH), BF16),
    rs_out=((NTP, ROWS, WIDTH), BF16),
    rs_in=((NTP, ROWS, WIDTH), BF16),
    ag=((NTP, ROWS, WIDTH), BF16),
    gain=((1, D), F32),
    ds_out=((NTP, ROWS, WIDTH), BF16),
    ds_in=((NTP, ROWS, WIDTH), BF16),
    proj=((2 * ROWS, 1024), F32),
)


def sized(passes):
    gathered = -(-(SORTED + passes * MID_ROWS) // 128) * 128
    return dict(WORK, back=((512, gathered), BF16), xs=((gathered, MSG), BF16))


def layer_kernel(passes, *refs):
    sizes = sized(passes)
    gathered = sizes["xs"][0][0]
    mid_end = SORTED + passes * MID_ROWS
    small_hbm = refs[:10]
    wq_hbm, wkv_hbm, wout_hbm, wgu_hbm, wdn_hbm, root_hbm, mid_hbm, leaf_hbm, held_hbm = refs[10:19]
    out_ref = refs[19]
    small = refs[20:30]
    v = dict(zip(sizes, refs[30 : 30 + len(sizes)]))
    table_s, copy_sem, hsem, qsem, asem, rsem, gsem, dsem = refs[30 + len(sizes) :]
    stream_v, again_v, mgain_v, lp_v, mp_v, rl_v, ml_v, ll_v, rr_v, freq_v = small
    rank = lax.axis_index("req")
    tp = lax.axis_index("tp")

    def req_peer(d):
        return lax.rem(rank + d, NREQ)

    def tp_peer(d):
        return lax.rem(tp + d, NTP)

    def send(src, dst, sems, d, target):
        copy = pltpu.make_async_remote_copy(
            src_ref=src,
            dst_ref=dst,
            send_sem=sems.at[0, d],
            recv_sem=sems.at[1, d],
            device_id=target,
        )
        copy.start()
        return copy

    barrier = pltpu.get_barrier_semaphore()
    for d in range(1, NREQ):
        pl.semaphore_signal(barrier, inc=1, device_id={"req": req_peer(d)})
    for d in range(1, NTP):
        pl.semaphore_signal(barrier, inc=1, device_id={"tp": tp_peer(d)})

    small_copies = [
        pltpu.make_async_copy(src, dst, copy_sem.at[i])
        for i, (src, dst) in enumerate(zip(small_hbm, small))
    ]
    wq_copy = pltpu.make_async_copy(wq_hbm, v["wq"], copy_sem.at[10])
    wkv_copy = pltpu.make_async_copy(wkv_hbm.reshape(2 * D, WIDTH), v["wkv"], copy_sem.at[11])
    root_copy = pltpu.make_async_copy(root_hbm.reshape(4096, WIDTH), v["root"], copy_sem.at[12])
    mid_copy = pltpu.make_async_copy(mid_hbm.reshape(4096, WIDTH), v["mid"], copy_sem.at[13])
    leaf_copy = pltpu.make_async_copy(leaf_hbm.reshape(8192, WIDTH), v["leaf"], copy_sem.at[14])
    wout_copy = pltpu.make_async_copy(wout_hbm, v["wout"], copy_sem.at[15])
    wgu_copy = pltpu.make_async_copy(wgu_hbm.reshape(2 * D, 1024), v["wgu"], copy_sem.at[16])
    wdn_copy = pltpu.make_async_copy(wdn_hbm, v["wdn"], copy_sem.at[17])
    held_copy = pltpu.make_async_copy(held_hbm.at[0], v["held"].at[tp], copy_sem.at[18])
    for copy in small_copies + [wq_copy, held_copy, wkv_copy, root_copy, mid_copy]:
        copy.start()
    for copy in small_copies:
        copy.wait()

    gain = again_v[...].reshape(1, D).astype(F32)
    x = stream_v[...].astype(F32)
    normed = (
        x * lax.rsqrt(jnp.mean(x * x, axis=-1, keepdims=True) + EPSILON) * gain
    ).astype(BF16)
    lp_row = lp_v[...].reshape(1, 512)
    mp_col = as_col(mp_v[...].reshape(1, 16).astype(F32))
    ml_col = as_col(ml_v[...].reshape(1, 16).astype(F32))
    rl_row = rl_v[...].reshape(1, 8).astype(F32)
    parent_len = total(jnp.where(iota((16, 8), 1).astype(F32) == mp_col, rl_row, 0.0), 1)
    belongs = iota((16, 512), 0) == lp_row
    base_row = total(jnp.where(belongs, parent_len + ml_col, 0.0), 0)
    mine = iota((ROWS, 512), 1) == iota((ROWS, 512), 0) + rank * ROWS
    leaf_len_row = ll_v[...].reshape(1, ROWS).astype(F32)
    positions = total(jnp.where(mine, base_row, 0.0), 1) + as_col(leaf_len_row)
    freq = freq_v[...]
    cosines, sines = rope_tables(positions, freq)
    wq_copy.wait()
    queries = rope(dot(normed, v["wq"][...]), cosines, sines).astype(BF16)
    queries = (queries.astype(F32) * (HEAD_DIM**-0.5)).astype(BF16)
    held_copy.wait()
    pl.semaphore_wait(barrier, NREQ + NTP - 2)

    after, ahead, across, sibling = tp_peer(2), tp_peer(6), tp_peer(4), tp + 1 - 2 * lax.rem(tp, 2)
    held = v["held"]
    low, high = slice(0, 128), slice(128, 256)
    held_copies = [
        send(held.at[tp], held.at[tp], hsem, 0, {"tp": after}),
        send(held.at[tp], held.at[tp], hsem, 1, {"tp": ahead}),
        send(held.at[tp], held.at[tp], hsem, 4, {"tp": sibling}),
    ]
    own_rows = pl.ds(pl.multiple_of(rank * ROWS, ROWS), ROWS)
    v["qall"][own_rows, :] = queries
    q_slot = v["qall"].at[own_rows]
    q_copies = [send(q_slot, q_slot, qsem, d, {"req": req_peer(d)}) for d in FAR_REQ]
    leaf_copy.start()
    wout_copy.start()

    root_row = total(jnp.where(belongs, mp_col, 0.0), 0)
    by_root = (iota((8, 512), 0).astype(F32) == root_row).astype(F32)
    in_mid = lp_row == rank
    groups = jnp.concatenate(
        [by_root, jnp.broadcast_to(in_mid.astype(F32), (8, 512))], axis=0
    ).astype(BF16)
    before = (iota((512, 512), 0) < iota((512, 512), 1)).astype(BF16)
    order = dot(groups, before)
    blocks = jnp.floor((total(by_root, 1) + (BLOCK - 1)) * (1.0 / BLOCK))
    first = total(jnp.where(iota((8, 8), 1) < iota((8, 8), 0), as_row(blocks), 0.0), 1)
    dest = total(by_root * (order[:8] + first * BLOCK), 0)
    ends = (first + blocks) <= iota((8, 128), 1).astype(F32)
    root_of = jnp.minimum(total(ends.astype(F32), 0), 7.0)
    v["table"][...] = jnp.broadcast_to(root_of, (8, 128)).astype(I32)
    table_copy = pltpu.make_async_copy(v["table"], table_s, copy_sem.at[19])
    table_copy.start()
    mid_order = order[8:9]
    v["pick"][...] = (iota((SORTED, 512), 0) == dest.astype(I32)).astype(BF16)
    turned = iota((512, 512), 1) == lax.rem(iota((512, 512), 0) + rank * ROWS, 512)
    final = total(jnp.where(turned, jnp.where(in_mid, SORTED + mid_order, dest), 0.0), 1).astype(I32)
    v["back"][...] = (iota((512, gathered), 1) == final).astype(BF16)
    if gathered > mid_end:
        v["xs"][mid_end:, :] = jnp.zeros((gathered - mid_end, MSG), BF16)
    lane256 = iota((1, 256), 1)
    for r in range(8):
        v["root_bias"][r] = jnp.where(
            (lane256 + rank * 256).astype(F32) < rl_row[:, r : r + 1], 0.0, NEG_FILL
        )
    own_len = total(jnp.where(iota((16, 1), 0) == rank, ml_col, 0.0), 0)
    own_parent = total(jnp.where(iota((16, 1), 0) == rank, parent_len, 0.0), 0)
    rr = rr_v[...]
    rr_col = as_col(rr.astype(F32))
    slot_col = rr_col.astype(I32)
    hit_hi = (iota((16, 256), 0) == rr // 128).astype(BF16)
    hit_lo = (iota((256, 128), 1) == slot_col % 128).astype(BF16)
    token = (iota((16, 128), 0) * 128 + iota((16, 128), 1)).astype(F32)
    alive = (token < own_len) & (dot(hit_hi, hit_lo) < 0.5)
    v["mid_bias"][...] = jnp.where(alive, 0.0, NEG_FILL)
    new_bias = jnp.where(rr.astype(F32) < own_len, 0.0, NEG_FILL)
    held_cos, held_sin = rope_tables(own_parent + rr_col, freq)

    r2, c2 = iota((256, 256), 0), iota((256, 256), 1)
    split = (c2 == jnp.where(r2 < 128, 2 * r2, 2 * r2 - 255)).astype(BF16)
    wkv_copy.wait()
    split_pairs(split, v["wkv"], v["wk"], v["wv"], 16)
    root_copy.wait()
    for k in range(16):
        both = dot(split, v["root"][k * 256 : (k + 1) * 256, :]).astype(BF16)
        half = slice((k % 2) * 128, (k % 2) * 128 + 128)
        v["root_k"][k // 2, half, :] = both[:128]
        v["root_v"][k // 2, half, :] = both[128:]
    held_copies[0].wait_recv()
    held_copies[1].wait_recv()
    held_copies += [
        send(held.at[ahead, low], held.at[ahead, low], hsem, 2, {"tp": after}),
        send(held.at[after, high], held.at[after, high], hsem, 3, {"tp": ahead}),
        send(held.at[ahead], held.at[ahead], hsem, 5, {"tp": sibling}),
        send(held.at[after], held.at[after], hsem, 6, {"tp": sibling}),
    ]

    mid_copy.wait()
    split_pairs(split, v["mid"], v["mid_k"], v["mid_v"], 16)
    key_new = rope(dot(normed, v["wk"][...]), cosines, sines).astype(BF16)
    value_new = dot(normed, v["wv"][...]).astype(BF16)

    for copy in q_copies:
        copy.wait_recv()
    v["qs"][...] = dot(v["pick"][...], v["qall"][...]).astype(BF16)
    held_copies[3].wait_recv()
    held_copies[4].wait_recv()
    held_copies += [
        send(held.at[across, low], held.at[across, low], hsem, 7, {"tp": sibling}),
        send(held.at[across, high], held.at[across, high], hsem, 8, {"tp": sibling}),
    ]
    block_mask = (iota((128, WIDTH), 0) // BLOCK == iota((128, WIDTH), 1) // HEAD_DIM).astype(BF16)
    table_copy.wait()

    def root_blocks(i, carry):
        ats = [
            pl.ds(pl.multiple_of((i * GROUP + u) * BLOCK, BLOCK), BLOCK) for u in range(GROUP)
        ]
        roots = [jnp.clip(table_s[0, i * GROUP + u], 0, 7) for u in range(GROUP)]
        qbds = [jnp.concatenate([v["qs"][at, :]] * HEADS, axis=0) * block_mask for at in ats]
        scores = [
            dot_t(qbd, v["root_k"][root]) + v["root_bias"][root] for qbd, root in zip(qbds, roots)
        ]
        tops = [jnp.max(score, axis=1, keepdims=True) for score in scores]
        weights = [jnp.exp(score - m) for score, m in zip(scores, tops)]
        sums = [total(weight, 1) for weight in weights]
        accs = [
            dot(weight.astype(BF16), v["root_v"][root]) for weight, root in zip(weights, roots)
        ]
        outs = []
        for m, row_sum, acc in zip(tops, sums, accs):
            out = head_columns(acc, BLOCK, WIDTH) / head_columns(row_sum, BLOCK, WIDTH)
            outs.append(packed(out, head_columns(m + jnp.log(row_sum), BLOCK, STATS)))
        for at, out in zip(ats, outs):
            v["xs"][at, :] = out
        return carry

    lax.fori_loop(0, BLOCKS // GROUP, root_blocks, 0)

    for copy in [held_copies[2]] + held_copies[5:]:
        copy.wait_recv()
    square = jnp.zeros((256, 1), F32)
    for c in range(NTP):
        part = v["held"][c].astype(F32)
        square = square + total(part * part, 1)
    scale = lax.rsqrt(square * (1.0 / D) + EPSILON)
    keys = jnp.zeros((256, WIDTH), F32)
    values = jnp.zeros((256, WIDTH), F32)
    for c in range(NTP):
        rows = slice(c * 256, (c + 1) * 256)
        part = (v["held"][c].astype(F32) * scale * gain[:, rows]).astype(BF16)
        keys = keys + dot(part, v["wk"][rows, :])
        values = values + dot(part, v["wv"][rows, :])
    v["new_k"][...] = rope(keys, held_cos, held_sin).astype(BF16)
    v["new_v"][...] = values.astype(BF16)

    mid_mask = (iota((256, WIDTH), 0) // MID_ROWS == iota((256, WIDTH), 1) // HEAD_DIM).astype(BF16)
    e0, e1 = iota((STATS, WIDTH), 0), iota((STATS, WIDTH), 1)
    expand3 = ((e0 < 12) & ((e0 % HEADS) == e1 // HEAD_DIM)).astype(BF16)
    lane64 = iota((MID_ROWS, STATS), 1)

    def mid_pass(p):
        chosen = (iota((MID_ROWS, 512), 0) + p * MID_ROWS == mid_order.astype(I32)) & in_mid
        mid_dest = total(jnp.where(chosen, dest, 0.0), 1)
        q_mid = dot(chosen.astype(BF16), v["qall"][...]).astype(BF16)
        take = (iota((MID_ROWS, SORTED), 1) == mid_dest.astype(I32)).astype(BF16)
        rooted = dot(take, v["xs"][:SORTED, :])
        qbd = jnp.concatenate([q_mid] * HEADS, axis=0) * mid_mask
        fresh = dot_t(qbd, v["new_k"][...]) + new_bias
        m = jnp.max(fresh, axis=1, keepdims=True)
        for c in range(8):
            cols = slice(c * 256, (c + 1) * 256)
            bias = jnp.concatenate(
                [v["mid_bias"][2 * c : 2 * c + 1, :], v["mid_bias"][2 * c + 1 : 2 * c + 2, :]], axis=1
            )
            scores = dot_t(qbd, v["mid_k"][cols, :]) + bias
            v["scores"][:, cols] = scores
            m = jnp.maximum(m, jnp.max(scores, axis=1, keepdims=True))
        weights = jnp.exp(fresh - m)
        row_sum = total(weights, 1)
        acc = dot(weights.astype(BF16), v["new_v"][...])
        for c in range(8):
            cols = slice(c * 256, (c + 1) * 256)
            weights = jnp.exp(v["scores"][:, cols] - m)
            row_sum = row_sum + total(weights, 1)
            v["weights"][:, cols] = weights.astype(BF16)
        acc = acc + dot(v["weights"][...], v["mid_v"][...])
        mid_out = head_columns(acc, MID_ROWS, WIDTH) / head_columns(row_sum, MID_ROWS, WIDTH)
        mid_lse = m + jnp.log(row_sum)
        lse_a = dot(rooted[:, WIDTH:].astype(BF16), expand3)
        lse_b = head_columns(mid_lse, MID_ROWS, WIDTH)
        top = jnp.maximum(lse_a, lse_b)
        part_a, part_b = jnp.exp(lse_a - top), jnp.exp(lse_b - top)
        merged = (part_a * rooted[:, :WIDTH] + part_b * mid_out) / (part_a + part_b)
        lse_a = jnp.where(lane64 < 4, unpacked_lse(rooted[:, WIDTH:]), 0.0)
        lse_a = lse_a + pltpu.roll(lse_a, 4, 1) + pltpu.roll(lse_a, 8, 1)
        lse_b = head_columns(mid_lse, MID_ROWS, STATS)
        top = jnp.maximum(lse_a, lse_b)
        joined = top + jnp.log(jnp.exp(lse_a - top) + jnp.exp(lse_b - top))
        at = SORTED if passes == 1 else pl.multiple_of(SORTED + p * MID_ROWS, MID_ROWS)
        v["xs"][pl.ds(at, MID_ROWS), :] = packed(merged, joined)

    if passes == 1:
        mid_pass(0)
    else:

        def mid_step(p, carry):
            mid_pass(p)
            return carry

        lax.fori_loop(0, passes, mid_step, 0)

    lane128, row128 = iota((128, STATS), 1), iota((128, STATS), 0)
    to_place = ((row128 < 12) & (row128 % HEADS == lane128 // ROWS)).astype(BF16)
    diagonal = lane128 % ROWS == row128 % ROWS
    row8 = iota((8, WIDTH), 0)
    a_copies = []
    for g in (2, 1, 3, 0):
        natural = dot(v["back"][g * 128 : (g + 1) * 128, :], v["xs"][...])
        placed = dot(natural[:, WIDTH:].astype(BF16), to_place)
        placed = jnp.where(diagonal, placed, 0.0)
        for d in range(g * 4, g * 4 + 4):
            rows = slice((d - g * 4) * ROWS, (d - g * 4 + 1) * ROWS)
            v["parts"][d, :ROWS, :] = natural[rows, :WIDTH].astype(BF16)
            lse = total(placed[rows], 0)
            a, b, c = three_terms(jnp.concatenate([lse, jnp.zeros((1, STATS), F32)], axis=1))
            tail = jnp.where(
                row8 == 0,
                a.astype(F32),
                jnp.where(row8 == 1, b.astype(F32), jnp.where(row8 == 2, c.astype(F32), 0.0)),
            )
            v["parts"][d, ROWS:, :] = tail.astype(BF16)
            if d > 0:
                a_copies.append(
                    send(v["parts"].at[d], v["arrived"].at[d], asem, d, {"req": req_peer(d)})
                )
    wgu_copy.start()
    wdn_copy.start()
    v["arrived"][0] = v["parts"][0]

    repeat = (iota((256, ROWS), 0) // 8 == iota((256, ROWS), 1)).astype(BF16)
    head_mask = (r2 % 8) == (c2 // HEAD_DIM)
    qrep = jnp.where(head_mask, dot(repeat, queries), 0.0)
    v["leaf_q"][...] = qrep.astype(BF16)
    self_score = total(qrep * dot(repeat, key_new), 1)
    live_len = total(repeat.astype(F32) * leaf_len_row, 1)
    leaf_copy.wait()
    for r in range(ROWS):
        v["leaf_s"][r * 8 : (r + 1) * 8, :] = dot_t(
            v["leaf_q"][r * 8 : (r + 1) * 8, :], v["leaf"][r * 256 : (r + 1) * 256, :]
        )
    live = ((c2 % 2) == 1) & ((c2 // 2).astype(F32) < live_len)
    scores = jnp.where(live, shift_pairs(v["leaf_s"][...]), NEG_FILL)
    best = jnp.maximum(jnp.max(scores, axis=1, keepdims=True), self_score)
    weights = jnp.exp(scores - best)
    self_weight = jnp.exp(self_score - best)
    row_sum = total(weights, 1) + self_weight
    v["leaf_q"][...] = weights.astype(BF16)
    for r in range(ROWS):
        v["leaf_s"][r * 8 : (r + 1) * 8, :] = dot(
            v["leaf_q"][r * 8 : (r + 1) * 8, :], v["leaf"][r * 256 : (r + 1) * 256, :]
        )
    acc = v["leaf_s"][...] + self_weight.astype(BF16).astype(F32) * dot(repeat, value_new)
    acc = jnp.where(head_mask, acc / row_sum, 0.0)
    leaf_out = jnp.sum(acc.reshape(ROWS, 8, WIDTH), axis=1)
    lse = best + jnp.log(row_sum)
    place = ((r2 % 8) * ROWS + r2 // 8)[:, :STATS] == c2[:, :STATS]
    leaf_lse = total(jnp.where(place, lse, 0.0), 0)

    for copy in a_copies:
        copy.wait_recv()
    lses = [total(v["arrived"][s, ROWS:, :STATS].astype(F32), 0) for s in range(NREQ)]
    lses.append(leaf_lse)
    best = lses[0]
    for value in lses[1:]:
        best = jnp.maximum(best, value)
    shares = [jnp.exp(value - best) for value in lses]
    row_sum = shares[0]
    for value in shares[1:]:
        row_sum = row_sum + value
    diagonal = iota((ROWS, STATS), 1) % ROWS == iota((ROWS, STATS), 0)
    expand = ((r2 % STATS) // ROWS == c2 // HEAD_DIM).astype(BF16)
    pieces = []
    for share in shares:
        share = jnp.where(diagonal, share / row_sum, 0.0)
        high = share.astype(BF16)
        pieces.append(jnp.concatenate([high, (share - high.astype(F32)).astype(BF16)], axis=1))
    factors = dot(jnp.concatenate(pieces, axis=0), expand)
    attended = jnp.zeros((ROWS, WIDTH), F32)
    for s in range(NREQ + 1):
        source = v["arrived"][s, :ROWS, :].astype(F32) if s < NREQ else leaf_out
        attended = attended + factors[s * ROWS : (s + 1) * ROWS] * source
    attended = attended.astype(BF16)

    own_cols = pl.ds(pl.multiple_of(tp * WIDTH, WIDTH), WIDTH)

    def scatter(left, weight_v, outgoing, incoming, sems):
        copies = {}
        for d in FAR_TP:
            peer = tp_peer(d)
            cols = pl.ds(pl.multiple_of(peer * WIDTH, WIDTH), WIDTH)
            outgoing[d] = dot(left, weight_v[:, cols]).astype(BF16)
            copies[d] = send(outgoing.at[d], incoming.at[d], sems, d, {"tp": peer})
        return copies, dot(left, weight_v[:, own_cols])

    wout_copy.wait()
    r_copies, own_part = scatter(attended, v["wout"], v["rs_out"], v["rs_in"], rsem)
    residual = own_part + stream_v[:, own_cols].astype(F32)
    i2, j2 = iota((256, 512), 0), iota((256, 512), 1)
    to_even = (j2 == 2 * i2).astype(BF16)
    to_odd = (j2 == 2 * i2 + 1).astype(BF16)
    gain_row = mgain_v[...].reshape(1, D).astype(F32)
    v["gain"][...] = gain_row
    for d in NEAR_TP:
        r_copies[d].wait_recv()
        residual = residual + v["rs_in"][d].astype(F32)

    v["ag"][0] = residual.astype(BF16)
    g_copies = {
        d: send(v["ag"].at[0], v["ag"].at[d], gsem, d, {"tp": tp_peer(d)}) for d in FAR_TP
    }
    wgu_copy.wait()
    squares = jnp.zeros((ROWS, WIDTH), F32)
    for d in (0, *NEAR_TP):
        if d > 0:
            g_copies[d].wait_recv()
        owner = tp_peer(NTP - d)
        part = v["ag"][d].astype(F32)
        squares = squares + part * part
        gain_cols = pl.ds(pl.multiple_of(owner * WIDTH, WIDTH), WIDTH)
        chunk = (part * v["gain"][:, gain_cols]).astype(BF16)
        mixed = jnp.concatenate([dot(chunk, to_even), dot(chunk, to_odd)], axis=0).astype(BF16)
        rows = pl.ds(pl.multiple_of(owner * 512, 512), 512)
        for n in range(4):
            cols = slice(n * 256, (n + 1) * 256)
            product = dot(mixed, v["wgu"][rows, cols])
            if d == 0:
                v["proj"][:, cols] = product
            else:
                v["proj"][:, cols] += product
    scale = lax.rsqrt(total(squares, 1) * (1.0 / D) + EPSILON)
    gate = v["proj"][:ROWS, :] * scale
    up = v["proj"][ROWS:, :] * scale
    hidden = (gate / (1.0 + jnp.exp(-gate)) * up).astype(BF16)
    wdn_copy.wait()
    d_copies, own_part = scatter(hidden, v["wdn"], v["ds_out"], v["ds_in"], dsem)
    result = residual + own_part
    for d in NEAR_TP:
        d_copies[d].wait_recv()
        result = result + v["ds_in"][d].astype(F32)
    out_ref[...] = result.astype(BF16)
    late = [*r_copies.values(), *g_copies.values(), *d_copies.values()]
    for copy in held_copies + q_copies + a_copies + late:
        copy.wait_send()


def layer_device(
    passes,
    stream,
    attn_gain,
    mlp_gain,
    w_query,
    w_keyval,
    w_out,
    w_gate_up,
    w_down,
    root_cache,
    mid_cache,
    leaf_cache,
    held_hidden,
    recompute_rows,
    root_len,
    mid_len,
    leaf_len,
    mid_parent,
    leaf_parent,
):
    freq = np.exp(np.arange(32, dtype=np.float32) * np.float32(-2.0 * math.log(THETA_BASE) / HEAD_DIM))
    freq = jnp.asarray(np.tile(freq.astype(np.float32), 4)[None, :])
    dma = pltpu.SemaphoreType.DMA
    return pl.pallas_call(
        functools.partial(layer_kernel, passes),
        name="layer" if passes == 1 else "layer_crowded",
        out_shape=jax.ShapeDtypeStruct((ROWS, WIDTH), BF16),
        in_specs=[pl.BlockSpec(memory_space=pltpu.HBM)] * 19,
        out_specs=pl.BlockSpec(memory_space=pltpu.VMEM),
        scratch_shapes=[pltpu.VMEM(*s) for s in SMALL]
        + [pltpu.VMEM(*s) for s in sized(passes).values()]
        + [
            pltpu.SMEM((8, 128), I32),
            dma((20,)),
            dma((2, 9)),
            dma((2, NREQ)),
            dma((2, NREQ)),
            dma((2, NTP)),
            dma((2, NTP)),
            dma((2, NTP)),
        ],
        compiler_params=pltpu.CompilerParams(
            collective_id=0 if passes == 1 else 1, has_side_effects=True, vmem_limit_bytes=56 * 1024 * 1024
        ),
    )(
        stream,
        attn_gain,
        mlp_gain,
        leaf_parent,
        mid_parent,
        root_len,
        mid_len,
        leaf_len,
        recompute_rows,
        freq,
        w_query,
        w_keyval,
        w_out,
        w_gate_up,
        w_down,
        root_cache,
        mid_cache,
        leaf_cache,
        held_hidden,
    )


def on_device(*args):
    leaf_parent = args[17]
    counts = jnp.sum(
        (leaf_parent[None, :] == jnp.arange(16, dtype=I32)[:, None]).astype(I32), axis=1
    )
    usual = functools.partial(layer_device, 1)
    crowded = functools.partial(layer_device, 512 // MID_ROWS)
    return lax.cond(jnp.max(counts) <= MID_ROWS, usual, crowded, *args)


def solution(mesh):
    placed = (
        P("req", None),
        P(),
        P(),
        P(None, "tp"),
        P(None, None, "tp"),
        P("tp", None),
        P(None, None, "tp"),
        P("tp", None),
        P(None, "req", None, "tp"),
        P("req", None, None, "tp"),
        P("req", None, None, "tp"),
        P("req", None, "tp"),
        P("req", None),
        P(),
        P(),
        P("req"),
        P(),
        P(),
    )
    return jax.shard_map(
        on_device, mesh=mesh, in_specs=placed, out_specs=P("req", "tp"), check_vma=False
    )
```

```python
import functools
import math

import jax
import jax.numpy as jnp
import numpy as np
from jax import lax
from jax.experimental import pallas as pl
from jax.experimental.pallas import tpu as pltpu
from jax.sharding import PartitionSpec as P

F32 = jnp.float32
BF16 = jnp.bfloat16
I32 = jnp.int32
D = 2048
HEAD_DIM = 64
EPSILON = 1e-05
THETA_BASE = 130000.0
NEG_FILL = -1e30
NREQ = 16
NTP = 8
ROWS = 32
WIDTH = 256
HEADS = 4
BLOCK = 32
BLOCKS = 24
GROUP = 8
SORTED = BLOCKS * BLOCK
MID_ROWS = 64
STATS = 128
MSG = WIDTH + STATS


def iota(shape, dim):
    return lax.broadcasted_iota(I32, shape, dim)


def dot(a, b):
    return jnp.dot(a, b, preferred_element_type=F32)


def dot_t(a, b):
    return lax.dot_general(a, b, (((1,), (1,)), ((), ())), preferred_element_type=F32)


def as_col(row):
    n = row.shape[1]
    eye = iota((n, n), 0) == iota((n, n), 1)
    return jnp.sum(jnp.where(eye, row, 0.0), axis=1, keepdims=True)


def as_row(col):
    n = col.shape[0]
    eye = iota((n, n), 0) == iota((n, n), 1)
    return jnp.sum(jnp.where(eye, col, 0.0), axis=0, keepdims=True)


def rope_tables(positions, inv_freq):
    angles = positions * inv_freq
    return jnp.cos(angles), jnp.sin(angles)


def rope(values, cosines, sines):
    n = values.shape[0]
    low = (iota((n, 128), 1) % 64) < 32
    parts = []
    for t in range(2):
        v = values[:, t * 128 : (t + 1) * 128]
        turned = jnp.where(low, -pltpu.roll(v, 96, 1), pltpu.roll(v, 32, 1))
        parts.append(v * cosines + turned * sines)
    return jnp.concatenate(parts, axis=1)


def shift_pairs(scores):
    width = scores.shape[1]
    return jnp.concatenate(
        [pltpu.roll(scores[:, i : i + 128], 1, 1) for i in range(0, width, 128)], axis=1
    )


def three_terms(values):
    first = values.astype(BF16)
    rest = values - first.astype(F32)
    second = rest.astype(BF16)
    third = (rest - second.astype(F32)).astype(BF16)
    return first, second, third


def total(values, axis):
    return jnp.sum(values, axis=axis, keepdims=True)


def head_columns(stacked, rows, width):
    lanes = iota((rows, width), 1)
    group = lanes // HEAD_DIM if width == WIDTH else lanes % HEADS
    picked = jnp.broadcast_to(stacked[:rows], (rows, width))
    for h in range(1, HEADS):
        picked = jnp.where(group == h, stacked[h * rows : (h + 1) * rows], picked)
    return picked


def packed(out, lse):
    lanes = iota(lse.shape, 1)
    a, b, c = three_terms(lse)
    stats = jnp.where(
        lanes < 4,
        a.astype(F32),
        jnp.where(lanes < 8, b.astype(F32), jnp.where(lanes < 12, c.astype(F32), 0.0)),
    )
    return jnp.concatenate([out, stats], axis=1).astype(BF16)


def unpacked_lse(stats):
    return stats + pltpu.roll(stats, 124, 1) + pltpu.roll(stats, 120, 1)


def split_pairs(split, pairs_v, first_v, second_v, tiles):
    for k in range(tiles):
        both = dot(split, pairs_v[k * 256 : (k + 1) * 256, :]).astype(BF16)
        first_v[k * 128 : (k + 1) * 128, :] = both[:128]
        second_v[k * 128 : (k + 1) * 128, :] = both[128:]


SMALL = (
    ((ROWS, D), BF16),
    ((D,), BF16),
    ((D,), BF16),
    ((512,), I32),
    ((16,), I32),
    ((8,), I32),
    ((16,), I32),
    ((ROWS,), I32),
    ((1, 256), I32),
    ((1, 128), F32),
)
WORK = dict(
    wq=((D, WIDTH), BF16),
    wkv=((2 * D, WIDTH), BF16),
    wk=((D, WIDTH), BF16),
    wv=((D, WIDTH), BF16),
    wout=((WIDTH, D), BF16),
    wgu=((2 * D, 1024), BF16),
    wdn=((1024, D), BF16),
    root=((4096, WIDTH), BF16),
    root_k=((8, 256, WIDTH), BF16),
    root_v=((8, 256, WIDTH), BF16),
    root_bias=((8, 1, 256), F32),
    mid=((4096, WIDTH), BF16),
    mid_k=((2048, WIDTH), BF16),
    mid_v=((2048, WIDTH), BF16),
    mid_bias=((16, 128), F32),
    leaf=((8192, WIDTH), BF16),
    held=((NTP, 256, 256), BF16),
    qall=((512, WIDTH), BF16),
    pick=((SORTED, 512), BF16),
    qs=((SORTED, WIDTH), BF16),
    table=((8, 128), I32),
    new_k=((256, WIDTH), BF16),
    new_v=((256, WIDTH), BF16),
    scores=((256, 2048), F32),
    weights=((256, 2048), BF16),
    leaf_q=((256, WIDTH), BF16),
    leaf_s=((256, WIDTH), F32),
    parts=((NREQ, ROWS + 8, WIDTH), BF16),
    arrived=((NREQ, ROWS + 8, WIDTH), BF16),
    rs_out=((NTP, ROWS, WIDTH), BF16),
    rs_in=((NTP, ROWS, WIDTH), BF16),
    ag=((NTP, ROWS, WIDTH), BF16),
    gain=((1, D), F32),
    ds_out=((NTP, ROWS, WIDTH), BF16),
    ds_in=((NTP, ROWS, WIDTH), BF16),
    proj=((2 * ROWS, 1024), F32),
)


def sized(passes):
    gathered = -(-(SORTED + passes * MID_ROWS) // 128) * 128
    return dict(WORK, back=((512, gathered), BF16), xs=((gathered, MSG), BF16))


def layer_kernel(passes, *refs):
    sizes = sized(passes)
    gathered = sizes["xs"][0][0]
    mid_end = SORTED + passes * MID_ROWS
    small_hbm = refs[:10]
    wq_hbm, wkv_hbm, wout_hbm, wgu_hbm, wdn_hbm, root_hbm, mid_hbm, leaf_hbm, held_hbm = refs[10:19]
    out_ref = refs[19]
    small = refs[20:30]
    v = dict(zip(sizes, refs[30 : 30 + len(sizes)]))
    table_s, copy_sem, hsem, qsem, asem, rsem, gsem, dsem = refs[30 + len(sizes) :]
    stream_v, again_v, mgain_v, lp_v, mp_v, rl_v, ml_v, ll_v, rr_v, freq_v = small
    rank = lax.axis_index("req")
    tp = lax.axis_index("tp")

    def req_peer(d):
        return lax.rem(rank + d, NREQ)

    def tp_peer(d):
        return lax.rem(tp + d, NTP)

    def send(src, dst, sems, d, target):
        copy = pltpu.make_async_remote_copy(
            src_ref=src,
            dst_ref=dst,
            send_sem=sems.at[0, d],
            recv_sem=sems.at[1, d],
            device_id=target,
        )
        copy.start()
        return copy

    barrier = pltpu.get_barrier_semaphore()
    for d in range(1, NREQ):
        pl.semaphore_signal(barrier, inc=1, device_id={"req": req_peer(d)})
    for d in range(1, NTP):
        pl.semaphore_signal(barrier, inc=1, device_id={"tp": tp_peer(d)})

    small_copies = [
        pltpu.make_async_copy(src, dst, copy_sem.at[i])
        for i, (src, dst) in enumerate(zip(small_hbm, small))
    ]
    wq_copy = pltpu.make_async_copy(wq_hbm, v["wq"], copy_sem.at[10])
    wkv_copy = pltpu.make_async_copy(wkv_hbm.reshape(2 * D, WIDTH), v["wkv"], copy_sem.at[11])
    root_copy = pltpu.make_async_copy(root_hbm.reshape(4096, WIDTH), v["root"], copy_sem.at[12])
    mid_copy = pltpu.make_async_copy(mid_hbm.reshape(4096, WIDTH), v["mid"], copy_sem.at[13])
    leaf_copy = pltpu.make_async_copy(leaf_hbm.reshape(8192, WIDTH), v["leaf"], copy_sem.at[14])
    wout_copy = pltpu.make_async_copy(wout_hbm, v["wout"], copy_sem.at[15])
    wgu_copy = pltpu.make_async_copy(wgu_hbm.reshape(2 * D, 1024), v["wgu"], copy_sem.at[16])
    wdn_copy = pltpu.make_async_copy(wdn_hbm, v["wdn"], copy_sem.at[17])
    held_copy = pltpu.make_async_copy(held_hbm.at[0], v["held"].at[tp], copy_sem.at[18])
    for copy in small_copies + [wq_copy, held_copy, wkv_copy, root_copy, mid_copy]:
        copy.start()
    for copy in small_copies:
        copy.wait()

    gain = again_v[...].reshape(1, D).astype(F32)
    x = stream_v[...].astype(F32)
    normed = (
        x * lax.rsqrt(jnp.mean(x * x, axis=-1, keepdims=True) + EPSILON) * gain
    ).astype(BF16)
    lp_row = lp_v[...].reshape(1, 512)
    mp_col = as_col(mp_v[...].reshape(1, 16).astype(F32))
    ml_col = as_col(ml_v[...].reshape(1, 16).astype(F32))
    rl_row = rl_v[...].reshape(1, 8).astype(F32)
    parent_len = total(jnp.where(iota((16, 8), 1).astype(F32) == mp_col, rl_row, 0.0), 1)
    belongs = iota((16, 512), 0) == lp_row
    base_row = total(jnp.where(belongs, parent_len + ml_col, 0.0), 0)
    mine = iota((ROWS, 512), 1) == iota((ROWS, 512), 0) + rank * ROWS
    leaf_len_row = ll_v[...].reshape(1, ROWS).astype(F32)
    positions = total(jnp.where(mine, base_row, 0.0), 1) + as_col(leaf_len_row)
    freq = freq_v[...]
    cosines, sines = rope_tables(positions, freq)
    wq_copy.wait()
    queries = rope(dot(normed, v["wq"][...]), cosines, sines).astype(BF16)
    queries = (queries.astype(F32) * (HEAD_DIM**-0.5)).astype(BF16)
    held_copy.wait()
    pl.semaphore_wait(barrier, NREQ + NTP - 2)

    after, ahead, across, sibling = tp_peer(2), tp_peer(6), tp_peer(4), tp + 1 - 2 * lax.rem(tp, 2)
    held = v["held"]
    low, high = slice(0, 128), slice(128, 256)
    held_copies = [
        send(held.at[tp], held.at[tp], hsem, 0, {"tp": after}),
        send(held.at[tp], held.at[tp], hsem, 1, {"tp": ahead}),
        send(held.at[tp], held.at[tp], hsem, 4, {"tp": sibling}),
    ]
    own_rows = pl.ds(pl.multiple_of(rank * ROWS, ROWS), ROWS)
    v["qall"][own_rows, :] = queries
    q_slot = v["qall"].at[own_rows]
    q_copies = [send(q_slot, q_slot, qsem, d, {"req": req_peer(d)}) for d in range(1, NREQ)]
    for copy in (leaf_copy, wout_copy, wgu_copy, wdn_copy):
        copy.start()

    root_row = total(jnp.where(belongs, mp_col, 0.0), 0)
    by_root = (iota((8, 512), 0).astype(F32) == root_row).astype(F32)
    in_mid = lp_row == rank
    groups = jnp.concatenate(
        [by_root, jnp.broadcast_to(in_mid.astype(F32), (8, 512))], axis=0
    ).astype(BF16)
    before = (iota((512, 512), 0) < iota((512, 512), 1)).astype(BF16)
    order = dot(groups, before)
    blocks = jnp.floor((total(by_root, 1) + (BLOCK - 1)) * (1.0 / BLOCK))
    first = total(jnp.where(iota((8, 8), 1) < iota((8, 8), 0), as_row(blocks), 0.0), 1)
    dest = total(by_root * (order[:8] + first * BLOCK), 0)
    ends = (first + blocks) <= iota((8, 128), 1).astype(F32)
    root_of = jnp.minimum(total(ends.astype(F32), 0), 7.0)
    v["table"][...] = jnp.broadcast_to(root_of, (8, 128)).astype(I32)
    table_copy = pltpu.make_async_copy(v["table"], table_s, copy_sem.at[19])
    table_copy.start()
    mid_order = order[8:9]
    v["pick"][...] = (iota((SORTED, 512), 0) == dest.astype(I32)).astype(BF16)
    turned = iota((512, 512), 1) == lax.rem(iota((512, 512), 0) + rank * ROWS, 512)
    final = total(jnp.where(turned, jnp.where(in_mid, SORTED + mid_order, dest), 0.0), 1).astype(I32)
    v["back"][...] = (iota((512, gathered), 1) == final).astype(BF16)
    if gathered > mid_end:
        v["xs"][mid_end:, :] = jnp.zeros((gathered - mid_end, MSG), BF16)
    lane256 = iota((1, 256), 1)
    for r in range(8):
        v["root_bias"][r] = jnp.where(
            (lane256 + rank * 256).astype(F32) < rl_row[:, r : r + 1], 0.0, NEG_FILL
        )
    own_len = total(jnp.where(iota((16, 1), 0) == rank, ml_col, 0.0), 0)
    own_parent = total(jnp.where(iota((16, 1), 0) == rank, parent_len, 0.0), 0)
    rr = rr_v[...]
    rr_col = as_col(rr.astype(F32))
    slot_col = rr_col.astype(I32)
    hit_hi = (iota((16, 256), 0) == rr // 128).astype(BF16)
    hit_lo = (iota((256, 128), 1) == slot_col % 128).astype(BF16)
    token = (iota((16, 128), 0) * 128 + iota((16, 128), 1)).astype(F32)
    alive = (token < own_len) & (dot(hit_hi, hit_lo) < 0.5)
    v["mid_bias"][...] = jnp.where(alive, 0.0, NEG_FILL)
    new_bias = jnp.where(rr.astype(F32) < own_len, 0.0, NEG_FILL)
    held_cos, held_sin = rope_tables(own_parent + rr_col, freq)

    r2, c2 = iota((256, 256), 0), iota((256, 256), 1)
    split = (c2 == jnp.where(r2 < 128, 2 * r2, 2 * r2 - 255)).astype(BF16)
    wkv_copy.wait()
    split_pairs(split, v["wkv"], v["wk"], v["wv"], 16)
    root_copy.wait()
    for k in range(16):
        both = dot(split, v["root"][k * 256 : (k + 1) * 256, :]).astype(BF16)
        half = slice((k % 2) * 128, (k % 2) * 128 + 128)
        v["root_k"][k // 2, half, :] = both[:128]
        v["root_v"][k // 2, half, :] = both[128:]
    held_copies[0].wait_recv()
    held_copies[1].wait_recv()
    held_copies += [
        send(held.at[ahead, low], held.at[ahead, low], hsem, 2, {"tp": after}),
        send(held.at[after, high], held.at[after, high], hsem, 3, {"tp": ahead}),
        send(held.at[ahead], held.at[ahead], hsem, 5, {"tp": sibling}),
        send(held.at[after], held.at[after], hsem, 6, {"tp": sibling}),
    ]

    mid_copy.wait()
    split_pairs(split, v["mid"], v["mid_k"], v["mid_v"], 16)

    for copy in q_copies:
        copy.wait_recv()
    v["qs"][...] = dot(v["pick"][...], v["qall"][...]).astype(BF16)
    held_copies[3].wait_recv()
    held_copies[4].wait_recv()
    held_copies += [
        send(held.at[across, low], held.at[across, low], hsem, 7, {"tp": sibling}),
        send(held.at[across, high], held.at[across, high], hsem, 8, {"tp": sibling}),
    ]
    block_mask = (iota((128, WIDTH), 0) // BLOCK == iota((128, WIDTH), 1) // HEAD_DIM).astype(BF16)
    table_copy.wait()

    def root_blocks(i, carry):
        ats = [
            pl.ds(pl.multiple_of((i * GROUP + u) * BLOCK, BLOCK), BLOCK) for u in range(GROUP)
        ]
        roots = [jnp.clip(table_s[0, i * GROUP + u], 0, 7) for u in range(GROUP)]
        qbds = [jnp.concatenate([v["qs"][at, :]] * HEADS, axis=0) * block_mask for at in ats]
        scores = [
            dot_t(qbd, v["root_k"][root]) + v["root_bias"][root] for qbd, root in zip(qbds, roots)
        ]
        tops = [jnp.max(score, axis=1, keepdims=True) for score in scores]
        weights = [jnp.exp(score - m) for score, m in zip(scores, tops)]
        sums = [total(weight, 1) for weight in weights]
        accs = [
            dot(weight.astype(BF16), v["root_v"][root]) for weight, root in zip(weights, roots)
        ]
        outs = []
        for m, row_sum, acc in zip(tops, sums, accs):
            out = head_columns(acc, BLOCK, WIDTH) / head_columns(row_sum, BLOCK, WIDTH)
            outs.append(packed(out, head_columns(m + jnp.log(row_sum), BLOCK, STATS)))
        for at, out in zip(ats, outs):
            v["xs"][at, :] = out
        return carry

    lax.fori_loop(0, BLOCKS // GROUP, root_blocks, 0)

    mid_mask = (iota((256, WIDTH), 0) // MID_ROWS == iota((256, WIDTH), 1) // HEAD_DIM).astype(BF16)
    e0, e1 = iota((STATS, WIDTH), 0), iota((STATS, WIDTH), 1)
    expand3 = ((e0 < 12) & ((e0 % HEADS) == e1 // HEAD_DIM)).astype(BF16)
    lane64 = iota((MID_ROWS, STATS), 1)
    lane128, row128 = iota((128, STATS), 1), iota((128, STATS), 0)
    to_place = ((row128 < 12) & (row128 % HEADS == lane128 // ROWS)).astype(BF16)
    in_place = lane128 % ROWS == row128 % ROWS
    row8 = iota((8, WIDTH), 0)

    for copy in [held_copies[2]] + held_copies[5:]:
        copy.wait_recv()
    square = jnp.zeros((256, 1), F32)
    for c in range(NTP):
        part = v["held"][c].astype(F32)
        square = square + total(part * part, 1)
    scale = lax.rsqrt(square * (1.0 / D) + EPSILON)
    keys = jnp.zeros((256, WIDTH), F32)
    values = jnp.zeros((256, WIDTH), F32)
    for c in range(NTP):
        rows = slice(c * 256, (c + 1) * 256)
        part = (v["held"][c].astype(F32) * scale * gain[:, rows]).astype(BF16)
        keys = keys + dot(part, v["wk"][rows, :])
        values = values + dot(part, v["wv"][rows, :])
    v["new_k"][...] = rope(keys, held_cos, held_sin).astype(BF16)
    v["new_v"][...] = values.astype(BF16)

    def mid_pass(p):
        chosen = (iota((MID_ROWS, 512), 0) + p * MID_ROWS == mid_order.astype(I32)) & in_mid
        mid_dest = total(jnp.where(chosen, dest, 0.0), 1)
        q_mid = dot(chosen.astype(BF16), v["qall"][...]).astype(BF16)
        take = (iota((MID_ROWS, SORTED), 1) == mid_dest.astype(I32)).astype(BF16)
        rooted = dot(take, v["xs"][:SORTED, :])
        qbd = jnp.concatenate([q_mid] * HEADS, axis=0) * mid_mask
        fresh = dot_t(qbd, v["new_k"][...]) + new_bias
        m = jnp.max(fresh, axis=1, keepdims=True)
        for c in range(8):
            cols = slice(c * 256, (c + 1) * 256)
            bias = jnp.concatenate(
                [v["mid_bias"][2 * c : 2 * c + 1, :], v["mid_bias"][2 * c + 1 : 2 * c + 2, :]], axis=1
            )
            scores = dot_t(qbd, v["mid_k"][cols, :]) + bias
            v["scores"][:, cols] = scores
            m = jnp.maximum(m, jnp.max(scores, axis=1, keepdims=True))
        weights = jnp.exp(fresh - m)
        row_sum = total(weights, 1)
        acc = dot(weights.astype(BF16), v["new_v"][...])
        for c in range(8):
            cols = slice(c * 256, (c + 1) * 256)
            weights = jnp.exp(v["scores"][:, cols] - m)
            row_sum = row_sum + total(weights, 1)
            v["weights"][:, cols] = weights.astype(BF16)
        acc = acc + dot(v["weights"][...], v["mid_v"][...])
        mid_out = head_columns(acc, MID_ROWS, WIDTH) / head_columns(row_sum, MID_ROWS, WIDTH)
        mid_lse = m + jnp.log(row_sum)
        lse_a = dot(rooted[:, WIDTH:].astype(BF16), expand3)
        lse_b = head_columns(mid_lse, MID_ROWS, WIDTH)
        top = jnp.maximum(lse_a, lse_b)
        part_a, part_b = jnp.exp(lse_a - top), jnp.exp(lse_b - top)
        merged = (part_a * rooted[:, :WIDTH] + part_b * mid_out) / (part_a + part_b)
        lse_a = jnp.where(lane64 < 4, unpacked_lse(rooted[:, WIDTH:]), 0.0)
        lse_a = lse_a + pltpu.roll(lse_a, 4, 1) + pltpu.roll(lse_a, 8, 1)
        lse_b = head_columns(mid_lse, MID_ROWS, STATS)
        top = jnp.maximum(lse_a, lse_b)
        joined = top + jnp.log(jnp.exp(lse_a - top) + jnp.exp(lse_b - top))
        at = SORTED if passes == 1 else pl.multiple_of(SORTED + p * MID_ROWS, MID_ROWS)
        v["xs"][pl.ds(at, MID_ROWS), :] = packed(merged, joined)

    if passes == 1:
        mid_pass(0)
    else:

        def mid_step(p, carry):
            mid_pass(p)
            return carry

        lax.fori_loop(0, passes, mid_step, 0)

    a_copies = []
    for g in range(4):
        natural = dot(v["back"][g * 128 : (g + 1) * 128, :], v["xs"][...])
        placed = dot(natural[:, WIDTH:].astype(BF16), to_place)
        placed = jnp.where(in_place, placed, 0.0)
        for d in range(g * 4, g * 4 + 4):
            rows = slice((d - g * 4) * ROWS, (d - g * 4 + 1) * ROWS)
            v["parts"][d, :ROWS, :] = natural[rows, :WIDTH].astype(BF16)
            lse = total(placed[rows], 0)
            a, b, c = three_terms(jnp.concatenate([lse, jnp.zeros((1, STATS), F32)], axis=1))
            tail = jnp.where(
                row8 == 0,
                a.astype(F32),
                jnp.where(row8 == 1, b.astype(F32), jnp.where(row8 == 2, c.astype(F32), 0.0)),
            )
            v["parts"][d, ROWS:, :] = tail.astype(BF16)
            if d > 0:
                a_copies.append(
                    send(v["parts"].at[d], v["arrived"].at[d], asem, d, {"req": req_peer(d)})
                )
    v["arrived"][0] = v["parts"][0]

    key_new = rope(dot(normed, v["wk"][...]), cosines, sines).astype(BF16)
    value_new = dot(normed, v["wv"][...]).astype(BF16)
    repeat = (iota((256, ROWS), 0) // 8 == iota((256, ROWS), 1)).astype(BF16)
    head_mask = (r2 % 8) == (c2 // HEAD_DIM)
    qrep = jnp.where(head_mask, dot(repeat, queries), 0.0)
    v["leaf_q"][...] = qrep.astype(BF16)
    self_score = total(qrep * dot(repeat, key_new), 1)
    live_len = total(repeat.astype(F32) * leaf_len_row, 1)
    leaf_copy.wait()
    for r in range(ROWS):
        v["leaf_s"][r * 8 : (r + 1) * 8, :] = dot_t(
            v["leaf_q"][r * 8 : (r + 1) * 8, :], v["leaf"][r * 256 : (r + 1) * 256, :]
        )
    live = ((c2 % 2) == 1) & ((c2 // 2).astype(F32) < live_len)
    scores = jnp.where(live, shift_pairs(v["leaf_s"][...]), NEG_FILL)
    best = jnp.maximum(jnp.max(scores, axis=1, keepdims=True), self_score)
    weights = jnp.exp(scores - best)
    self_weight = jnp.exp(self_score - best)
    row_sum = total(weights, 1) + self_weight
    v["leaf_q"][...] = weights.astype(BF16)
    for r in range(ROWS):
        v["leaf_s"][r * 8 : (r + 1) * 8, :] = dot(
            v["leaf_q"][r * 8 : (r + 1) * 8, :], v["leaf"][r * 256 : (r + 1) * 256, :]
        )
    acc = v["leaf_s"][...] + self_weight.astype(BF16).astype(F32) * dot(repeat, value_new)
    acc = jnp.where(head_mask, acc / row_sum, 0.0)
    leaf_out = jnp.sum(acc.reshape(ROWS, 8, WIDTH), axis=1)
    lse = best + jnp.log(row_sum)
    place = ((r2 % 8) * ROWS + r2 // 8)[:, :STATS] == c2[:, :STATS]
    leaf_lse = total(jnp.where(place, lse, 0.0), 0)

    diagonal = iota((ROWS, STATS), 1) % ROWS == iota((ROWS, STATS), 0)
    expand = ((r2 % STATS) // ROWS == c2 // HEAD_DIM).astype(BF16)
    for copy in a_copies:
        copy.wait_recv()
    lses = [total(v["arrived"][s, ROWS:, :STATS].astype(F32), 0) for s in range(NREQ)]
    lses.append(leaf_lse)
    best = lses[0]
    for value in lses[1:]:
        best = jnp.maximum(best, value)
    shares = [jnp.exp(value - best) for value in lses]
    row_sum = shares[0]
    for value in shares[1:]:
        row_sum = row_sum + value
    pieces = []
    for share in shares:
        share = jnp.where(diagonal, share / row_sum, 0.0)
        high = share.astype(BF16)
        pieces.append(jnp.concatenate([high, (share - high.astype(F32)).astype(BF16)], axis=1))
    factors = dot(jnp.concatenate(pieces, axis=0), expand)
    attended = jnp.zeros((ROWS, WIDTH), F32)
    for s in range(NREQ + 1):
        source = v["arrived"][s, :ROWS, :].astype(F32) if s < NREQ else leaf_out
        attended = attended + factors[s * ROWS : (s + 1) * ROWS] * source
    attended = attended.astype(BF16)

    own_cols = pl.ds(pl.multiple_of(tp * WIDTH, WIDTH), WIDTH)

    def scatter(left, weight_v, outgoing, incoming, sems):
        copies = []
        for d in range(1, NTP):
            peer = tp_peer(d)
            cols = pl.ds(pl.multiple_of(peer * WIDTH, WIDTH), WIDTH)
            outgoing[d] = dot(left, weight_v[:, cols]).astype(BF16)
            copies.append(send(outgoing.at[d], incoming.at[d], sems, d, {"tp": peer}))
        return copies, dot(left, weight_v[:, own_cols])

    wout_copy.wait()
    r_copies, own_part = scatter(attended, v["wout"], v["rs_out"], v["rs_in"], rsem)
    residual = own_part + stream_v[:, own_cols].astype(F32)
    i2, j2 = iota((256, 512), 0), iota((256, 512), 1)
    to_even = (j2 == 2 * i2).astype(BF16)
    to_odd = (j2 == 2 * i2 + 1).astype(BF16)
    gain_row = mgain_v[...].reshape(1, D).astype(F32)
    v["gain"][...] = gain_row
    for d in range(1, NTP):
        r_copies[d - 1].wait_recv()
        residual = residual + v["rs_in"][d].astype(F32)

    v["ag"][0] = residual.astype(BF16)
    g_copies = [
        send(v["ag"].at[0], v["ag"].at[d], gsem, d, {"tp": tp_peer(d)}) for d in range(1, NTP)
    ]
    wgu_copy.wait()
    squares = jnp.zeros((ROWS, WIDTH), F32)
    for d in range(NTP):
        if d > 0:
            g_copies[d - 1].wait_recv()
        owner = tp_peer(NTP - d)
        part = v["ag"][d].astype(F32)
        squares = squares + part * part
        gain_cols = pl.ds(pl.multiple_of(owner * WIDTH, WIDTH), WIDTH)
        chunk = (part * v["gain"][:, gain_cols]).astype(BF16)
        mixed = jnp.concatenate([dot(chunk, to_even), dot(chunk, to_odd)], axis=0).astype(BF16)
        rows = pl.ds(pl.multiple_of(owner * 512, 512), 512)
        for n in range(4):
            cols = slice(n * 256, (n + 1) * 256)
            product = dot(mixed, v["wgu"][rows, cols])
            if d == 0:
                v["proj"][:, cols] = product
            else:
                v["proj"][:, cols] += product
    scale = lax.rsqrt(total(squares, 1) * (1.0 / D) + EPSILON)
    gate = v["proj"][:ROWS, :] * scale
    up = v["proj"][ROWS:, :] * scale
    hidden = (gate / (1.0 + jnp.exp(-gate)) * up).astype(BF16)
    wdn_copy.wait()
    d_copies, own_part = scatter(hidden, v["wdn"], v["ds_out"], v["ds_in"], dsem)
    result = residual + own_part
    for d in range(1, NTP):
        d_copies[d - 1].wait_recv()
        result = result + v["ds_in"][d].astype(F32)
    out_ref[...] = result.astype(BF16)
    for copy in held_copies + q_copies + a_copies + r_copies + g_copies + d_copies:
        copy.wait_send()


def layer_device(
    passes,
    stream,
    attn_gain,
    mlp_gain,
    w_query,
    w_keyval,
    w_out,
    w_gate_up,
    w_down,
    root_cache,
    mid_cache,
    leaf_cache,
    held_hidden,
    recompute_rows,
    root_len,
    mid_len,
    leaf_len,
    mid_parent,
    leaf_parent,
):
    freq = np.exp(np.arange(32, dtype=np.float32) * np.float32(-2.0 * math.log(THETA_BASE) / HEAD_DIM))
    freq = jnp.asarray(np.tile(freq.astype(np.float32), 4)[None, :])
    dma = pltpu.SemaphoreType.DMA
    return pl.pallas_call(
        functools.partial(layer_kernel, passes),
        name="layer" if passes == 1 else "layer_crowded",
        out_shape=jax.ShapeDtypeStruct((ROWS, WIDTH), BF16),
        in_specs=[pl.BlockSpec(memory_space=pltpu.HBM)] * 19,
        out_specs=pl.BlockSpec(memory_space=pltpu.VMEM),
        scratch_shapes=[pltpu.VMEM(*s) for s in SMALL]
        + [pltpu.VMEM(*s) for s in sized(passes).values()]
        + [
            pltpu.SMEM((8, 128), I32),
            dma((20,)),
            dma((2, 9)),
            dma((2, NREQ)),
            dma((2, NREQ)),
            dma((2, NTP)),
            dma((2, NTP)),
            dma((2, NTP)),
        ],
        compiler_params=pltpu.CompilerParams(
            collective_id=0 if passes == 1 else 1, has_side_effects=True, vmem_limit_bytes=56 * 1024 * 1024
        ),
    )(
        stream,
        attn_gain,
        mlp_gain,
        leaf_parent,
        mid_parent,
        root_len,
        mid_len,
        leaf_len,
        recompute_rows,
        freq,
        w_query,
        w_keyval,
        w_out,
        w_gate_up,
        w_down,
        root_cache,
        mid_cache,
        leaf_cache,
        held_hidden,
    )


def on_device(*args):
    leaf_parent = args[17]
    counts = jnp.sum(
        (leaf_parent[None, :] == jnp.arange(16, dtype=I32)[:, None]).astype(I32), axis=1
    )
    usual = functools.partial(layer_device, 1)
    crowded = functools.partial(layer_device, 512 // MID_ROWS)
    return lax.cond(jnp.max(counts) <= MID_ROWS, usual, crowded, *args)


def solution(mesh):
    placed = (
        P("req", None),
        P(),
        P(),
        P(None, "tp"),
        P(None, None, "tp"),
        P("tp", None),
        P(None, None, "tp"),
        P("tp", None),
        P(None, "req", None, "tp"),
        P("req", None, None, "tp"),
        P("req", None, None, "tp"),
        P("req", None, "tp"),
        P("req", None),
        P(),
        P(),
        P("req"),
        P(),
        P(),
    )
    return jax.shard_map(
        on_device, mesh=mesh, in_specs=placed, out_specs=P("req", "tp"), check_vma=False
    )
```
